256 devices in a mesh: rep: 2 (over y_hi), dp: 2 (over y_lo), seq: 64 (over x, z, core).
Axes of the slice: x: 4, y: 4 (y_hi: 2, y_lo: 2; y = y_hi * 2 + y_lo), z: 8, core: 2. Of those that a mesh axis runs over, the one named last changes fastest.
Arguments:
- tokens: bfloat16 [4, 128, 8, 16, 768], P(('rep', 'dp'), 'seq'), may hold values from -6 to 6
- cotangent: bfloat16 [4, 128, 8, 16, 768], P(('rep', 'dp'), 'seq'), may hold values from -6 to 6
- w_qkv: bfloat16 [768, 2304], P('dp'), may hold values from -0.21875 to 0.21875
- w_proj: bfloat16 [768, 768], P('dp'), may hold values from -0.21875 to 0.21875
- conv_weight: float32 [27, 768], replicated, may hold values from -1.25 to 1.25
- norm_gain: float32 [768], replicated, may hold values from 0.5 to 1.5
- head_scale: float32 [24], replicated, may hold values from 2 to 20
- shift_offsets: int32 [2], replicated, may hold values from 1 to 7, as said below
Outputs:
- output: bfloat16 [4, 128, 8, 16, 768], P(('rep', 'dp'), 'seq')
- grad_tokens: bfloat16 [4, 128, 8, 16, 768], P(('rep', 'dp'), 'seq')
- grad_qkv: float32 [768, 2304], P('dp')
- grad_proj: float32 [768, 768], P('dp')
- grad_conv: float32 [27, 768], replicated
- grad_gain: float32 [768], replicated
- grad_scale: float32 [24], replicated
The draws below stay inside these ranges and needn't reach their ends.
Inputs may be any that keep to these rules, and one draw needn't show every extreme that they name: `shift_offsets`: the two offsets differ.
All inputs are finite; a program needn't handle non-finite values.
Results may differ from the reference program's by a relative error of at most 0.014.
The reference program's roundings to bfloat16 on the way count: a program that leaves them out, or rounds other values in their place, can miss the bound.
Values may be sent and summed in bfloat16 or wider, within the bound.
A program may use at most 128 MiB of HBM per device.

```python
import math
import jax
import jax.numpy as jnp
from jax import lax

C = 768
HEADS = 24
WD = 4
WH = 8
WW = 8
DL = 2
HH = 8
WIDE = 16
DEPTH = 128
GROUPS = 4


def draw_shift_offsets(key, part):
    largest = min(WH, WW) - 1
    which = jax.random.randint(jax.random.fold_in(key, 11), (), 0, 2)
    other = jax.random.randint(jax.random.fold_in(key, 12), (), 1, largest)
    top = jnp.array(largest, jnp.int32)
    first = jnp.where(which == 0, top, other.astype(jnp.int32))
    second = jnp.where(which == 0, other.astype(jnp.int32), top)
    return jnp.stack([first, second]).astype(jnp.int32)


def block_scale(own_key, extent, shards, low, high):
    def one(position, shards_of):
        draws = jax.random.uniform(jax.random.fold_in(jax.random.fold_in(own_key, 6), position), (shards_of,), jnp.float32, low / len(shards), high / len(shards))
        return jnp.repeat(jnp.exp(draws), extent[position] // shards_of).reshape((-1,) + (1,) * (len(extent) - position - 1))

    loudness = one(*shards[0])
    for cut in shards[1:]:
        loudness = loudness * one(*cut)
    return loudness


def scatter_about(key, dims, scale, bound, shards=(), dtype=jnp.bfloat16):
    values = scale * jax.random.normal(key, dims, jnp.float32)
    if shards:
        values = values * block_scale(key, dims, shards, -0.22, 0.18)
    return jnp.clip(values, -bound, bound).astype(dtype)


def setup_inputs(seed: int = 0) -> dict:
    splits = jax.random.split(jax.random.key(seed), 9)
    return {
        "tokens": scatter_about(splits[0], (GROUPS, DEPTH, HH, WIDE, C), 1.0, 6.0, ((0, 4), (1, 64))),
        "cotangent": scatter_about(splits[1], (GROUPS, DEPTH, HH, WIDE, C), 1.0, 6.0, ((0, 4), (1, 64))),
        "w_qkv": scatter_about(splits[2], (C, 3 * C), C ** -0.5, 0.21875, ((0, 2),)),
        "w_proj": scatter_about(splits[3], (C, C), C ** -0.5, 0.21875, ((0, 2),)),
        "conv_weight": scatter_about(splits[4], (27, C), 27 ** -0.5, 1.25, (), jnp.float32),
        "norm_gain": jnp.clip(1.0 + 0.1 * jax.random.normal(splits[5], (C,), jnp.float32), 0.5, 1.5),
        "head_scale": jnp.clip(jnp.exp(jax.random.uniform(splits[6], (HEADS,), jnp.float32, math.log(2.0), math.log(20.0))), 2.0, 20.0),
        "shift_offsets": draw_shift_offsets(jax.random.fold_in(splits[8], 71), 0),
    }


def tap_sum(padded, weight, slab_depth, height, grid_width, flipped):
    summed = jnp.zeros((slab_depth, height, grid_width, padded.shape[-1]), jnp.float32)
    for depth_tap in range(3):
        for row_tap in range(3):
            for col_tap in range(3):
                tap_index = 9 * depth_tap + 3 * row_tap + col_tap
                if flipped:
                    starts = (2 - depth_tap, 2 - row_tap, 2 - col_tap)
                else:
                    starts = (depth_tap, row_tap, col_tap)
                window_part = padded[starts[0]:starts[0] + slab_depth, starts[1]:starts[1] + height, starts[2]:starts[2] + grid_width]
                summed = summed + weight[tap_index] * window_part.astype(jnp.float32)
    return summed

def into_windows(field):
    slab_depth, height, grid_width, channels = field.shape
    shaped = field.reshape(slab_depth // WD, WD, height // WH, WH, grid_width // WW, WW, channels)
    shaped = shaped.transpose(0, 2, 4, 1, 3, 5, 6)
    return shaped.reshape(slab_depth // WD, height // WH * (grid_width // WW), WD * WH * WW, channels)

def out_of_windows(blocks, slab_depth, height, grid_width):
    channels = blocks.shape[-1]
    shaped = blocks.reshape(slab_depth // WD, height // WH, grid_width // WW, WD, WH, WW, channels)
    shaped = shaped.transpose(0, 3, 1, 4, 2, 5, 6)
    return shaped.reshape(slab_depth, height, grid_width, channels)

def unit_rows(values):
    as_float = values.astype(jnp.float32)
    radius = jnp.sqrt(lax.optimization_barrier(jnp.sum(as_float * as_float, axis=-1, keepdims=True)) + 1.0)
    return (as_float, radius, (as_float / radius).astype(jnp.bfloat16))

def radius_back(as_float, radius, back_unit):
    inner = lax.optimization_barrier(jnp.sum(as_float * back_unit, axis=-1, keepdims=True))
    return back_unit / radius - as_float * inner / (radius * radius * radius)

def window_forward(unit_query, unit_key, values, allowed, head_scale):
    cosine = jnp.einsum('wqhe,wkhe->whqk', unit_query.astype(jnp.float32), unit_key.astype(jnp.float32))
    expo = jnp.exp(head_scale[:, None, None] * cosine) * allowed[:, None]
    probability = expo / lax.optimization_barrier(jnp.sum(expo, axis=-1, keepdims=True))
    weights = probability.astype(jnp.bfloat16)
    attended = jnp.einsum('whqk,wkhe->wqhe', weights.astype(jnp.float32), values.astype(jnp.float32)).astype(jnp.bfloat16)
    return (cosine, probability, weights, attended)

def window_backward(unit_query, unit_key, values, allowed, head_scale, back_attended):
    cosine, probability, weights, unused = window_forward(unit_query, unit_key, values, allowed, head_scale)
    back_float = back_attended.astype(jnp.float32)
    back_value = jnp.einsum('whqk,wqhe->wkhe', weights.astype(jnp.float32), back_float)
    back_prob = jnp.einsum('wqhe,wkhe->whqk', back_float, values.astype(jnp.float32))
    back_score = probability * (back_prob - lax.optimization_barrier(jnp.sum(probability * back_prob, axis=-1, keepdims=True)))
    scale_rows = lax.optimization_barrier(jnp.sum(back_score * cosine, axis=-1))
    scaled = (back_score * head_scale[:, None, None]).astype(jnp.bfloat16)
    back_uq = jnp.einsum('whqk,wkhe->wqhe', scaled.astype(jnp.float32), unit_key.astype(jnp.float32))
    back_uk = jnp.einsum('whqk,wqhe->wkhe', scaled.astype(jnp.float32), unit_query.astype(jnp.float32))
    return (back_uq, back_uk, back_value, scale_rows)

def one_group(tokens, cotangent, w_qkv, w_proj, conv_weight, norm_gain, head_scale, shift_offsets):
    slab_depth, height, grid_width, channels = tokens.shape
    head_count = head_scale.shape[0]
    head_dim = channels // head_count
    rows_shift = shift_offsets[0]
    cols_shift = shift_offsets[1]
    spatial = ((1, 1), (1, 1), (1, 1), (0, 0))
    padded_tokens = jnp.pad(tokens, spatial)
    mixed_field = tokens.astype(jnp.float32) + tap_sum(padded_tokens, conv_weight, slab_depth, height, grid_width, False)
    centred = mixed_field - lax.optimization_barrier(jnp.mean(mixed_field, axis=-1, keepdims=True))
    inverse_std = lax.rsqrt(lax.optimization_barrier(jnp.mean(centred * centred, axis=-1, keepdims=True)) + 1e-05)
    unit_field = centred * inverse_std
    normed = (unit_field * norm_gain).astype(jnp.bfloat16)
    shifted = jnp.roll(normed, (-DL, -rows_shift, -cols_shift), axis=(0, 1, 2))
    position_count = slab_depth * height * grid_width
    shifted_rows = shifted.reshape(position_count, channels)
    qkv = jnp.dot(shifted_rows, w_qkv, preferred_element_type=jnp.float32).astype(jnp.bfloat16)
    qkv_windows = into_windows(qkv.reshape(slab_depth, height, grid_width, 3 * channels))
    row_code = 2 * (jnp.arange(height) >= height - rows_shift).astype(jnp.int32)
    col_code = (jnp.arange(grid_width) >= grid_width - cols_shift).astype(jnp.int32)
    grid_code = jnp.broadcast_to((row_code[:, None] + col_code[None, :])[None], (slab_depth, height, grid_width))
    code_windows = into_windows(grid_code[..., None])[..., 0]
    block_count = qkv_windows.shape[1]
    positions = qkv_windows.shape[2]

    def split_heads(part):
        return part.reshape(block_count, positions, head_count, head_dim)

    def prepare(qkv_block, code_block):
        allowed = (code_block[:, :, None] == code_block[:, None, :]).astype(jnp.float32)
        query = split_heads(qkv_block[..., :channels])
        key_part = split_heads(qkv_block[..., channels:2 * channels])
        value_part = split_heads(qkv_block[..., 2 * channels:])
        return (allowed, query, key_part, value_part)

    def forward_block(packed):
        allowed, query, key_part, value_part = prepare(packed[0], packed[1])
        unused_a, unused_b, unit_query = unit_rows(query)
        unused_c, unused_d, unit_key = unit_rows(key_part)
        return window_forward(unit_query, unit_key, value_part, allowed, head_scale)[3]
    attended = lax.map(forward_block, (qkv_windows, code_windows))
    attended = attended.reshape(attended.shape[0], block_count, positions, channels)
    restored = jnp.roll(out_of_windows(attended, slab_depth, height, grid_width), (DL, rows_shift, cols_shift), axis=(0, 1, 2))
    restored_rows = restored.reshape(position_count, channels)
    projected = jnp.dot(restored_rows, w_proj, preferred_element_type=jnp.float32)
    output = (mixed_field + projected.reshape(slab_depth, height, grid_width, channels)).astype(jnp.bfloat16)
    cotangent_rows = cotangent.reshape(position_count, channels)
    back_restored = jnp.dot(cotangent_rows, w_proj.T, preferred_element_type=jnp.float32).astype(jnp.bfloat16)
    back_attended = jnp.roll(back_restored.reshape(slab_depth, height, grid_width, channels), (-DL, -rows_shift, -cols_shift), axis=(0, 1, 2))
    back_windows = into_windows(back_attended)

    def backward_block(packed):
        allowed, query, key_part, value_part = prepare(packed[0], packed[1])
        query_float, query_radius, unit_query = unit_rows(query)
        key_float, key_radius, unit_key = unit_rows(key_part)
        back_heads = split_heads(packed[2])
        back_uq, back_uk, back_value, scale_rows = window_backward(unit_query, unit_key, value_part, allowed, head_scale, back_heads)
        back_query = radius_back(query_float, query_radius, back_uq)
        back_key = radius_back(key_float, key_radius, back_uk)
        joined = jnp.concatenate([back_query.reshape(block_count, positions, channels), back_key.reshape(block_count, positions, channels), back_value.reshape(block_count, positions, channels)], axis=-1)
        return (joined.astype(jnp.bfloat16), lax.optimization_barrier(jnp.sum(scale_rows, axis=(0, 2))))
    back_qkv_windows, scale_parts = lax.map(backward_block, (qkv_windows, code_windows, back_windows))
    back_qkv = out_of_windows(back_qkv_windows, slab_depth, height, grid_width)
    back_qkv_rows = back_qkv.reshape(position_count, 3 * channels)
    qkv_part = jnp.dot(shifted_rows.T, back_qkv_rows, preferred_element_type=jnp.float32)
    proj_part = jnp.dot(restored_rows.T, cotangent_rows, preferred_element_type=jnp.float32)
    back_shifted = jnp.dot(back_qkv_rows, w_qkv.T, preferred_element_type=jnp.float32).astype(jnp.bfloat16)
    back_normed = jnp.roll(back_shifted.reshape(slab_depth, height, grid_width, channels), (DL, rows_shift, cols_shift), axis=(0, 1, 2))
    back_float = back_normed.astype(jnp.float32)
    gain_part = lax.optimization_barrier(jnp.sum(back_float * unit_field, axis=(0, 1, 2)))
    grad_unit = back_float * norm_gain
    back_mixed = cotangent.astype(jnp.float32) + inverse_std * (grad_unit - lax.optimization_barrier(jnp.mean(grad_unit, axis=-1, keepdims=True)) - unit_field * lax.optimization_barrier(jnp.mean(grad_unit * unit_field, axis=-1, keepdims=True)))
    padded_back = jnp.pad(back_mixed, spatial)
    grad_tokens = (back_mixed + tap_sum(padded_back, conv_weight, slab_depth, height, grid_width, True)).astype(jnp.bfloat16)
    conv_rows = []
    for depth_tap in range(3):
        for row_tap in range(3):
            for col_tap in range(3):
                window_part = padded_tokens[depth_tap:depth_tap + slab_depth, row_tap:row_tap + height, col_tap:col_tap + grid_width]
                conv_rows.append(lax.optimization_barrier(jnp.sum(back_mixed * window_part.astype(jnp.float32), axis=(0, 1, 2))))
    conv_part = jnp.stack(conv_rows)
    return (output, grad_tokens, qkv_part, proj_part, conv_part, gain_part, lax.optimization_barrier(jnp.sum(scale_parts, axis=0)))

def reference(tokens, cotangent, w_qkv, w_proj, conv_weight, norm_gain, head_scale, shift_offsets):

    def per_group(packed):
        return one_group(packed[0], packed[1], w_qkv, w_proj, conv_weight, norm_gain, head_scale, shift_offsets)
    results = lax.map(per_group, (tokens, cotangent))
    factor = 1.0 / math.sqrt(GROUPS * DEPTH * HH * WIDE)
    return (results[0], results[1], lax.optimization_barrier(jnp.sum(results[2], axis=0)) * factor, lax.optimization_barrier(jnp.sum(results[3], axis=0)) * factor, lax.optimization_barrier(jnp.sum(results[4], axis=0)) * factor, lax.optimization_barrier(jnp.sum(results[5], axis=0)) * factor, lax.optimization_barrier(jnp.sum(results[6], axis=0)) * factor)
```

```python
import math

import jax
import jax.numpy as jnp
from jax import lax
from jax.experimental import pallas as pl
from jax.experimental.pallas import tpu as pltpu
from jax.sharding import PartitionSpec as P

WH = 8
WW = 8
MESH = pl.DeviceIdType.MESH
XC = 4
ZC = 8


def reduce_kernel(g, out, ra0, ra1, sa0, sa1, rb0, rb1, sb, rc,
                  a_send, a_recv, b_send, b_recv, c_send, c_recv, d_send, d_recv,
                  e_send, e_recv, f_send, f_recv, h_send, h_recv):
    rep, dp, seq = lax.axis_index("rep"), lax.axis_index("dp"), lax.axis_index("seq")
    core = lax.rem(seq, 2)
    z = lax.rem(seq // 2, ZC)
    x = seq // (2 * ZC)
    y = rep * 2 + dp
    half = ZC // 2

    def at_y(step):
        there = lax.rem(y + step, 4)
        return (there // 2, lax.rem(there, 2), seq)

    def at_x(step):
        there = lax.rem(x + step, XC)
        return (rep, dp, (there * ZC + z) * 2 + core)

    def at_z(step):
        there = lax.rem(z + step, ZC)
        return (rep, dp, (x * ZC + there) * 2 + core)

    other_core = (rep, dp, (x * ZC + z) * 2 + 1 - core)
    other_rep = (1 - rep, dp, seq)
    peers = [at_y(k) for k in range(1, 4)] + [at_x(k) for k in range(1, XC)]
    peers += [at_z(k) for k in range(1, ZC)] + [other_core]
    barrier = pltpu.get_barrier_semaphore()
    for peer in peers:
        pl.semaphore_signal(barrier, inc=1, device_id=peer, device_id_type=MESH)
    pl.semaphore_wait(barrier, len(peers))

    def send(src, dst, s, r, to):
        c = pltpu.make_async_remote_copy(
            src_ref=src, dst_ref=dst, send_sem=s, recv_sem=r, device_id=to, device_id_type=MESH
        )
        c.start()
        return c

    copies = []
    for k in range(1, 4):
        to = at_y(k)
        copies.append(send(g.at[to[1], to[0], :, pl.ds(0, half)], ra0.at[k - 1],
                           a_send.at[k - 1], a_recv.at[k - 1], to))
    for k in range(1, XC):
        to = at_x(k)
        there = lax.rem(x + k, XC)
        copies.append(send(g.at[:, :, there, pl.ds(half, half)], ra1.at[k - 1],
                           a_send.at[k + 2], a_recv.at[k + 2], to))
    for c in copies:
        c.wait()

    def add_a0(i, carry):
        total = g[dp, rep, i, pl.ds(0, half)].astype(jnp.float32)
        for k in range(3):
            total = total + ra0[k, i].astype(jnp.float32)
        sa0[i] = total.astype(jnp.bfloat16)
        return carry

    lax.fori_loop(0, XC, add_a0, 0)

    def add_a1(i, carry):
        d, r = lax.rem(i, 2), i // 2
        total = g[d, r, x, pl.ds(half, half)].astype(jnp.float32)
        for k in range(XC - 1):
            total = total + ra1[k, d, r].astype(jnp.float32)
        sa1[d, r] = total.astype(jnp.bfloat16)
        return carry

    lax.fori_loop(0, 4, add_a1, 0)

    copies = []
    for k in range(1, XC):
        there = lax.rem(x + k, XC)
        copies.append(send(sa0.at[there], rb0.at[k - 1], b_send.at[k - 1], b_recv.at[k - 1], at_x(k)))
    for k in range(1, 4):
        to = at_y(k)
        copies.append(send(sa1.at[to[1], to[0]], rb1.at[k - 1], b_send.at[k + 2], b_recv.at[k + 2], to))
    for c in copies:
        c.wait()

    def add_b(i, carry):
        total = sa0[x, i].astype(jnp.float32)
        for k in range(XC - 1):
            total = total + rb0[k, i].astype(jnp.float32)
        sb[i] = total.astype(jnp.bfloat16)
        total = sa1[dp, rep, i].astype(jnp.float32)
        for k in range(3):
            total = total + rb1[k, i].astype(jnp.float32)
        sb[i + half] = total.astype(jnp.bfloat16)
        return carry

    lax.fori_loop(0, half, add_b, 0)

    copies = []
    for k in range(1, ZC):
        there = lax.rem(z + k, ZC)
        copies.append(send(sb.at[there], rc.at[k - 1], c_send.at[k - 1], c_recv.at[k - 1], at_z(k)))
    for c in copies:
        c.wait()
    total = sb[z].astype(jnp.float32)
    for k in range(ZC - 1):
        total = total + rc[k].astype(jnp.float32)
    out[core, rep, x, z] = total.astype(jnp.bfloat16)

    copies = []
    for k in range(1, ZC):
        mine = out.at[core, rep, x, z]
        copies.append(send(mine, mine, d_send.at[k - 1], d_recv.at[k - 1], at_z(k)))
    for c in copies:
        c.wait()
    mine = out.at[core, rep, x]
    to_rep = send(mine, mine, e_send, e_recv, other_rep)
    handed = [send(mine, mine, h_send.at[0], h_recv.at[0], other_core)]
    to_rep.wait()
    theirs = out.at[core, 1 - rep, x]
    both = out.at[core, :, x]
    copies = []
    for k in range(1, XC):
        copies.append(send(both, both, f_send.at[k - 1], f_recv.at[k - 1], at_x(k)))
    handed.append(send(theirs, theirs, h_send.at[1], h_recv.at[1], other_core))
    for k in range(1, XC):
        copies[k - 1].wait()
        came = lax.rem(x + XC - k, XC)
        piece = out.at[core, :, came]
        handed.append(send(piece, piece, h_send.at[k + 1], h_recv.at[k + 1], other_core))
    for c in handed:
        c.wait()


def reduce_all(g):
    tail = g.shape[4:]
    half = ZC // 2
    bf = jnp.bfloat16
    dma = pltpu.SemaphoreType.DMA
    return pl.pallas_call(
        reduce_kernel,
        out_shape=jax.ShapeDtypeStruct((2, 2, XC, ZC) + tail, bf),
        in_specs=[pl.BlockSpec(memory_space=pltpu.VMEM)],
        out_specs=pl.BlockSpec(memory_space=pltpu.VMEM),
        scratch_shapes=[
            pltpu.VMEM((3, XC, half) + tail, bf),
            pltpu.VMEM((XC - 1, 2, 2, half) + tail, bf),
            pltpu.VMEM((XC, half) + tail, bf),
            pltpu.VMEM((2, 2, half) + tail, bf),
            pltpu.VMEM((XC - 1, half) + tail, bf),
            pltpu.VMEM((3, half) + tail, bf),
            pltpu.VMEM((ZC,) + tail, bf),
            pltpu.VMEM((ZC - 1,) + tail, bf),
            dma((6,)), dma((6,)), dma((6,)), dma((6,)),
            dma((ZC - 1,)), dma((ZC - 1,)), dma((ZC - 1,)), dma((ZC - 1,)),
            dma, dma, dma((XC - 1,)), dma((XC - 1,)), dma((XC + 1,)), dma((XC + 1,)),
        ],
        compiler_params=pltpu.CompilerParams(
            collective_id=0, has_side_effects=True, vmem_limit_bytes=40 << 20
        ),
        cost_estimate=pl.CostEstimate(flops=10_000_000, bytes_accessed=60_000_000, transcendentals=0),
        name="grad_reduce",
    )(g)


def passed_along(x, axis, by):
    count = lax.axis_size(axis)
    return lax.ppermute(x, axis, [(i, (i + by) % count) for i in range(count)])


def with_halo(x, sides, width):
    for axis, dim in sides:
        count, length = (lax.axis_size(axis), x.shape[dim])
        up = [(i, (i + 1) % count) for i in range(count - 1)]
        down = [(j, i) for i, j in up]
        last = lax.slice_in_dim(x, length - width, length, axis=dim)
        initial = lax.slice_in_dim(x, 0, width, axis=dim)
        before = lax.ppermute(last, axis, up)
        after = lax.ppermute(initial, axis, down)
        x = jnp.concatenate([before, x, after], axis=dim)
    return x


def from_partner(x, axis, bit):
    return lax.ppermute(x, axis, [(i, i ^ 1 << bit) for i in range(lax.axis_size(axis))])


def tap_sum(padded, weight, slab_depth, height, grid_width, flipped):
    summed = jnp.zeros((slab_depth, height, grid_width, padded.shape[-1]), jnp.float32)
    for depth_tap in range(3):
        for row_tap in range(3):
            for col_tap in range(3):
                tap_index = 9 * depth_tap + 3 * row_tap + col_tap
                if flipped:
                    starts = (2 - depth_tap, 2 - row_tap, 2 - col_tap)
                else:
                    starts = (depth_tap, row_tap, col_tap)
                window_part = padded[
                    starts[0] : starts[0] + slab_depth,
                    starts[1] : starts[1] + height,
                    starts[2] : starts[2] + grid_width,
                ]
                summed = summed + weight[tap_index] * window_part.astype(jnp.float32)
    return summed


def into_blocks(field):
    slab_depth, height, grid_width, channels = field.shape
    shaped = field.reshape(slab_depth, height // WH, WH, grid_width // WW, WW, channels)
    shaped = shaped.transpose(1, 3, 0, 2, 4, 5)
    return shaped.reshape(height // WH * (grid_width // WW), slab_depth * WH * WW, channels)


def out_of_blocks(blocks, slab_depth, height, grid_width):
    channels = blocks.shape[-1]
    shaped = blocks.reshape(height // WH, grid_width // WW, slab_depth, WH, WW, channels)
    shaped = shaped.transpose(2, 0, 3, 1, 4, 5)
    return shaped.reshape(slab_depth, height, grid_width, channels)


def roll_local(field, rows_shift, cols_shift, direction):
    return jnp.roll(field, (direction * rows_shift, direction * cols_shift), axis=(1, 2))


def into_frame(field, rows_shift, cols_shift):
    return passed_along(roll_local(field, rows_shift, cols_shift, -1), "seq", -1)


def out_of_frame(field, rows_shift, cols_shift):
    moved = passed_along(field, "seq", 1)
    return roll_local(moved, rows_shift, cols_shift, 1)


def unit_rows(values):
    as_float = values.astype(jnp.float32)
    radius = jnp.sqrt(jnp.sum(as_float * as_float, axis=-1, keepdims=True) + 1.0)
    return (as_float, radius, (as_float / radius).astype(jnp.bfloat16))


def radius_back(as_float, radius, back_unit):
    inner = jnp.sum(as_float * back_unit, axis=-1, keepdims=True)
    return back_unit / radius - as_float * inner / (radius * radius * radius)


def window_forward(unit_query, unit_key, values, allowed, head_scale):
    cosine = jnp.einsum("wqhe,wkhe->whqk", unit_query, unit_key, preferred_element_type=jnp.float32)
    expo = jnp.exp(head_scale[:, None, None] * cosine) * allowed[:, None]
    probability = expo / jnp.sum(expo, axis=-1, keepdims=True)
    weights = probability.astype(jnp.bfloat16)
    attended = jnp.einsum(
        "whqk,wkhe->wqhe", weights, values, preferred_element_type=jnp.float32
    ).astype(jnp.bfloat16)
    return (cosine, probability, weights, attended)


def window_backward(unit_query, unit_key, values, head_scale, back_attended, forward_parts):
    cosine, probability, weights = forward_parts
    back_value = jnp.einsum(
        "whqk,wqhe->wkhe", weights, back_attended, preferred_element_type=jnp.float32
    )
    back_prob = jnp.einsum(
        "wqhe,wkhe->whqk", back_attended, values, preferred_element_type=jnp.float32
    )
    back_score = probability * (
        back_prob - jnp.sum(probability * back_prob, axis=-1, keepdims=True)
    )
    scale_rows = jnp.sum(back_score * cosine, axis=-1)
    scaled = (back_score * head_scale[:, None, None]).astype(jnp.bfloat16)
    back_uq = jnp.einsum("whqk,wkhe->wqhe", scaled, unit_key, preferred_element_type=jnp.float32)
    back_uk = jnp.einsum("whqk,wqhe->wkhe", scaled, unit_query, preferred_element_type=jnp.float32)
    return (back_uq, back_uk, back_value, scale_rows)


def order_halves(mine, other, upper_half):
    return jnp.where(
        upper_half, jnp.concatenate([other, mine], axis=1), jnp.concatenate([mine, other], axis=1)
    )


def pick_half(both, upper_half):
    middle = both.shape[1] // 2
    lower = both[:, :middle]
    higher = both[:, middle:]
    return (jnp.where(upper_half, higher, lower), jnp.where(upper_half, lower, higher))


def per_device(tokens, cotangent, w_qkv, w_proj, conv_weight, norm_gain, head_scale, shift_offsets):
    full_qkv, full_proj = (
        lax.all_gather(w_qkv, "dp", axis=0, tiled=True),
        lax.all_gather(w_proj, "dp", axis=0, tiled=True),
    )
    slab = tokens[0]
    slab_depth, height, grid_width, channels = slab.shape
    head_count = head_scale.shape[0]
    head_dim = channels // head_count
    seq_count = lax.axis_size("seq")
    seq_index = lax.axis_index("seq")
    rows_shift = shift_offsets[0]
    cols_shift = shift_offsets[1]
    spatial = ((0, 0), (1, 1), (1, 1), (0, 0))
    padded_tokens = jnp.pad(with_halo(slab, (("seq", 0),), 1), spatial)
    mixed_field = slab.astype(jnp.float32) + tap_sum(
        padded_tokens, conv_weight, slab_depth, height, grid_width, False
    )
    centred = mixed_field - jnp.mean(mixed_field, axis=-1, keepdims=True)
    inverse_std = lax.rsqrt(jnp.mean(centred * centred, axis=-1, keepdims=True) + 1e-05)
    unit_field = centred * inverse_std
    normed = (unit_field * norm_gain).astype(jnp.bfloat16)
    position_count = slab_depth * height * grid_width
    row_code = 2 * (jnp.arange(height) >= height - rows_shift).astype(jnp.int32)
    col_code = (jnp.arange(grid_width) >= grid_width - cols_shift).astype(jnp.int32)
    plane_code = row_code[:, None] + col_code[None, :]
    grid_code = jnp.broadcast_to(plane_code[None, :, :, None], (slab_depth, height, grid_width, 1))
    block_code = into_blocks(grid_code)[..., 0]
    cotangent_rows = cotangent[0].reshape(position_count, channels)
    back_restored = jnp.einsum(
        "tc,dc->td", cotangent_rows, full_proj, preferred_element_type=jnp.float32
    ).astype(jnp.bfloat16)
    back_restored_field = back_restored.reshape(slab_depth, height, grid_width, channels)
    shifted = into_frame(normed, rows_shift, cols_shift)
    shifted_rows = shifted.reshape(position_count, channels)
    qkv = jnp.dot(shifted_rows, full_qkv, preferred_element_type=jnp.float32).astype(jnp.bfloat16)
    qkv = qkv.reshape(slab_depth, height, grid_width, 3 * channels)
    upper_half = seq_index % 2 == 1
    partner_kv = from_partner(qkv[..., channels:], "seq", 0)
    key_code = order_halves(block_code, block_code, upper_half)
    my_allowed = (block_code[:, :, None] == key_code[:, None, :]).astype(jnp.float32)
    my_blocks = into_blocks(qkv)
    block_count = my_blocks.shape[0]
    half_positions = my_blocks.shape[1]

    def split_heads(part):
        return part.reshape(block_count, half_positions, head_count, head_dim)

    def merge_heads(part):
        return part.reshape(block_count, half_positions, channels)

    query = split_heads(my_blocks[..., :channels])
    my_key = split_heads(my_blocks[..., channels : 2 * channels])
    my_value = split_heads(my_blocks[..., 2 * channels :])
    partner_blocks = into_blocks(partner_kv)
    partner_key = split_heads(partner_blocks[..., :channels])
    partner_value = split_heads(partner_blocks[..., channels:])
    query_float, query_radius, unit_query = unit_rows(query)
    key_float, key_radius, my_unit_key = unit_rows(my_key)
    unused_a, unused_b, partner_unit_key = unit_rows(partner_key)
    unit_key = order_halves(my_unit_key, partner_unit_key, upper_half)
    all_values = order_halves(my_value, partner_value, upper_half)
    forward_all = window_forward(unit_query, unit_key, all_values, my_allowed, head_scale)
    restored = out_of_frame(
        out_of_blocks(merge_heads(forward_all[3]), slab_depth, height, grid_width),
        rows_shift,
        cols_shift,
    )
    back_attended = into_frame(back_restored_field, rows_shift, cols_shift)
    back_heads = split_heads(into_blocks(back_attended))
    back_uq, back_uk, back_value, scale_rows = window_backward(
        unit_query, unit_key, all_values, head_scale, back_heads, forward_all[:3]
    )
    scale_part = jnp.sum(scale_rows, axis=(0, 2))
    mine_uk, other_uk = pick_half(back_uk, upper_half)
    mine_value, other_value = pick_half(back_value, upper_half)
    received = from_partner(
        jnp.stack([other_uk, other_value]).astype(jnp.bfloat16), "seq", 0
    ).astype(jnp.float32)
    mine_uk = mine_uk + received[0]
    mine_value = mine_value + received[1]
    back_query = radius_back(query_float, query_radius, back_uq)
    back_key = radius_back(key_float, key_radius, mine_uk)
    back_blocks = jnp.concatenate(
        [merge_heads(back_query), merge_heads(back_key), merge_heads(mine_value)], axis=-1
    ).astype(jnp.bfloat16)
    back_qkv_rows = out_of_blocks(back_blocks, slab_depth, height, grid_width).reshape(
        position_count, 3 * channels
    )
    back_shifted = jnp.einsum(
        "tj,cj->tc", back_qkv_rows, full_qkv, preferred_element_type=jnp.float32
    ).astype(jnp.bfloat16)
    back_normed = out_of_frame(
        back_shifted.reshape(slab_depth, height, grid_width, channels), rows_shift, cols_shift
    )
    restored_rows = restored.reshape(position_count, channels)
    projected = jnp.dot(restored_rows, full_proj, preferred_element_type=jnp.float32)
    output = (mixed_field + projected.reshape(slab_depth, height, grid_width, channels)).astype(
        jnp.bfloat16
    )
    back_float = back_normed.astype(jnp.float32)
    gain_part = jnp.sum(back_float * unit_field, axis=(0, 1, 2))
    grad_unit = back_float * norm_gain
    back_mixed = cotangent[0].astype(jnp.float32) + inverse_std * (
        grad_unit
        - jnp.mean(grad_unit, axis=-1, keepdims=True)
        - unit_field * jnp.mean(grad_unit * unit_field, axis=-1, keepdims=True)
    )
    padded_back = jnp.pad(
        with_halo(back_mixed.astype(jnp.bfloat16), (("seq", 0),), 1).astype(back_mixed.dtype),
        spatial,
    )
    grad_tokens = (
        back_mixed + tap_sum(padded_back, conv_weight, slab_depth, height, grid_width, True)
    ).astype(jnp.bfloat16)
    conv_rows = []
    for depth_tap in range(3):
        for row_tap in range(3):
            for col_tap in range(3):
                window_part = padded_tokens[
                    depth_tap : depth_tap + slab_depth,
                    row_tap : row_tap + height,
                    col_tap : col_tap + grid_width,
                ]
                conv_rows.append(
                    jnp.sum(back_mixed * window_part.astype(jnp.float32), axis=(0, 1, 2))
                )
    conv_part = jnp.stack(conv_rows)
    qkv_term = jnp.einsum(
        "tc,tj->cj", shifted_rows, back_qkv_rows, preferred_element_type=jnp.float32
    )
    proj_term = jnp.einsum(
        "tc,tj->cj", restored_rows, cotangent_rows, preferred_element_type=jnp.float32
    )
    grads = jnp.concatenate([qkv_term, proj_term], axis=1)
    width = grads.shape[1] // 2
    odd = seq_index % 2 == 1
    mine = jnp.where(odd, grads[:, width:], grads[:, :width])
    given = jnp.where(odd, grads[:, :width], grads[:, width:]).astype(jnp.bfloat16)
    mine = mine + from_partner(given, "seq", 0).astype(jnp.float32)
    tiles = mine.reshape(2, 2, XC, channels // (32 * XC), 8, width // 128, 128)
    tiles = tiles.transpose(0, 1, 2, 3, 5, 4, 6).astype(jnp.bfloat16)
    summed = reduce_all(tiles.reshape(2, 2, XC, ZC, -1, 8, 128))
    summed = summed.reshape(2, 2, XC, channels // (32 * XC), width // 128, 8, 128)
    totals = summed.transpose(1, 2, 3, 5, 0, 4, 6).reshape(channels // 2, 2 * width)
    totals = totals.astype(jnp.float32)
    conv_total, gain_total, scale_total = lax.psum(
        (conv_part, gain_part, scale_part), ("rep", "dp", "seq")
    )
    factor = 1.0 / math.sqrt(
        lax.axis_size("rep") * lax.axis_size("dp") * seq_count * position_count
    )
    return (
        output[None],
        grad_tokens[None],
        totals[:, : 3 * channels] * factor,
        totals[:, 3 * channels :] * factor,
        conv_total * factor,
        gain_total * factor,
        scale_total * factor,
    )


def solution(mesh):
    in_specs = (
        P(("rep", "dp"), "seq", None, None, None),
        P(("rep", "dp"), "seq", None, None, None),
        P("dp", None),
        P("dp", None),
        P(),
        P(),
        P(),
        P(),
    )
    out_specs = (
        P(("rep", "dp"), "seq", None, None, None),
        P(("rep", "dp"), "seq", None, None, None),
        P("dp", None),
        P("dp", None),
        P(),
        P(),
        P(),
    )
    return jax.shard_map(
        per_device, mesh=mesh, in_specs=in_specs, out_specs=out_specs, check_vma=False
    )
```

```python
import math

import jax
import jax.numpy as jnp
from jax import lax
from jax.experimental import pallas as pl
from jax.experimental.pallas import tpu as pltpu
from jax.sharding import PartitionSpec as P

MESH = pl.DeviceIdType.MESH
BF = jnp.bfloat16
F32 = jnp.float32
XC = 4
ZC = 8
SEQ = 64
C = 768
MINE = 384
VMEM = pl.BlockSpec(memory_space=pltpu.VMEM)
SMEM = pl.BlockSpec(memory_space=pltpu.SMEM)
DMA = pltpu.SemaphoreType.DMA


def nn(a, b):
    return lax.dot_general(a, b, (((1,), (0,)), ((), ())), preferred_element_type=F32)


def nt(a, b):
    return lax.dot_general(a, b, (((1,), (1,)), ((), ())), preferred_element_type=F32)


def tn(a, b):
    return lax.dot_general(a, b, (((0,), (0,)), ((), ())), preferred_element_type=F32)


def iota(shape, dim):
    return lax.broadcasted_iota(jnp.int32, shape, dim)


def place():
    rep, dp, seq = lax.axis_index("rep"), lax.axis_index("dp"), lax.axis_index("seq")
    return (rep, dp, seq, lax.rem(seq, 2))


def send(src, dst, s, r, to):
    c = pltpu.make_async_remote_copy(
        src_ref=src, dst_ref=dst, send_sem=s, recv_sem=r, device_id=to, device_id_type=MESH
    )
    c.start()
    return c


def greet(peers):
    barrier = pltpu.get_barrier_semaphore()
    for peer in peers:
        pl.semaphore_signal(barrier, inc=1, device_id=peer, device_id_type=MESH)
    pl.semaphore_wait(barrier, len(peers))


def fill_padded(xf, before, own, after):
    rows = jnp.zeros((4, 1, 16, C), F32)
    xf[:, 0:1] = rows
    xf[:, 9:10] = rows
    xf[0, 1:9] = before
    xf[1:3, 1:9] = own
    xf[3, 1:9] = after


def taps(xf, weight, d, lanes, flipped):
    sums = [jnp.zeros((8, 16, 128), F32) for _ in range(3)]
    for a in range(3):
        for b in range(3):
            rows = xf[d + a, b : b + 8, :, lanes]
            for e in range(3):
                t = 9 * a + 3 * b + e
                t = 26 - t if flipped else t
                sums[e] = sums[e] + weight[t : t + 1, lanes][None] * rows
    w = iota((8, 16, 128), 1)
    left = jnp.where(w == 0, 0.0, pltpu.roll(sums[0], 1, 1))
    right = jnp.where(w == 15, 0.0, pltpu.roll(sums[2], 15, 1))
    return sums[1] + left + right


def chunk(j):
    return pl.ds(pl.multiple_of(j * 128, 128), 128)


def normalise(rows):
    centred = rows - jnp.mean(rows, axis=-1, keepdims=True)
    inverse = lax.rsqrt(jnp.mean(centred * centred, axis=-1, keepdims=True) + 1e-05)
    return (centred * inverse, inverse)


def mix_kernel(tokens, cot, wq_in, wp_in, weight, gain, nwin, cwin, wq, wp, mixed, halo,
               xf, h_send, h_recv, w_send, w_recv, l_sem):
    rep, dp, seq, core = place()
    y = rep * 2 + dp
    up = (rep, dp, lax.rem(seq + 1, SEQ))
    down = (rep, dp, lax.rem(seq + SEQ - 1, SEQ))
    partner = (rep, dp, lax.rem(seq + SEQ - 1 + 2 * core, SEQ))
    other_core = (rep, dp, seq + 1 - 2 * core)
    y_to = lax.rem(y + 3 + 2 * core, 4)
    y_from = lax.rem(y + 1 + 2 * core, 4)
    y_peer = (y_to // 2, lax.rem(y_to, 2), seq)
    y_source = (y_from // 2, lax.rem(y_from, 2), seq)
    greet([up, down, y_peer, y_source])
    own = 1 - core
    halos = [
        send(tokens.at[0], halo.at[1], h_send.at[0], h_recv.at[0], down),
        send(tokens.at[1], halo.at[0], h_send.at[1], h_recv.at[1], up),
    ]
    weights = [
        send(wq_in.at[core], wq.at[core, dp], w_send.at[0], w_recv.at[0], y_peer),
        send(wp_in.at[core], wp.at[core, dp], w_send.at[1], w_recv.at[1], y_peer),
    ]
    cots = send(cot, cwin.at[own], h_send.at[2], h_recv.at[2], partner)
    local = [
        pltpu.make_async_copy(cot, cwin.at[own], l_sem.at[0]),
        pltpu.make_async_copy(wq_in, wq.at[:, dp], l_sem.at[1]),
        pltpu.make_async_copy(wp_in, wp.at[:, dp], l_sem.at[2]),
    ]
    for c in local:
        c.start()
    for c in halos:
        c.wait()
    first = jnp.where(seq == 0, 0.0, 1.0).astype(F32)
    last = jnp.where(seq == SEQ - 1, 0.0, 1.0).astype(F32)
    fill_padded(xf, halo[0].astype(F32) * first, tokens[...].astype(F32), halo[1].astype(F32) * last)

    def filter_step(i, carry):
        d, j = i // 6, lax.rem(i, 6)
        lanes = chunk(j)
        mixed[d, :, :, lanes] = xf[d + 1, 1:9, :, lanes] + taps(xf, weight, d, lanes, False)
        return carry

    lax.fori_loop(0, 12, filter_step, 0)

    def norm_step(i, carry):
        d, h = i // 2, lax.rem(i, 2) * 4
        unit, _ = normalise(mixed[d, pl.ds(h, 4)].reshape(64, C))
        nwin[own, pl.ds(pl.multiple_of(i * 64, 64), 64)] = (unit * gain[...]).astype(BF)
        return carry

    lax.fori_loop(0, 4, norm_step, 0)
    norms = send(nwin.at[own], nwin.at[own], h_send.at[3], h_recv.at[3], partner)
    for c in weights:
        c.wait()
    back = [
        send(wq.at[core, 1 - dp], wq.at[core, 1 - dp], w_send.at[2], w_recv.at[2], other_core),
        send(wp.at[core, 1 - dp], wp.at[core, 1 - dp], w_send.at[3], w_recv.at[3], other_core),
    ]
    for c in local:
        c.wait()
    cots.wait()
    norms.wait()
    for c in back:
        c.wait()


def mix(tokens, cot, wq, wp, weight, gain):
    shape = jax.ShapeDtypeStruct
    return pl.pallas_call(
        mix_kernel,
        out_shape=(
            shape((2, 256, C), BF), shape((2, 256, C), BF),
            shape((2, 2, MINE, 3 * MINE), BF), shape((2, 2, MINE // 2, C), BF),
            shape((2, 8, 16, C), F32), shape((2, 8, 16, C), BF),
        ),
        in_specs=[VMEM] * 6,
        out_specs=(VMEM,) * 6,
        scratch_shapes=[
            pltpu.VMEM((4, 10, 16, C), F32),
            DMA((4,)), DMA((4,)), DMA((4,)), DMA((4,)), DMA((3,)),
        ],
        compiler_params=pltpu.CompilerParams(
            collective_id=1, has_side_effects=True, vmem_limit_bytes=48 << 20
        ),
        name="mix",
    )(tokens, cot, wq, wp, weight, gain)


def source_of(n, r):
    b, d, h, j = n >> 8, (n >> 6) & 3, (n >> 3) & 7, n & 7
    return d * 128 + h * 16 + ((8 * b + j + r) & 15)


def head_sums(x, ones):
    high = x.astype(BF)
    low = (x - high.astype(F32)).astype(BF)
    return nn(high, ones) + nn(low, ones)


def attend_kernel(shift, scales, nwin, cwin, wq, wp, own_out, given_out, g_out, scale_out,
                  x_s, ct_s, qkv_s, ba_s, att_s, bqkv_s, allow_s, gq_s, gp_s):
    core = lax.rem(lax.axis_index("seq"), 2)
    s, r = shift[0], shift[1]
    select = jnp.where(iota((512, 512), 1) == source_of(iota((512, 512), 0), r), 1.0, 0.0).astype(BF)
    x_s[...] = nn(select, nwin[...].reshape(512, C)).astype(BF)
    ct_s[...] = nn(select, cwin[...].reshape(512, C)).astype(BF)
    qkv_s[...] = nn(x_s[...], wq[core].reshape(C, 3 * MINE)).astype(BF)
    ba_s[...] = nt(ct_s[...], wp[core].reshape(MINE, C)).astype(BF)

    def code(n, b):
        h, j = (n >> 3) & 7, n & 7
        return jnp.where(h < s, 2, 0) + jnp.where(8 * b + j + r >= 16, 1, 0)

    for b in range(2):
        same = code(iota((256, 256), 0), b) == code(iota((256, 256), 1), b)
        allow_s[b] = jnp.where(same, 1.0, 0.0).astype(F32)
    ones = jnp.where(iota((128, 128), 0) // 32 == iota((128, 128), 1) // 32, 1.0, 0.0).astype(BF)
    lane_head = iota((256, 128), 1) // 32

    def group(i, carry):
        b, g = i // 3, lax.rem(i, 3)
        rows = pl.ds(pl.multiple_of(b * 256, 256), 256)

        def part(k):
            return pl.ds(pl.multiple_of(g * 128 + k * MINE, 128), 128)

        query = qkv_s[rows, part(0)].astype(F32)
        key = qkv_s[rows, part(1)].astype(F32)
        value = qkv_s[rows, part(2)]
        ba = ba_s[rows, part(0)]
        inv_q = lax.rsqrt(head_sums(query * query, ones) + 1.0)
        inv_k = lax.rsqrt(head_sums(key * key, ones) + 1.0)
        uq = (query * inv_q).astype(BF)
        uk = (key * inv_k).astype(BF)
        att = jnp.zeros((256, 128), F32)
        back_v = jnp.zeros((256, 128), F32)
        back_uq = jnp.zeros((256, 128), F32)
        back_uk = jnp.zeros((256, 128), F32)
        zero = jnp.zeros((256, 128), BF)
        for h in range(4):
            here = lane_head == h
            scale = scales[core, g * 4 + h]
            uq_h = jnp.where(here, uq, zero)
            uk_h = jnp.where(here, uk, zero)
            v_h = jnp.where(here, value, zero)
            ba_h = jnp.where(here, ba, zero)
            cosine = nt(uk_h, uq)
            expo = jnp.exp(scale * cosine) * allow_s[b]
            prob = expo * (1.0 / jnp.sum(expo, axis=0, keepdims=True))
            weights = prob.astype(BF)
            att = att + tn(weights, v_h)
            back_v = back_v + nn(weights, ba_h)
            back_prob = nt(v_h, ba)
            mean = jnp.sum(prob * back_prob, axis=0, keepdims=True)
            back_score = prob * (back_prob - mean)
            scale_out[b, pl.ds(g * 4 + h, 1)] = jnp.sum(back_score * cosine, axis=0, keepdims=True)
            scaled = (back_score * scale).astype(BF)
            back_uq = back_uq + tn(scaled, uk_h)
            back_uk = back_uk + nn(scaled, uq_h)
        att_s[rows, part(0)] = att.astype(BF)
        inner_q = head_sums(query * back_uq, ones)
        inner_k = head_sums(key * back_uk, ones)
        back_q = back_uq * inv_q - query * inner_q * (inv_q * inv_q * inv_q)
        back_k = back_uk * inv_k - key * inner_k * (inv_k * inv_k * inv_k)
        bqkv_s[rows, part(0)] = back_q.astype(BF)
        bqkv_s[rows, part(1)] = back_k.astype(BF)
        bqkv_s[rows, part(2)] = back_v.astype(BF)
        return carry

    lax.fori_loop(0, 6, group, 0)
    for half, out in ((1 - core, own_out), (core, given_out)):
        target = source_of(iota((256, 512), 1), r)
        restore = jnp.where(iota((256, 512), 0) + 256 * half == target, 1.0, 0.0).astype(BF)
        out[:, 0:MINE] = nn(restore, att_s[...]).astype(BF)
        out[:, MINE:] = nn(restore, bqkv_s[...]).astype(BF)
    gq_s[...] = tn(x_s[...], bqkv_s[...])
    gp_s[...] = tn(att_s[...], ct_s[...])

    def store(i, carry):
        d, p, x = i // 8, lax.rem(i // 4, 2), lax.rem(i, 4)
        for c in range(9):
            block = gq_s[pl.ds(pl.multiple_of(i * 48, 48), 48), c * 128 : (c + 1) * 128]
            g_out[d, p, x, c * 6 : c * 6 + 6] = block.reshape(6, 8, 128).astype(BF)
        for c in range(6):
            block = gp_s[pl.ds(pl.multiple_of(i * 24, 24), 24), c * 128 : (c + 1) * 128]
            g_out[d, p, x, 54 + c * 3 : 57 + c * 3] = block.reshape(3, 8, 128).astype(BF)
        return carry

    lax.fori_loop(0, 16, store, 0)


def attend(shift, scales, nwin, cwin, wq, wp):
    shape = jax.ShapeDtypeStruct
    return pl.pallas_call(
        attend_kernel,
        out_shape=(
            shape((256, 4 * MINE), BF), shape((256, 4 * MINE), BF),
            shape((2, 2, XC, 72, 8, 128), BF), shape((2, 12, 256), F32),
        ),
        in_specs=[SMEM, SMEM] + [VMEM] * 4,
        out_specs=(VMEM,) * 4,
        scratch_shapes=[
            pltpu.VMEM((512, C), BF), pltpu.VMEM((512, C), BF),
            pltpu.VMEM((512, 3 * MINE), BF), pltpu.VMEM((512, MINE), BF),
            pltpu.VMEM((512, MINE), BF), pltpu.VMEM((512, 3 * MINE), BF),
            pltpu.VMEM((2, 256, 256), F32), pltpu.VMEM((C, 3 * MINE), F32), pltpu.VMEM((MINE, C), F32),
        ],
        compiler_params=pltpu.CompilerParams(vmem_limit_bytes=48 << 20),
        name="attend",
    )(shift, scales, nwin, cwin, wq, wp)


def project_kernel(own, recv, wq, wp, mixed, cot, gain, out, bm, bmh, gain_out, bn_s):
    _, _, _, core = place()
    proj = nn(own[:, 0:MINE], wp[core].reshape(MINE, C))
    proj = proj + nn(recv[:, 0:MINE], wp[1 - core].reshape(MINE, C))
    out[...] = (mixed[...].reshape(256, C) + proj).astype(BF).reshape(2, 8, 16, C)
    back = nt(own[:, MINE:], wq[core].reshape(C, 3 * MINE))
    back = back + nt(recv[:, MINE:], wq[1 - core].reshape(C, 3 * MINE))
    bn_s[...] = back.astype(BF)

    def step(i, total):
        d, h = i // 2, lax.rem(i, 2) * 4
        rows = pl.ds(pl.multiple_of(i * 64, 64), 64)
        unit, inverse = normalise(mixed[d, pl.ds(h, 4)].reshape(64, C))
        back_float = bn_s[rows].astype(F32)
        total = total + jnp.sum((back_float * unit).reshape(8, 8, C), axis=0)
        grad_unit = back_float * gain[...]
        mean = jnp.mean(grad_unit, axis=-1, keepdims=True)
        slope = jnp.mean(grad_unit * unit, axis=-1, keepdims=True)
        result = cot[rows].astype(F32) + inverse * (grad_unit - mean - unit * slope)
        bm[d, pl.ds(h, 4)] = result.reshape(4, 16, C)
        bmh[d, pl.ds(h, 4)] = result.astype(BF).reshape(4, 16, C)
        return total

    total = lax.fori_loop(0, 4, step, jnp.zeros((8, C), F32))
    gain_out[...] = jnp.sum(total, axis=0, keepdims=True)


def project(own, recv, wq, wp, mixed, cot, gain):
    shape = jax.ShapeDtypeStruct
    field = (2, 8, 16, C)
    return pl.pallas_call(
        project_kernel,
        out_shape=(shape(field, BF), shape(field, F32), shape(field, BF), shape((1, C), F32)),
        in_specs=[VMEM] * 7,
        out_specs=(VMEM,) * 4,
        scratch_shapes=[pltpu.VMEM((256, C), BF)],
        compiler_params=pltpu.CompilerParams(vmem_limit_bytes=48 << 20),
        name="project",
    )(own, recv, wq, wp, mixed, cot, gain)


def unmix_kernel(bm, before, after, tokens, halo, weight, grad, conv_out, xf, tf, sh):
    _, _, seq, _ = place()
    first = jnp.where(seq == 0, 0.0, 1.0).astype(F32)
    last = jnp.where(seq == SEQ - 1, 0.0, 1.0).astype(F32)
    fill_padded(xf, before[...].astype(F32) * first, bm[...], after[...].astype(F32) * last)
    fill_padded(tf, halo[0].astype(F32) * first, tokens[...].astype(F32), halo[1].astype(F32) * last)

    def step(i, carry):
        d, j = i // 6, lax.rem(i, 6)
        lanes = chunk(j)
        own = xf[d + 1, 1:9, :, lanes]
        grad[d, :, :, lanes] = (own + taps(xf, weight, d, lanes, True)).astype(BF)
        w = iota((8, 16, 128), 1)
        sh[0, d, :, :, lanes] = jnp.where(w == 15, 0.0, pltpu.roll(own, 15, 1))
        sh[1, d, :, :, lanes] = own
        sh[2, d, :, :, lanes] = jnp.where(w == 0, 0.0, pltpu.roll(own, 1, 1))
        return carry

    lax.fori_loop(0, 12, step, 0)

    def conv_step(j, carry):
        lanes = chunk(j)
        for a in range(3):
            for b in range(3):
                rows = tf[a : a + 2, b : b + 8, :, lanes]
                for e in range(3):
                    total = jnp.sum((sh[e, :, :, :, lanes] * rows).reshape(16, 16, 128), axis=0)
                    t = 9 * a + 3 * b + e
                    conv_out[t : t + 1, lanes] = jnp.sum(total, axis=0, keepdims=True)
        return carry

    lax.fori_loop(0, 6, conv_step, 0)


def unmix(bm, before, after, tokens, halo, weight):
    shape = jax.ShapeDtypeStruct
    return pl.pallas_call(
        unmix_kernel,
        out_shape=(shape((2, 8, 16, C), BF), shape((27, C), F32)),
        in_specs=[VMEM] * 6,
        out_specs=(VMEM,) * 2,
        scratch_shapes=[
            pltpu.VMEM((4, 10, 16, C), F32), pltpu.VMEM((4, 10, 16, C), F32),
            pltpu.VMEM((3, 2, 8, 16, C), F32),
        ],
        compiler_params=pltpu.CompilerParams(vmem_limit_bytes=48 << 20),
        name="unmix",
    )(bm, before, after, tokens, halo, weight)


def reduce_kernel(g, small, out, small_out, ra0, ra1, sa0, sa1, rb0, rb1, sb, rc,
                   sy, sx, sz, qa, qb, qc,
               a_send, a_recv, b_send, b_recv, c_send, c_recv, d_send, d_recv,
                  e_send, e_recv, f_send, f_recv, h_send, h_recv):
    rep, dp, seq = lax.axis_index("rep"), lax.axis_index("dp"), lax.axis_index("seq")
    core = lax.rem(seq, 2)
    z = lax.rem(seq // 2, ZC)
    x = seq // (2 * ZC)
    y = rep * 2 + dp
    half = ZC // 2

    def at_y(step):
        there = lax.rem(y + step, 4)
        return (there // 2, lax.rem(there, 2), seq)

    def at_x(step):
        there = lax.rem(x + step, XC)
        return (rep, dp, (there * ZC + z) * 2 + core)

    def at_z(step):
        there = lax.rem(z + step, ZC)
        return (rep, dp, (x * ZC + there) * 2 + core)

    other_core = (rep, dp, (x * ZC + z) * 2 + 1 - core)
    other_rep = (1 - rep, dp, seq)
    peers = [at_y(k) for k in range(1, 4)] + [at_x(k) for k in range(1, XC)]
    peers += [at_z(k) for k in range(1, ZC)] + [other_core]
    greet(peers)

    copies = []
    for k in range(1, 4):
        to = at_y(k)
        copies.append(send(g.at[to[1], to[0], :, pl.ds(0, half)], ra0.at[k - 1],
                           a_send.at[k - 1], a_recv.at[k - 1], to))
    for k in range(1, XC):
        to = at_x(k)
        there = lax.rem(x + k, XC)
        copies.append(send(g.at[:, :, there, pl.ds(half, half)], ra1.at[k - 1],
                           a_send.at[k + 2], a_recv.at[k + 2], to))
    for k in range(1, 4):
        copies.append(send(small, qa.at[k - 1], a_send.at[k + 5], a_recv.at[k + 5], at_y(k)))
    for c in copies:
        c.wait()

    def add_a0(i, carry):
        total = g[dp, rep, i, pl.ds(0, half)].astype(jnp.float32)
        for k in range(3):
            total = total + ra0[k, i].astype(jnp.float32)
        sa0[i] = total.astype(jnp.bfloat16)
        return carry

    lax.fori_loop(0, XC, add_a0, 0)

    def add_a1(i, carry):
        d, r = lax.rem(i, 2), i // 2
        total = g[d, r, x, pl.ds(half, half)].astype(jnp.float32)
        for k in range(XC - 1):
            total = total + ra1[k, d, r].astype(jnp.float32)
        sa1[d, r] = total.astype(jnp.bfloat16)
        return carry

    lax.fori_loop(0, 4, add_a1, 0)
    sy[...] = small[...] + qa[0] + qa[1] + qa[2]

    copies = []
    for k in range(1, XC):
        there = lax.rem(x + k, XC)
        copies.append(send(sa0.at[there], rb0.at[k - 1], b_send.at[k - 1], b_recv.at[k - 1], at_x(k)))
    for k in range(1, 4):
        to = at_y(k)
        copies.append(send(sa1.at[to[1], to[0]], rb1.at[k - 1], b_send.at[k + 2], b_recv.at[k + 2], to))
    for k in range(1, XC):
        copies.append(send(sy, qb.at[k - 1], b_send.at[k + 5], b_recv.at[k + 5], at_x(k)))
    for c in copies:
        c.wait()

    def add_b(i, carry):
        total = sa0[x, i].astype(jnp.float32)
        for k in range(XC - 1):
            total = total + rb0[k, i].astype(jnp.float32)
        sb[i] = total.astype(jnp.bfloat16)
        total = sa1[dp, rep, i].astype(jnp.float32)
        for k in range(3):
            total = total + rb1[k, i].astype(jnp.float32)
        sb[i + half] = total.astype(jnp.bfloat16)
        return carry

    lax.fori_loop(0, half, add_b, 0)
    sx[...] = sy[...] + qb[0] + qb[1] + qb[2]

    copies = []
    for k in range(1, ZC):
        there = lax.rem(z + k, ZC)
        copies.append(send(sb.at[there], rc.at[k - 1], c_send.at[k - 1], c_recv.at[k - 1], at_z(k)))
        copies.append(send(sx.at[there], qc.at[k - 1], c_send.at[k + ZC - 2], c_recv.at[k + ZC - 2], at_z(k)))
    for c in copies:
        c.wait()
    total = sb[z].astype(jnp.float32)
    for k in range(ZC - 1):
        total = total + rc[k].astype(jnp.float32)
    out[core, rep, x, z] = total.astype(jnp.bfloat16)
    total = sx[z]
    for k in range(ZC - 1):
        total = total + qc[k]
    sz[core, z] = total

    copies = []
    for k in range(1, ZC):
        mine = out.at[core, rep, x, z]
        copies.append(send(mine, mine, d_send.at[k - 1], d_recv.at[k - 1], at_z(k)))
        copies.append(send(sz.at[core, z], sz.at[core, z], d_send.at[k + ZC - 2], d_recv.at[k + ZC - 2], at_z(k)))
    for c in copies:
        c.wait()
    mine = out.at[core, rep, x]
    to_rep = send(mine, mine, e_send, e_recv, other_rep)
    handed = [send(mine, mine, h_send.at[0], h_recv.at[0], other_core)]
    handed.append(send(sz.at[core], sz.at[core], h_send.at[XC + 1], h_recv.at[XC + 1], other_core))
    to_rep.wait()
    theirs = out.at[core, 1 - rep, x]
    both = out.at[core, :, x]
    copies = []
    for k in range(1, XC):
        copies.append(send(both, both, f_send.at[k - 1], f_recv.at[k - 1], at_x(k)))
    handed.append(send(theirs, theirs, h_send.at[1], h_recv.at[1], other_core))
    for k in range(1, XC):
        copies[k - 1].wait()
        came = lax.rem(x + XC - k, XC)
        piece = out.at[core, :, came]
        handed.append(send(piece, piece, h_send.at[k + 1], h_recv.at[k + 1], other_core))
    for c in handed:
        c.wait()
    small_out[...] = sz[0] + sz[1]


def reduce_all(g, small):
    tail = g.shape[4:]
    half = ZC // 2
    bf = jnp.bfloat16
    dma = pltpu.SemaphoreType.DMA
    return pl.pallas_call(
        reduce_kernel,
        out_shape=(
            jax.ShapeDtypeStruct((2, 2, XC, ZC) + tail, bf),
            jax.ShapeDtypeStruct(small.shape, F32),
        ),
        in_specs=[VMEM] * 2,
        out_specs=(VMEM,) * 2,
        scratch_shapes=[
            pltpu.VMEM((3, XC, half) + tail, bf),
            pltpu.VMEM((XC - 1, 2, 2, half) + tail, bf),
            pltpu.VMEM((XC, half) + tail, bf),
            pltpu.VMEM((2, 2, half) + tail, bf),
            pltpu.VMEM((XC - 1, half) + tail, bf),
            pltpu.VMEM((3, half) + tail, bf),
            pltpu.VMEM((ZC,) + tail, bf),
            pltpu.VMEM((ZC - 1,) + tail, bf),
            pltpu.VMEM(small.shape, F32), pltpu.VMEM(small.shape, F32), pltpu.VMEM((2,) + small.shape, F32),
            pltpu.VMEM((3,) + small.shape, F32), pltpu.VMEM((XC - 1,) + small.shape, F32),
            pltpu.VMEM((ZC - 1,) + small.shape[1:], F32),
            dma((9,)), dma((9,)), dma((9,)), dma((9,)),
            dma((2 * ZC - 2,)), dma((2 * ZC - 2,)), dma((2 * ZC - 2,)), dma((2 * ZC - 2,)),
            dma, dma, dma((XC - 1,)), dma((XC - 1,)), dma((XC + 2,)), dma((XC + 2,)),
        ],
        compiler_params=pltpu.CompilerParams(
            collective_id=0, has_side_effects=True, vmem_limit_bytes=40 << 20
        ),
        cost_estimate=pl.CostEstimate(flops=10_000_000, bytes_accessed=60_000_000, transcendentals=0),
        name="grad_reduce",
    )(g, small)


def per_device(tokens, cotangent, w_qkv, w_proj, conv_weight, norm_gain, head_scale, shift_offsets):
    slab = tokens[0]
    seq_index = lax.axis_index("seq")
    core = seq_index % 2
    rows = w_qkv.shape[0]
    cot = cotangent[0].reshape(256, C)
    gain = norm_gain.reshape(1, C)
    wq = w_qkv.reshape(rows, 3, 2, 2, 192)
    wq = jnp.stack([wq[:, :, :, c].reshape(rows, 3 * MINE) for c in range(2)])
    wp = w_proj.reshape(2, 192, C)
    scales = head_scale.reshape(2, 2, 6).transpose(1, 0, 2).reshape(2, 12)
    nwin, cwin, wq, wp, mixed, halo = mix(slab, cot, wq, wp, conv_weight, gain)
    own, given, grads, scale_rows = attend(shift_offsets, scales, nwin, cwin, wq, wp)
    pairs = [(i, (i + (1 if i % 2 else -1)) % SEQ) for i in range(SEQ)]
    recv = lax.ppermute(given, "seq", pairs)
    output, bm, bmh, gain_part = project(own, recv, wq, wp, mixed, cot, gain)
    before = lax.ppermute(bmh[1], "seq", [(i, i + 1) for i in range(SEQ - 1)])
    after = lax.ppermute(bmh[0], "seq", [(i + 1, i) for i in range(SEQ - 1)])
    grad_tokens, conv_part = unmix(bm, before, after, slab, halo, conv_weight)
    mine = jnp.sum(scale_rows, axis=(0, 2)).reshape(2, 1, 6)
    mine = jnp.where(core == 0, jnp.pad(mine, ((0, 0), (0, 1), (0, 0))), jnp.pad(mine, ((0, 0), (1, 0), (0, 0))))
    small = jnp.concatenate([
        conv_part.reshape(-1, 128), gain_part.reshape(-1, 128),
        jnp.pad(mine.reshape(1, 24), ((0, 23), (0, 104))),
    ])
    summed, small = reduce_all(grads.reshape(2, 2, XC, ZC, 9, 8, 128), small.reshape(8, 24, 128))
    small = small.reshape(192, 128)
    factor = 1.0 / math.sqrt(
        lax.axis_size("rep") * lax.axis_size("dp") * SEQ * 256
    )
    summed = summed.reshape(2, 2, XC, 72, 8, 128).astype(F32) * factor
    part = summed[:, :, :, :54].reshape(2, 2, XC, 9, 6, 8, 128).transpose(1, 2, 4, 5, 0, 3, 6)
    part = part.reshape(384, 2, 3, 2, 192).transpose(0, 2, 3, 1, 4).reshape(384, 3 * C)
    proj = summed[:, :, :, 54:].reshape(2, 2, XC, 6, 3, 8, 128).transpose(0, 1, 2, 4, 5, 3, 6)
    small = small * factor
    return (
        output[None],
        grad_tokens[None],
        part,
        proj.reshape(384, C),
        small[:162].reshape(27, C),
        small[162:168].reshape(C),
        small[168, :24],
    )


def solution(mesh):
    in_specs = (
        P(("rep", "dp"), "seq", None, None, None),
        P(("rep", "dp"), "seq", None, None, None),
        P("dp", None),
        P("dp", None),
        P(),
        P(),
        P(),
        P(),
    )
    out_specs = (
        P(("rep", "dp"), "seq", None, None, None),
        P(("rep", "dp"), "seq", None, None, None),
        P("dp", None),
        P("dp", None),
        P(),
        P(),
        P(),
    )
    return jax.shard_map(
        per_device, mesh=mesh, in_specs=in_specs, out_specs=out_specs, check_vma=False
    )
```

```python
import math

import jax
import jax.numpy as jnp
from jax import lax
from jax.experimental import pallas as pl
from jax.experimental.pallas import tpu as pltpu
from jax.sharding import PartitionSpec as P

MESH = pl.DeviceIdType.MESH
BF = jnp.bfloat16
F32 = jnp.float32
XC = 4
ZC = 8
SEQ = 64
C = 768
MINE = 384
VMEM = pl.BlockSpec(memory_space=pltpu.VMEM)
SMEM = pl.BlockSpec(memory_space=pltpu.SMEM)
DMA = pltpu.SemaphoreType.DMA


def nn(a, b):
    return lax.dot_general(a, b, (((1,), (0,)), ((), ())), preferred_element_type=F32)


def nt(a, b):
    return lax.dot_general(a, b, (((1,), (1,)), ((), ())), preferred_element_type=F32)


def tn(a, b):
    return lax.dot_general(a, b, (((0,), (0,)), ((), ())), preferred_element_type=F32)


def iota(shape, dim):
    return lax.broadcasted_iota(jnp.int32, shape, dim)


def place():
    rep, dp, seq = lax.axis_index("rep"), lax.axis_index("dp"), lax.axis_index("seq")
    return (rep, dp, seq, lax.rem(seq, 2))


def send(src, dst, s, r, to):
    c = pltpu.make_async_remote_copy(
        src_ref=src, dst_ref=dst, send_sem=s, recv_sem=r, device_id=to, device_id_type=MESH
    )
    c.start()
    return c


def greet(peers):
    barrier = pltpu.get_barrier_semaphore()
    for peer in peers:
        pl.semaphore_signal(barrier, inc=1, device_id=peer, device_id_type=MESH)
    pl.semaphore_wait(barrier, len(peers))


def fill_padded(xf, before, own, after):
    rows = jnp.zeros((4, 1, 16, C), F32)
    xf[:, 0:1] = rows
    xf[:, 9:10] = rows
    xf[0, 1:9] = before
    xf[1:3, 1:9] = own
    xf[3, 1:9] = after


def taps(xf, weight, d, lanes, flipped):
    sums = [jnp.zeros((8, 16, 128), F32) for _ in range(3)]
    for a in range(3):
        for b in range(3):
            rows = xf[d + a, b : b + 8, :, lanes]
            for e in range(3):
                t = 9 * a + 3 * b + e
                t = 26 - t if flipped else t
                sums[e] = sums[e] + weight[t : t + 1, lanes][None] * rows
    w = iota((8, 16, 128), 1)
    left = jnp.where(w == 0, 0.0, pltpu.roll(sums[0], 1, 1))
    right = jnp.where(w == 15, 0.0, pltpu.roll(sums[2], 15, 1))
    return sums[1] + left + right


def chunk(j):
    return pl.ds(pl.multiple_of(j * 128, 128), 128)


def normalise(rows):
    centred = rows - jnp.mean(rows, axis=-1, keepdims=True)
    inverse = lax.rsqrt(jnp.mean(centred * centred, axis=-1, keepdims=True) + 1e-05)
    return (centred * inverse, inverse)


def arrange(w, into, dp):
    lane, other = iota((128, 128), 0), iota((128, 128), 1)
    moves = {}
    for had in range(2):
        for gets in range(2):
            hit = (lane - 64 * had == other - 64 * gets) & (other // 64 == gets)
            moves[had, gets] = jnp.where(hit, 1.0, 0.0).astype(BF)
    for c in range(2):
        for k in range(9):
            pieces = []
            for gets in range(2):
                part, block = (2 * k + gets) // 6, (2 * k + gets) % 6
                old = part * 12 + block // 3 * 6 + c * 3 + block % 3
                start = old // 2 * 128
                pieces.append(nn(w[:, start : start + 128], moves[old % 2, gets]))
            into[c, dp, :, k * 128 : k * 128 + 128] = (pieces[0] + pieces[1]).astype(BF)


def mix_kernel(tokens, cot, wq_in, wp_in, weight, gain, nwin, cwin, wq, wp, mixed, halo,
               xf, h_send, h_recv, w_send, w_recv, l_sem):
    rep, dp, seq, core = place()
    y = rep * 2 + dp
    up = (rep, dp, lax.rem(seq + 1, SEQ))
    down = (rep, dp, lax.rem(seq + SEQ - 1, SEQ))
    partner = (rep, dp, lax.rem(seq + SEQ - 1 + 2 * core, SEQ))
    other_core = (rep, dp, seq + 1 - 2 * core)
    y_to = lax.rem(y + 3 + 2 * core, 4)
    y_from = lax.rem(y + 1 + 2 * core, 4)
    y_peer = (y_to // 2, lax.rem(y_to, 2), seq)
    y_source = (y_from // 2, lax.rem(y_from, 2), seq)
    greet([up, down, y_peer, y_source])
    own = 1 - core
    halos = [
        send(tokens.at[0], halo.at[1], h_send.at[0], h_recv.at[0], down),
        send(tokens.at[1], halo.at[0], h_send.at[1], h_recv.at[1], up),
    ]
    cots = send(cot, cwin.at[own], h_send.at[2], h_recv.at[2], partner)
    local = [
        pltpu.make_async_copy(cot, cwin.at[own], l_sem.at[0]),
        pltpu.make_async_copy(wp_in, wp.at[:, dp], l_sem.at[1]),
    ]
    for c in local:
        c.start()
    arrange(wq_in, wq, dp)
    weights = [
        send(wq.at[core, dp], wq.at[core, dp], w_send.at[0], w_recv.at[0], y_peer),
        send(wp_in.at[core], wp.at[core, dp], w_send.at[1], w_recv.at[1], y_peer),
    ]
    for c in halos:
        c.wait()
    first = jnp.where(seq == 0, 0.0, 1.0).astype(F32)
    last = jnp.where(seq == SEQ - 1, 0.0, 1.0).astype(F32)
    fill_padded(xf, halo[0].astype(F32) * first, tokens[...].astype(F32), halo[1].astype(F32) * last)

    def filter_step(i, carry):
        d, j = i // 6, lax.rem(i, 6)
        lanes = chunk(j)
        mixed[d, :, :, lanes] = xf[d + 1, 1:9, :, lanes] + taps(xf, weight, d, lanes, False)
        return carry

    lax.fori_loop(0, 12, filter_step, 0)

    def norm_step(i, carry):
        d, h = i // 2, lax.rem(i, 2) * 4
        unit, _ = normalise(mixed[d, pl.ds(h, 4)].reshape(64, C))
        nwin[own, pl.ds(pl.multiple_of(i * 64, 64), 64)] = (unit * gain[...]).astype(BF)
        return carry

    lax.fori_loop(0, 4, norm_step, 0)
    norms = send(nwin.at[own], nwin.at[own], h_send.at[3], h_recv.at[3], partner)
    for c in weights:
        c.wait()
    back = [
        send(wq.at[core, 1 - dp], wq.at[core, 1 - dp], w_send.at[2], w_recv.at[2], other_core),
        send(wp.at[core, 1 - dp], wp.at[core, 1 - dp], w_send.at[3], w_recv.at[3], other_core),
    ]
    for c in local:
        c.wait()
    cots.wait()
    norms.wait()
    for c in back:
        c.wait()


def mix(tokens, cot, wq, wp, weight, gain):
    shape = jax.ShapeDtypeStruct
    return pl.pallas_call(
        mix_kernel,
        out_shape=(
            shape((2, 256, C), BF), shape((2, 256, C), BF),
            shape((2, 2, MINE, 3 * MINE), BF), shape((2, 2, MINE // 2, C), BF),
            shape((2, 8, 16, C), F32), shape((2, 8, 16, C), BF),
        ),
        in_specs=[VMEM] * 6,
        out_specs=(VMEM,) * 6,
        scratch_shapes=[
            pltpu.VMEM((4, 10, 16, C), F32),
            DMA((4,)), DMA((4,)), DMA((4,)), DMA((4,)), DMA((2,)),
        ],
        compiler_params=pltpu.CompilerParams(
            collective_id=1, has_side_effects=True, vmem_limit_bytes=48 << 20
        ),
        name="mix",
    )(tokens, cot, wq, wp, weight, gain)


def source_of(n, r):
    b, d, h, j = n >> 8, (n >> 6) & 3, (n >> 3) & 7, n & 7
    return d * 128 + h * 16 + ((8 * b + j + r) & 15)


def head_sums(x, ones):
    high = x.astype(BF)
    low = (x - high.astype(F32)).astype(BF)
    return nn(high, ones) + nn(low, ones)


def attend_kernel(shift, scales, nwin, cwin, wq, wp, own_out, given_out, g_out, scale_out,
                  x_s, ct_s, qkv_s, ba_s, att_s, bqkv_s, allow_s, gq_s, gp_s):
    core = lax.rem(lax.axis_index("seq"), 2)
    s, r = shift[0], shift[1]
    select = jnp.where(iota((512, 512), 1) == source_of(iota((512, 512), 0), r), 1.0, 0.0).astype(BF)
    x_s[...] = nn(select, nwin[...].reshape(512, C)).astype(BF)
    ct_s[...] = nn(select, cwin[...].reshape(512, C)).astype(BF)
    qkv_s[...] = nn(x_s[...], wq[core].reshape(C, 3 * MINE)).astype(BF)
    ba_s[...] = nt(ct_s[...], wp[core].reshape(MINE, C)).astype(BF)

    def code(n, b):
        h, j = (n >> 3) & 7, n & 7
        return jnp.where(h < s, 2, 0) + jnp.where(8 * b + j + r >= 16, 1, 0)

    for b in range(2):
        same = code(iota((256, 256), 0), b) == code(iota((256, 256), 1), b)
        allow_s[b] = jnp.where(same, 1.0, 0.0).astype(F32)
    scale_out[...] = jnp.zeros((2, 16, 256), F32)
    ones = jnp.where(iota((128, 128), 0) // 32 == iota((128, 128), 1) // 32, 1.0, 0.0).astype(BF)
    lane_head = iota((256, 128), 1) // 32

    def group(i, carry):
        b, g = i // 3, lax.rem(i, 3)
        rows = pl.ds(pl.multiple_of(b * 256, 256), 256)

        def part(k):
            return pl.ds(pl.multiple_of(g * 128 + k * MINE, 128), 128)

        query = qkv_s[rows, part(0)].astype(F32)
        key = qkv_s[rows, part(1)].astype(F32)
        value = qkv_s[rows, part(2)]
        ba = ba_s[rows, part(0)]
        inv_q = lax.rsqrt(head_sums(query * query, ones) + 1.0)
        inv_k = lax.rsqrt(head_sums(key * key, ones) + 1.0)
        uq = (query * inv_q).astype(BF)
        uk = (key * inv_k).astype(BF)
        att = jnp.zeros((256, 128), F32)
        back_v = jnp.zeros((256, 128), F32)
        back_uq = jnp.zeros((256, 128), F32)
        back_uk = jnp.zeros((256, 128), F32)
        zero = jnp.zeros((256, 128), BF)
        for h in range(4):
            here = lane_head == h
            scale = scales[core, g * 4 + h]
            uq_h = jnp.where(here, uq, zero)
            uk_h = jnp.where(here, uk, zero)
            v_h = jnp.where(here, value, zero)
            ba_h = jnp.where(here, ba, zero)
            cosine = nt(uk_h, uq)
            expo = jnp.exp(scale * cosine) * allow_s[b]
            prob = expo * (1.0 / jnp.sum(expo, axis=0, keepdims=True))
            weights = prob.astype(BF)
            att = att + tn(weights, v_h)
            back_v = back_v + nn(weights, ba_h)
            back_prob = nt(v_h, ba)
            mean = jnp.sum(prob * back_prob, axis=0, keepdims=True)
            back_score = prob * (back_prob - mean)
            scale_out[b, pl.ds(g * 4 + h, 1)] = jnp.sum(back_score * cosine, axis=0, keepdims=True)
            scaled = (back_score * scale).astype(BF)
            back_uq = back_uq + tn(scaled, uk_h)
            back_uk = back_uk + nn(scaled, uq_h)
        att_s[rows, part(0)] = att.astype(BF)
        inner_q = head_sums(query * back_uq, ones)
        inner_k = head_sums(key * back_uk, ones)
        back_q = back_uq * inv_q - query * inner_q * (inv_q * inv_q * inv_q)
        back_k = back_uk * inv_k - key * inner_k * (inv_k * inv_k * inv_k)
        bqkv_s[rows, part(0)] = back_q.astype(BF)
        bqkv_s[rows, part(1)] = back_k.astype(BF)
        bqkv_s[rows, part(2)] = back_v.astype(BF)
        return carry

    lax.fori_loop(0, 6, group, 0)
    for half, out in ((1 - core, own_out), (core, given_out)):
        target = source_of(iota((256, 512), 1), r)
        restore = jnp.where(iota((256, 512), 0) + 256 * half == target, 1.0, 0.0).astype(BF)
        out[:, 0:MINE] = nn(restore, att_s[...]).astype(BF)
        out[:, MINE:] = nn(restore, bqkv_s[...]).astype(BF)
    gq_s[...] = tn(x_s[...], bqkv_s[...])
    gp_s[...] = tn(att_s[...], ct_s[...])

    def store(i, carry):
        d, p, x = i // 8, lax.rem(i // 4, 2), lax.rem(i, 4)
        for c in range(9):
            block = gq_s[pl.ds(pl.multiple_of(i * 48, 48), 48), c * 128 : (c + 1) * 128]
            g_out[d, p, x, c * 6 : c * 6 + 6] = block.reshape(6, 8, 128).astype(BF)
        for c in range(6):
            block = gp_s[pl.ds(pl.multiple_of(i * 24, 24), 24), c * 128 : (c + 1) * 128]
            g_out[d, p, x, 54 + c * 3 : 57 + c * 3] = block.reshape(3, 8, 128).astype(BF)
        return carry

    lax.fori_loop(0, 16, store, 0)


def attend(shift, scales, nwin, cwin, wq, wp):
    shape = jax.ShapeDtypeStruct
    return pl.pallas_call(
        attend_kernel,
        out_shape=(
            shape((256, 4 * MINE), BF), shape((256, 4 * MINE), BF),
            shape((2, 2, XC, 72, 8, 128), BF), shape((2, 16, 256), F32),
        ),
        in_specs=[SMEM, SMEM] + [VMEM] * 4,
        out_specs=(VMEM,) * 4,
        scratch_shapes=[
            pltpu.VMEM((512, C), BF), pltpu.VMEM((512, C), BF),
            pltpu.VMEM((512, 3 * MINE), BF), pltpu.VMEM((512, MINE), BF),
            pltpu.VMEM((512, MINE), BF), pltpu.VMEM((512, 3 * MINE), BF),
            pltpu.VMEM((2, 256, 256), F32), pltpu.VMEM((C, 3 * MINE), F32), pltpu.VMEM((MINE, C), F32),
        ],
        compiler_params=pltpu.CompilerParams(vmem_limit_bytes=48 << 20),
        name="attend",
    )(shift, scales, nwin, cwin, wq, wp)


def finish_kernel(own, given, g, scale_rows, wq, wp, mixed, cot, tokens, halo, weight, gain,
                  out, grad, gq_out, gp_out, conv_out, gain_out, scale_out,
                  recv, bn_s, bm, bmh, ph, xf, tf, sh, ra0, ra1, sa0, sa1, rb0, rb1, sb, rc, full,
                  sm, s2, s3, sz, qy1, qx1, qx2, qy2, qz, s_sem, r_sem):
    rep, dp, seq, core = place()
    z = lax.rem(seq // 2, ZC)
    x = seq // (2 * ZC)
    y = rep * 2 + dp

    def at_y(step):
        there = lax.rem(y + step, 4)
        return (there // 2, lax.rem(there, 2), seq)

    def at_x(step):
        there = lax.rem(x + step, XC)
        return (rep, dp, (there * ZC + z) * 2 + core)

    def at_z(step):
        there = lax.rem(z + step, ZC)
        return (rep, dp, (x * ZC + there) * 2 + core)

    up = (rep, dp, lax.rem(seq + 1, SEQ))
    down = (rep, dp, lax.rem(seq + SEQ - 1, SEQ))
    partner = (rep, dp, lax.rem(seq + SEQ - 1 + 2 * core, SEQ))
    other_core = (rep, dp, seq + 1 - 2 * core)
    other_rep = (1 - rep, dp, seq)
    peers = [at_y(k) for k in range(1, 4)] + [at_x(k) for k in range(1, XC)]
    peers += [at_z(k) for k in range(1, ZC)] + [up, down]
    greet(peers)
    used = [0]

    def go(src, dst, to):
        n = used[0]
        used[0] += 1
        return send(src, dst, s_sem.at[n], r_sem.at[n], to)

    def finish(copies):
        for c in copies:
            c.wait()

    low, high = pl.ds(0, 36), pl.ds(36, 36)
    exchange = go(given, recv, partner)
    stage = []
    for k in range(1, 4):
        to = at_y(k)
        stage.append(go(g.at[to[1], to[0], :, low], ra0.at[k - 1], to))
    for k in range(1, XC):
        stage.append(go(g.at[:, :, lax.rem(x + k, XC), high], ra1.at[k - 1], at_x(k)))

    first = jnp.where(seq == 0, 0.0, 1.0).astype(F32)
    last = jnp.where(seq == SEQ - 1, 0.0, 1.0).astype(F32)
    fill_padded(tf, halo[0].astype(F32) * first, tokens[...].astype(F32), halo[1].astype(F32) * last)
    exchange.wait()
    back = nt(own[:, MINE:], wq[core].reshape(C, 3 * MINE))
    back = back + nt(recv[:, MINE:], wq[1 - core].reshape(C, 3 * MINE))
    bn_s[...] = back.astype(BF)

    def norm_step(i, total):
        d, h = i // 2, lax.rem(i, 2) * 4
        rows = pl.ds(pl.multiple_of(i * 64, 64), 64)
        unit, inverse = normalise(mixed[d, pl.ds(h, 4)].reshape(64, C))
        back_float = bn_s[rows].astype(F32)
        total = total + jnp.sum((back_float * unit).reshape(8, 8, C), axis=0)
        grad_unit = back_float * gain[...]
        mean = jnp.mean(grad_unit, axis=-1, keepdims=True)
        slope = jnp.mean(grad_unit * unit, axis=-1, keepdims=True)
        result = cot[rows].astype(F32) + inverse * (grad_unit - mean - unit * slope)
        bm[d, pl.ds(h, 4)] = result.reshape(4, 16, C)
        bmh[d, pl.ds(h, 4)] = result.astype(BF).reshape(4, 16, C)
        return total

    gain_part = jnp.sum(lax.fori_loop(0, 4, norm_step, jnp.zeros((8, C), F32)), axis=0, keepdims=True)
    planes = [go(bmh.at[0], ph.at[1], down), go(bmh.at[1], ph.at[0], up)]
    proj = nn(own[:, 0:MINE], wp[core].reshape(MINE, C))
    proj = proj + nn(recv[:, 0:MINE], wp[1 - core].reshape(MINE, C))
    out[...] = (mixed[...].reshape(256, C) + proj).astype(BF).reshape(2, 8, 16, C)

    finish(stage)

    def add_a(i, carry):
        total = g[dp, rep, i, low].astype(F32)
        for k in range(3):
            total = total + ra0[k, i].astype(F32)
        sa0[i] = total.astype(BF)
        d, r = lax.rem(i, 2), i // 2
        total = g[d, r, x, high].astype(F32)
        for k in range(XC - 1):
            total = total + ra1[k, d, r].astype(F32)
        sa1[d, r] = total.astype(BF)
        return carry

    lax.fori_loop(0, 4, add_a, 0)
    stage = []
    for k in range(1, XC):
        stage.append(go(sa0.at[lax.rem(x + k, XC)], rb0.at[k - 1], at_x(k)))
    for k in range(1, 4):
        to = at_y(k)
        stage.append(go(sa1.at[to[1], to[0]], rb1.at[k - 1], to))

    finish(planes)
    fill_padded(xf, ph[0].astype(F32) * first, bm[...], ph[1].astype(F32) * last)

    def filter_step(i, carry):
        d, j = i // 6, lax.rem(i, 6)
        lanes = chunk(j)
        here = xf[d + 1, 1:9, :, lanes]
        grad[d, :, :, lanes] = (here + taps(xf, weight, d, lanes, True)).astype(BF)
        w = iota((8, 16, 128), 1)
        sh[0, d, :, :, lanes] = jnp.where(w == 15, 0.0, pltpu.roll(here, 15, 1))
        sh[1, d, :, :, lanes] = here
        sh[2, d, :, :, lanes] = jnp.where(w == 0, 0.0, pltpu.roll(here, 1, 1))
        return carry

    lax.fori_loop(0, 12, filter_step, 0)

    finish(stage)
    total = sa0[x].astype(F32)
    for k in range(XC - 1):
        total = total + rb0[k].astype(F32)
    sb[low] = total.astype(BF)
    total = sa1[dp, rep].astype(F32)
    for k in range(3):
        total = total + rb1[k].astype(F32)
    sb[high] = total.astype(BF)
    stage = []
    for k in range(1, ZC):
        stage.append(go(sb.at[pl.ds(lax.rem(z + k, ZC) * 9, 9)], rc.at[k - 1], at_z(k)))

    sm[...] = jnp.zeros((8, 32, 128), F32)

    def conv_step(j, carry):
        lanes = chunk(j)
        for a in range(3):
            for b in range(3):
                rows = tf[a : a + 2, b : b + 8, :, lanes]
                for e in range(3):
                    total = jnp.sum((sh[e, :, :, :, lanes] * rows).reshape(16, 16, 128), axis=0)
                    t = 9 * a + 3 * b + e
                    sm[j, t : t + 1] = jnp.sum(total, axis=0, keepdims=True)
        return carry

    lax.fori_loop(0, 6, conv_step, 0)
    for j in range(6):
        sm[j, 27:28] = gain_part[:, j * 128 : j * 128 + 128]
    scale = jnp.sum(scale_rows[0] + scale_rows[1], axis=-1, keepdims=True)
    sm[6, pl.ds(pl.multiple_of(core * 16, 16), 16)] = jnp.broadcast_to(scale, (16, 128))
    few, rest = pl.ds(0, 4), pl.ds(4, 4)
    little = []
    for k in range(1, 4):
        little.append(go(sm.at[few], qy1.at[k - 1], at_y(k)))
        little.append(go(sm.at[rest], qx1.at[k - 1], at_x(k)))

    finish(stage)
    mine = pl.ds(z * 9, 9)
    total = sb[mine].astype(F32)
    for k in range(ZC - 1):
        total = total + rc[k].astype(F32)
    full[core, rep, x, mine] = total.astype(BF)
    stage = []
    piece = full.at[core, rep, x, mine]
    for k in range(1, ZC):
        stage.append(go(piece, piece, at_z(k)))

    finish(little)
    s2[few] = sm[few] + qy1[0] + qy1[1] + qy1[2]
    s2[rest] = sm[rest] + qx1[0] + qx1[1] + qx1[2]
    little = []
    for k in range(1, 4):
        little.append(go(s2.at[few], qx2.at[k - 1], at_x(k)))
        little.append(go(s2.at[rest], qy2.at[k - 1], at_y(k)))

    finish(stage)
    piece = full.at[core, rep, x, low]
    stage = [go(piece, piece, other_rep)]
    piece = full.at[core, rep, x, high]
    stage += [go(piece, piece, at_x(k)) for k in range(1, XC)]
    piece = full.at[core, rep, x]
    handed = [go(piece, piece, other_core)]

    finish(little)
    s3[few] = s2[few] + qx2[0] + qx2[1] + qx2[2]
    s3[rest] = s2[rest] + qy2[0] + qy2[1] + qy2[2]
    little = [go(s3.at[lax.rem(z + k, ZC)], qz.at[k - 1], at_z(k)) for k in range(1, ZC)]

    finish(stage)
    piece = full.at[core, :, x, low]
    along = [go(piece, piece, at_x(k)) for k in range(1, XC)]
    piece = full.at[core, rep, :, high]
    across = go(piece, piece, other_rep)
    piece = full.at[core, 1 - rep, x, low]
    handed.append(go(piece, piece, other_core))
    for k in range(1, XC):
        piece = full.at[core, rep, lax.rem(x + k, XC), high]
        handed.append(go(piece, piece, other_core))

    finish(little)
    total = s3[z]
    for k in range(ZC - 1):
        total = total + qz[k]
    sz[core, z] = total
    little = [go(sz.at[core, z], sz.at[core, z], at_z(k)) for k in range(1, ZC)]

    for k in range(1, XC):
        along[k - 1].wait()
        piece = full.at[core, :, lax.rem(x + XC - k, XC), low]
        handed.append(go(piece, piece, other_core))
    across.wait()
    piece = full.at[core, 1 - rep, :, high]
    handed.append(go(piece, piece, other_core))
    finish(little)
    little = go(sz.at[core], sz.at[core], other_core)
    finish(handed)

    lane = iota((48, 128), 1)

    def assemble(i, carry):
        r, k = i // 4, lax.rem(i, 4)
        rows = pl.ds(pl.multiple_of(i * 48, 48), 48)
        for part in range(3):
            for m in range(6):
                halves = []
                for gets in range(2):
                    block = 2 * m + gets
                    c = block % 6 // 3
                    old = part * 6 + block // 6 * 3 + block % 3
                    tile = full[c, r, k, old // 2 * 6 : old // 2 * 6 + 6].astype(F32).reshape(48, 128)
                    halves.append(tile if old % 2 == gets else pltpu.roll(tile, 64, 1))
                start = part * C + m * 128
                gq_out[rows, start : start + 128] = jnp.where(lane < 64, halves[0], halves[1])
        for c in range(2):
            for m in range(6):
                tile = full[c, r, k, 54 + m * 3 : 57 + m * 3].astype(F32).reshape(24, 128)
                start = pl.multiple_of(c * 192 + i * 24, 8)
                gp_out[pl.ds(start, 24), m * 128 : m * 128 + 128] = tile
        return carry

    lax.fori_loop(0, 8, assemble, 0)
    little.wait()
    for j in range(6):
        total = sz[0, j] + sz[1, j]
        conv_out[:, j * 128 : j * 128 + 128] = total[0:27]
        gain_out[:, j * 128 : j * 128 + 128] = total[27:28]
    scale_out[...] = sz[0, 6] + sz[1, 6]


def finish_all(own, given, g, scale_rows, wq, wp, mixed, cot, tokens, halo, weight, gain):
    shape = jax.ShapeDtypeStruct
    field = (2, 8, 16, C)
    tile = (8, 128)
    some = (32, 128)
    copies = 1 + 6 + 2 + 6 + 7 + 6 + 7 + 6 + 5 + 7 + 4 + 4 + 7 + 4 + 1
    return pl.pallas_call(
        finish_kernel,
        out_shape=(
            shape(field, BF), shape(field, BF), shape((MINE, 3 * C), F32), shape((MINE, C), F32),
            shape((27, C), F32), shape((1, C), F32), shape(some, F32),
        ),
        in_specs=[VMEM] * 12,
        out_specs=(VMEM,) * 7,
        scratch_shapes=[
            pltpu.VMEM((256, 4 * MINE), BF), pltpu.VMEM((256, C), BF),
            pltpu.VMEM(field, F32), pltpu.VMEM(field, BF), pltpu.VMEM(field, BF),
            pltpu.VMEM((4, 10, 16, C), F32), pltpu.VMEM((4, 10, 16, C), F32), pltpu.VMEM((3,) + field, F32),
            pltpu.VMEM((3, XC, 36) + tile, BF), pltpu.VMEM((XC - 1, 2, 2, 36) + tile, BF),
            pltpu.VMEM((XC, 36) + tile, BF), pltpu.VMEM((2, 2, 36) + tile, BF),
            pltpu.VMEM((XC - 1, 36) + tile, BF), pltpu.VMEM((3, 36) + tile, BF),
            pltpu.VMEM((72,) + tile, BF), pltpu.VMEM((ZC - 1, 9) + tile, BF),
            pltpu.VMEM((2, 2, XC, 72) + tile, BF),
            pltpu.VMEM((8,) + some, F32), pltpu.VMEM((8,) + some, F32), pltpu.VMEM((8,) + some, F32),
            pltpu.VMEM((2, 8) + some, F32),
            pltpu.VMEM((3, 4) + some, F32), pltpu.VMEM((3, 4) + some, F32),
            pltpu.VMEM((3, 4) + some, F32), pltpu.VMEM((3, 4) + some, F32),
            pltpu.VMEM((ZC - 1,) + some, F32),
            DMA((copies,)), DMA((copies,)),
        ],
        compiler_params=pltpu.CompilerParams(
            collective_id=0, has_side_effects=True, vmem_limit_bytes=60 << 20
        ),
        name="finish",
    )(own, given, g, scale_rows, wq, wp, mixed, cot, tokens, halo, weight, gain)


def per_device(tokens, cotangent, w_qkv, w_proj, conv_weight, norm_gain, head_scale, shift_offsets):
    slab = tokens[0]
    cot = cotangent[0].reshape(256, C)
    gain = norm_gain.reshape(1, C)
    scales = head_scale.reshape(2, 2, 6).transpose(1, 0, 2).reshape(2, 12)
    nwin, cwin, wq, wp, mixed, halo = mix(slab, cot, w_qkv, w_proj.reshape(2, 192, C), conv_weight, gain)
    own, given, grads, scale_rows = attend(shift_offsets, scales, nwin, cwin, wq, wp)
    output, grad_tokens, grad_qkv, grad_proj, conv, gain_sum, scale = finish_all(
        own, given, grads, scale_rows, wq, wp, mixed, cot, slab, halo, conv_weight, gain
    )
    factor = 1.0 / math.sqrt(lax.axis_size("rep") * lax.axis_size("dp") * SEQ * 256)
    scale = scale[:, 0].reshape(2, 16)[:, :12].reshape(2, 2, 6).transpose(1, 0, 2).reshape(24)
    return (
        output[None],
        grad_tokens[None],
        grad_qkv * factor,
        grad_proj * factor,
        conv * factor,
        gain_sum.reshape(C) * factor,
        scale * factor,
    )


def solution(mesh):
    in_specs = (
        P(("rep", "dp"), "seq", None, None, None),
        P(("rep", "dp"), "seq", None, None, None),
        P("dp", None),
        P("dp", None),
        P(),
        P(),
        P(),
        P(),
    )
    out_specs = (
        P(("rep", "dp"), "seq", None, None, None),
        P(("rep", "dp"), "seq", None, None, None),
        P("dp", None),
        P("dp", None),
        P(),
        P(),
        P(),
    )
    return jax.shard_map(
        per_device, mesh=mesh, in_specs=in_specs, out_specs=out_specs, check_vma=False
    )
```

```python
import math

import jax
import jax.numpy as jnp
from jax import lax
from jax.experimental import pallas as pl
from jax.experimental.pallas import tpu as pltpu
from jax.sharding import PartitionSpec as P

MESH = pl.DeviceIdType.MESH
BF = jnp.bfloat16
F32 = jnp.float32
XC = 4
ZC = 8
SEQ = 64
C = 768
MINE = 384
TILES = (0, 36, 18)
VMEM = pl.BlockSpec(memory_space=pltpu.VMEM)
SMEM = pl.BlockSpec(memory_space=pltpu.SMEM)
DMA = pltpu.SemaphoreType.DMA


def nn(a, b):
    return lax.dot_general(a, b, (((1,), (0,)), ((), ())), preferred_element_type=F32)


def nt(a, b):
    return lax.dot_general(a, b, (((1,), (1,)), ((), ())), preferred_element_type=F32)


def tn(a, b):
    return lax.dot_general(a, b, (((0,), (0,)), ((), ())), preferred_element_type=F32)


def iota(shape, dim):
    return lax.broadcasted_iota(jnp.int32, shape, dim)


def place():
    rep, dp, seq = lax.axis_index("rep"), lax.axis_index("dp"), lax.axis_index("seq")
    return (rep, dp, seq, lax.rem(seq, 2))


def send(src, dst, s, r, to):
    c = pltpu.make_async_remote_copy(
        src_ref=src, dst_ref=dst, send_sem=s, recv_sem=r, device_id=to, device_id_type=MESH
    )
    c.start()
    return c


def greet(peers):
    barrier = pltpu.get_barrier_semaphore()
    for peer in peers:
        pl.semaphore_signal(barrier, inc=1, device_id=peer, device_id_type=MESH)
    pl.semaphore_wait(barrier, len(peers))


def fill_padded(xf, before, own, after):
    rows = jnp.zeros((4, 1, 16, C), F32)
    xf[:, 0:1] = rows
    xf[:, 9:10] = rows
    xf[0, 1:9] = before
    xf[1:3, 1:9] = own
    xf[3, 1:9] = after


def taps(xf, weight, d, lanes, flipped):
    sums = [jnp.zeros((8, 16, 128), F32) for _ in range(3)]
    for a in range(3):
        for b in range(3):
            rows = xf[d + a, b : b + 8, :, lanes]
            for e in range(3):
                t = 9 * a + 3 * b + e
                t = 26 - t if flipped else t
                sums[e] = sums[e] + weight[t : t + 1, lanes][None] * rows
    w = iota((8, 16, 128), 1)
    left = jnp.where(w == 0, 0.0, pltpu.roll(sums[0], 1, 1))
    right = jnp.where(w == 15, 0.0, pltpu.roll(sums[2], 15, 1))
    return sums[1] + left + right


def chunk(j):
    return pl.ds(pl.multiple_of(j * 128, 128), 128)


def normalise(rows):
    centred = rows - jnp.mean(rows, axis=-1, keepdims=True)
    inverse = lax.rsqrt(jnp.mean(centred * centred, axis=-1, keepdims=True) + 1e-05)
    return (centred * inverse, inverse)


def arrange(w, into, dp):
    lane, other = iota((128, 128), 0), iota((128, 128), 1)
    moves = {}
    for had in range(2):
        for gets in range(2):
            hit = (lane - 64 * had == other - 64 * gets) & (other // 64 == gets)
            moves[had, gets] = jnp.where(hit, 1.0, 0.0).astype(BF)
    for c in range(2):
        for k in range(9):
            part, group = k // 3, k % 3
            pieces = []
            for gets in range(2):
                block = 2 * group + gets
                old = part * 12 + block // 3 * 6 + c * 3 + block % 3
                start = old // 2 * 128
                pieces.append(nn(w[:, start : start + 128], moves[old % 2, gets]))
            start = group * MINE + part * 128
            into[c, dp, :, start : start + 128] = (pieces[0] + pieces[1]).astype(BF)


def source_of(n, r):
    b, d, h, j = n >> 8, (n >> 6) & 3, (n >> 3) & 7, n & 7
    return d * 128 + h * 16 + ((8 * b + j + r) & 15)


def head_sums(x, ones):
    high = x.astype(BF)
    low = (x - high.astype(F32)).astype(BF)
    return nn(high, ones) + nn(low, ones)


def attention(shift, scales, core, g, b, qkv_s, ba_s, att_s, bqkv_s, allow_s, scale_s):
    ones = jnp.where(iota((128, 128), 0) // 32 == iota((128, 128), 1) // 32, 1.0, 0.0).astype(BF)
    lane_head = iota((256, 128), 1) // 32
    rows = pl.ds(pl.multiple_of(b * 256, 256), 256)
    query = qkv_s[rows, 0:128].astype(F32)
    key = qkv_s[rows, 128:256].astype(F32)
    value = qkv_s[rows, 256:384]
    ba = ba_s[rows, g * 128 : g * 128 + 128]
    inv_q = lax.rsqrt(head_sums(query * query, ones) + 1.0)
    inv_k = lax.rsqrt(head_sums(key * key, ones) + 1.0)
    uq = (query * inv_q).astype(BF)
    uk = (key * inv_k).astype(BF)
    att = jnp.zeros((256, 128), F32)
    back_v = jnp.zeros((256, 128), F32)
    back_uq = jnp.zeros((256, 128), F32)
    back_uk = jnp.zeros((256, 128), F32)
    zero = jnp.zeros((256, 128), BF)
    for h in range(4):
        here = lane_head == h
        scale = scales[core, g * 4 + h]
        uq_h = jnp.where(here, uq, zero)
        uk_h = jnp.where(here, uk, zero)
        v_h = jnp.where(here, value, zero)
        ba_h = jnp.where(here, ba, zero)
        cosine = nt(uk_h, uq)
        expo = jnp.exp(scale * cosine) * allow_s[b]
        prob = expo * (1.0 / jnp.sum(expo, axis=0, keepdims=True))
        weights = prob.astype(BF)
        att = att + tn(weights, v_h)
        back_v = back_v + nn(weights, ba_h)
        back_prob = nt(v_h, ba)
        mean = jnp.sum(prob * back_prob, axis=0, keepdims=True)
        back_score = prob * (back_prob - mean)
        scale_s[b, g * 4 + h : g * 4 + h + 1] = jnp.sum(back_score * cosine, axis=0, keepdims=True)
        scaled = (back_score * scale).astype(BF)
        back_uq = back_uq + tn(scaled, uk_h)
        back_uk = back_uk + nn(scaled, uq_h)
    att_s[rows, g * 128 : g * 128 + 128] = att.astype(BF)
    inner_q = head_sums(query * back_uq, ones)
    inner_k = head_sums(key * back_uk, ones)
    back_q = back_uq * inv_q - query * inner_q * (inv_q * inv_q * inv_q)
    back_k = back_uk * inv_k - key * inner_k * (inv_k * inv_k * inv_k)
    bqkv_s[rows, 0:128] = back_q.astype(BF)
    bqkv_s[rows, 128:256] = back_k.astype(BF)
    bqkv_s[rows, 256:384] = back_v.astype(BF)


def block_kernel(shift, scales, tokens, cot, wq_in, wp_in, weight, gain,
                 out, grad, gq_out, gp_out, conv_out, gain_out, scale_out,
                 halo, nwin, cwin, wq, wp, mixed, sel, res, x_s, xt_s, ct_s, qkv_s, ba_s, att_s, bqkv_s, allow_s,
                 scale_s, gq_s, gp_s, g, own, given,
                 recv, bn_s, bm, bmh, ph, xf, tf, sh, ra0, ra1, sa0, sa1, rb0, rb1, sb, rc, full,
                 sm, s2, s3, sz, qy1, qx1, qx2, qy2, qz, s_sem, r_sem, l_sem):
    rep, dp, seq, core = place()
    z = lax.rem(seq // 2, ZC)
    x = seq // (2 * ZC)
    y = rep * 2 + dp

    def at_y(step):
        there = lax.rem(y + step, 4)
        return (there // 2, lax.rem(there, 2), seq)

    def at_x(step):
        there = lax.rem(x + step, XC)
        return (rep, dp, (there * ZC + z) * 2 + core)

    def at_z(step):
        there = lax.rem(z + step, ZC)
        return (rep, dp, (x * ZC + there) * 2 + core)

    up = (rep, dp, lax.rem(seq + 1, SEQ))
    down = (rep, dp, lax.rem(seq + SEQ - 1, SEQ))
    partner = (rep, dp, lax.rem(seq + SEQ - 1 + 2 * core, SEQ))
    other_core = (rep, dp, seq + 1 - 2 * core)
    other_rep = (1 - rep, dp, seq)
    peers = [at_y(k) for k in range(1, 4)] + [at_x(k) for k in range(1, XC)]
    peers += [at_z(k) for k in range(1, ZC)] + [up, down]
    greet(peers)
    used = [0]

    def go(src, dst, to):
        n = used[0]
        used[0] += 1
        return send(src, dst, s_sem.at[n], r_sem.at[n], to)

    def finish(copies):
        for c in copies:
            c.wait()

    low, high = pl.ds(0, 36), pl.ds(36, 36)
    first = jnp.where(seq == 0, 0.0, 1.0).astype(F32)
    last = jnp.where(seq == SEQ - 1, 0.0, 1.0).astype(F32)
    half = 1 - core
    halos = [go(tokens.at[0], halo.at[1], down), go(tokens.at[1], halo.at[0], up)]
    local = [
        pltpu.make_async_copy(cot, cwin.at[half], l_sem.at[0]),
        pltpu.make_async_copy(wp_in, wp.at[:, dp], l_sem.at[1]),
    ]
    for c in local:
        c.start()
    y_to = lax.rem(y + 3 + 2 * core, 4)
    y_peer = (y_to // 2, lax.rem(y_to, 2), seq)
    wp_came = go(wp_in.at[core], wp.at[core, dp], y_peer)
    cots = go(cot, cwin.at[half], partner)
    arrange(wq_in, wq, dp)
    wq_came = []
    for k in range(3):
        piece = wq.at[core, dp, :, k * MINE : k * MINE + MINE]
        wq_came.append(go(piece, piece, y_peer))
    finish(halos)
    fill_padded(tf, halo[0].astype(F32) * first, tokens[...].astype(F32), halo[1].astype(F32) * last)

    def mix_step(i, carry):
        d, j = i // 6, lax.rem(i, 6)
        lanes = chunk(j)
        mixed[d, :, :, lanes] = tf[d + 1, 1:9, :, lanes] + taps(tf, weight, d, lanes, False)
        return carry

    lax.fori_loop(0, 12, mix_step, 0)

    def unit_step(i, carry):
        d, h = i // 2, lax.rem(i, 2) * 4
        unit, _ = normalise(mixed[d, pl.ds(h, 4)].reshape(64, C))
        nwin[half, pl.ds(pl.multiple_of(i * 64, 64), 64)] = (unit * gain[...]).astype(BF)
        return carry

    lax.fori_loop(0, 4, unit_step, 0)
    norms = go(nwin.at[half], nwin.at[half], partner)

    s, r = shift[0], shift[1]
    sel[...] = jnp.where(iota((512, 512), 1) == source_of(iota((512, 512), 0), r), 1.0, 0.0).astype(BF)
    for k in range(2):
        target = source_of(iota((256, 512), 1), r)
        res[k] = jnp.where(iota((256, 512), 0) + 256 * k == target, 1.0, 0.0).astype(BF)

    def code(n, b):
        h, j = (n >> 3) & 7, n & 7
        return jnp.where(h < s, 2, 0) + jnp.where(8 * b + j + r >= 16, 1, 0)

    for b in range(2):
        same = code(iota((256, 256), 0), b) == code(iota((256, 256), 1), b)
        allow_s[b] = jnp.where(same, 1.0, 0.0).astype(F32)
    scale_s[...] = jnp.zeros((2, 16, 256), F32)
    for c in local:
        c.wait()
    cots.wait()
    ct_s[...] = nn(sel[...], cwin[...].reshape(512, C)).astype(BF)
    wp_came.wait()
    ba_s[...] = nt(ct_s[...], wp[core].reshape(MINE, C)).astype(BF)
    norms.wait()
    ordered = nn(sel[...], nwin[...].reshape(512, C))
    x_s[...] = ordered.astype(BF)
    xt_s[...] = ordered.T.astype(BF)

    exchanges, stage, swaps = [], [], []
    for k in range(3):
        wq_came[k].wait()
        if k == 2:
            piece = wq.at[core, 1 - dp]
            swaps.append(go(piece, piece, other_core))
            piece = wp.at[core, 1 - dp]
            swaps.append(go(piece, piece, other_core))
        columns = wq[core, :, :, k * MINE : k * MINE + MINE].reshape(C, MINE)
        qkv_s[...] = nn(x_s[...], columns).astype(BF)

        def window(b, carry):
            attention(shift, scales, core, k, b, qkv_s, ba_s, att_s, bqkv_s, allow_s, scale_s)
            return carry

        lax.fori_loop(0, 2, window, 0)
        lanes = slice(k * 128, k * 128 + 128)
        given[k, :, 0:128] = nn(res[core], att_s[:, lanes]).astype(BF)
        given[k, :, 128:] = nn(res[core], bqkv_s[...]).astype(BF)
        exchanges.append(go(given.at[k], recv.at[k], partner))
        gq_s[...] = nn(xt_s[...], bqkv_s[...])

        def store(i, carry):
            d, p, to = i // 8, lax.rem(i // 4, 2), lax.rem(i, 4)
            for c in range(3):
                block = gq_s[pl.ds(pl.multiple_of(i * 48, 48), 48), c * 128 : (c + 1) * 128]
                start = TILES[k] + c * 6
                g[d, p, to, start : start + 6] = block.reshape(6, 8, 128).astype(BF)
            return carry

        lax.fori_loop(0, 16, store, 0)
        tiles = pl.ds(TILES[k], 18)
        away = pl.ds(TILES[k] % 36, 18)
        for step in range(1, 4):
            if k == 1:
                stage.append(go(g.at[:, :, lax.rem(x + step, XC), tiles], ra1.at[step - 1, :, :, away], at_x(step)))
            else:
                to = at_y(step)
                stage.append(go(g.at[to[1], to[0], :, tiles], ra0.at[step - 1, :, away], to))
        own[k, :, 0:128] = nn(res[half], att_s[:, lanes]).astype(BF)
        own[k, :, 128:] = nn(res[half], bqkv_s[...]).astype(BF)
    gp_s[...] = tn(att_s[...], ct_s[...])

    def store_proj(i, carry):
        d, p, to = i // 8, lax.rem(i // 4, 2), lax.rem(i, 4)
        for c in range(6):
            block = gp_s[pl.ds(pl.multiple_of(i * 24, 24), 24), c * 128 : (c + 1) * 128]
            g[d, p, to, 54 + c * 3 : 57 + c * 3] = block.reshape(3, 8, 128).astype(BF)
        return carry

    lax.fori_loop(0, 16, store_proj, 0)
    tiles, away = pl.ds(54, 18), pl.ds(18, 18)
    for step in range(1, 4):
        stage.append(go(g.at[:, :, lax.rem(x + step, XC), tiles], ra1.at[step - 1, :, :, away], at_x(step)))

    def wq_of(c, k):
        return wq[c, :, :, k * MINE : k * MINE + MINE].reshape(C, MINE)

    finish(swaps)
    back = nt(own[0, :, 128:], wq_of(core, 0))
    for k in range(1, 3):
        back = back + nt(own[k, :, 128:], wq_of(core, k))
    for k in range(3):
        exchanges[k].wait()
        back = back + nt(recv[k, :, 128:], wq_of(1 - core, k))
    bn_s[...] = back.astype(BF)
    def norm_step(i, total):
        d, h = i // 2, lax.rem(i, 2) * 4
        rows = pl.ds(pl.multiple_of(i * 64, 64), 64)
        unit, inverse = normalise(mixed[d, pl.ds(h, 4)].reshape(64, C))
        back_float = bn_s[rows].astype(F32)
        total = total + jnp.sum((back_float * unit).reshape(8, 8, C), axis=0)
        grad_unit = back_float * gain[...]
        mean = jnp.mean(grad_unit, axis=-1, keepdims=True)
        slope = jnp.mean(grad_unit * unit, axis=-1, keepdims=True)
        result = cot[rows].astype(F32) + inverse * (grad_unit - mean - unit * slope)
        bm[d, pl.ds(h, 4)] = result.reshape(4, 16, C)
        bmh[d, pl.ds(h, 4)] = result.astype(BF).reshape(4, 16, C)
        return total

    gain_part = jnp.sum(lax.fori_loop(0, 4, norm_step, jnp.zeros((8, C), F32)), axis=0, keepdims=True)
    planes = [go(bmh.at[0], ph.at[1], down), go(bmh.at[1], ph.at[0], up)]
    finish(stage)

    def add_a(i, carry):
        total = g[dp, rep, i, low].astype(F32)
        for k in range(3):
            total = total + ra0[k, i].astype(F32)
        sa0[i] = total.astype(BF)
        d, r = lax.rem(i, 2), i // 2
        total = g[d, r, x, high].astype(F32)
        for k in range(XC - 1):
            total = total + ra1[k, d, r].astype(F32)
        sa1[d, r] = total.astype(BF)
        return carry

    lax.fori_loop(0, 4, add_a, 0)
    stage = []
    for k in range(1, XC):
        stage.append(go(sa0.at[lax.rem(x + k, XC)], rb0.at[k - 1], at_x(k)))
    for k in range(1, 4):
        to = at_y(k)
        stage.append(go(sa1.at[to[1], to[0]], rb1.at[k - 1], to))

    wp_mine, wp_other = wp[core].reshape(MINE, C), wp[1 - core].reshape(MINE, C)
    proj = jnp.zeros((256, C), F32)
    for k in range(3):
        rows = slice(k * 128, k * 128 + 128)
        proj = proj + nn(own[k, :, 0:128], wp_mine[rows]) + nn(recv[k, :, 0:128], wp_other[rows])
    out[...] = (mixed[...].reshape(256, C) + proj).astype(BF).reshape(2, 8, 16, C)

    finish(planes)
    fill_padded(xf, ph[0].astype(F32) * first, bm[...], ph[1].astype(F32) * last)

    def filter_step(i, carry):
        d, j = i // 6, lax.rem(i, 6)
        lanes = chunk(j)
        here = xf[d + 1, 1:9, :, lanes]
        grad[d, :, :, lanes] = (here + taps(xf, weight, d, lanes, True)).astype(BF)
        w = iota((8, 16, 128), 1)
        sh[0, d, :, :, lanes] = jnp.where(w == 15, 0.0, pltpu.roll(here, 15, 1))
        sh[1, d, :, :, lanes] = here
        sh[2, d, :, :, lanes] = jnp.where(w == 0, 0.0, pltpu.roll(here, 1, 1))
        return carry

    lax.fori_loop(0, 12, filter_step, 0)

    finish(stage)
    total = sa0[x].astype(F32)
    for k in range(XC - 1):
        total = total + rb0[k].astype(F32)
    sb[low] = total.astype(BF)
    total = sa1[dp, rep].astype(F32)
    for k in range(3):
        total = total + rb1[k].astype(F32)
    sb[high] = total.astype(BF)
    stage = []
    for k in range(1, ZC):
        stage.append(go(sb.at[pl.ds(lax.rem(z + k, ZC) * 9, 9)], rc.at[k - 1], at_z(k)))

    sm[...] = jnp.zeros((8, 32, 128), F32)

    def conv_step(j, carry):
        lanes = chunk(j)
        for a in range(3):
            for b in range(3):
                rows = tf[a : a + 2, b : b + 8, :, lanes]
                for e in range(3):
                    total = jnp.sum((sh[e, :, :, :, lanes] * rows).reshape(16, 16, 128), axis=0)
                    t = 9 * a + 3 * b + e
                    sm[j, t : t + 1] = jnp.sum(total, axis=0, keepdims=True)
        return carry

    lax.fori_loop(0, 6, conv_step, 0)
    for j in range(6):
        sm[j, 27:28] = gain_part[:, j * 128 : j * 128 + 128]
    scale = jnp.sum(scale_s[0] + scale_s[1], axis=-1, keepdims=True)
    sm[6, pl.ds(pl.multiple_of(core * 16, 16), 16)] = jnp.broadcast_to(scale, (16, 128))
    few, rest = pl.ds(0, 4), pl.ds(4, 4)
    little = []
    for k in range(1, 4):
        little.append(go(sm.at[few], qy1.at[k - 1], at_y(k)))
        little.append(go(sm.at[rest], qx1.at[k - 1], at_x(k)))

    finish(stage)
    mine = pl.ds(z * 9, 9)
    total = sb[mine].astype(F32)
    for k in range(ZC - 1):
        total = total + rc[k].astype(F32)
    full[core, rep, x, mine] = total.astype(BF)
    stage = []
    piece = full.at[core, rep, x, mine]
    for k in range(1, ZC):
        stage.append(go(piece, piece, at_z(k)))

    finish(little)
    s2[few] = sm[few] + qy1[0] + qy1[1] + qy1[2]
    s2[rest] = sm[rest] + qx1[0] + qx1[1] + qx1[2]
    little = []
    for k in range(1, 4):
        little.append(go(s2.at[few], qx2.at[k - 1], at_x(k)))
        little.append(go(s2.at[rest], qy2.at[k - 1], at_y(k)))

    finish(stage)
    piece = full.at[core, rep, x, low]
    stage = [go(piece, piece, other_rep)]
    piece = full.at[core, rep, x, high]
    stage += [go(piece, piece, at_x(k)) for k in range(1, XC)]
    piece = full.at[core, rep, x]
    handed = [go(piece, piece, other_core)]

    finish(little)
    s3[few] = s2[few] + qx2[0] + qx2[1] + qx2[2]
    s3[rest] = s2[rest] + qy2[0] + qy2[1] + qy2[2]
    little = [go(s3.at[lax.rem(z + k, ZC)], qz.at[k - 1], at_z(k)) for k in range(1, ZC)]

    finish(stage)
    piece = full.at[core, :, x, low]
    along = [go(piece, piece, at_x(k)) for k in range(1, XC)]
    piece = full.at[core, rep, :, high]
    across = go(piece, piece, other_rep)
    piece = full.at[core, 1 - rep, x, low]
    handed.append(go(piece, piece, other_core))
    for k in range(1, XC):
        piece = full.at[core, rep, lax.rem(x + k, XC), high]
        handed.append(go(piece, piece, other_core))

    finish(little)
    total = s3[z]
    for k in range(ZC - 1):
        total = total + qz[k]
    sz[core, z] = total
    little = [go(sz.at[core, z], sz.at[core, z], at_z(k)) for k in range(1, ZC)]

    for k in range(1, XC):
        along[k - 1].wait()
        piece = full.at[core, :, lax.rem(x + XC - k, XC), low]
        handed.append(go(piece, piece, other_core))
    across.wait()
    piece = full.at[core, 1 - rep, :, high]
    handed.append(go(piece, piece, other_core))
    finish(little)
    little = go(sz.at[core], sz.at[core], other_core)
    finish(handed)

    lane = iota((48, 128), 1)

    def assemble(i, carry):
        r, k = i // 4, lax.rem(i, 4)
        rows = pl.ds(pl.multiple_of(i * 48, 48), 48)
        for part in range(3):
            for m in range(6):
                halves = []
                for gets in range(2):
                    block = 2 * m + gets
                    c = block % 6 // 3
                    old = block // 6 * 3 + block % 3
                    start = TILES[old // 2] + part * 6
                    tile = full[c, r, k, start : start + 6].astype(F32).reshape(48, 128)
                    halves.append(tile if old % 2 == gets else pltpu.roll(tile, 64, 1))
                start = part * C + m * 128
                gq_out[rows, start : start + 128] = jnp.where(lane < 64, halves[0], halves[1])
        for c in range(2):
            for m in range(6):
                tile = full[c, r, k, 54 + m * 3 : 57 + m * 3].astype(F32).reshape(24, 128)
                start = pl.multiple_of(c * 192 + i * 24, 8)
                gp_out[pl.ds(start, 24), m * 128 : m * 128 + 128] = tile
        return carry

    lax.fori_loop(0, 8, assemble, 0)
    little.wait()
    for j in range(6):
        total = sz[0, j] + sz[1, j]
        conv_out[:, j * 128 : j * 128 + 128] = total[0:27]
        gain_out[:, j * 128 : j * 128 + 128] = total[27:28]
    scale_out[...] = sz[0, 6] + sz[1, 6]


def whole_block(shift, scales, tokens, cot, wq, wp, weight, gain):
    shape = jax.ShapeDtypeStruct
    field = (2, 8, 16, C)
    tile = (8, 128)
    some = (32, 128)
    V = pltpu.VMEM
    copies = 96
    return pl.pallas_call(
        block_kernel,
        out_shape=(
            shape(field, BF), shape(field, BF), shape((MINE, 3 * C), F32), shape((MINE, C), F32),
            shape((27, C), F32), shape((1, C), F32), shape(some, F32),
        ),
        in_specs=[SMEM, SMEM] + [VMEM] * 6,
        out_specs=(VMEM,) * 7,
        scratch_shapes=[
            V(field, BF), V((2, 256, C), BF), V((2, 256, C), BF),
            V((2, 2, MINE, 3 * MINE), BF), V((2, 2, MINE // 2, C), BF), V(field, F32),
            V((512, 512), BF), V((2, 256, 512), BF),
            V((512, C), BF), V((C, 512), BF), V((512, C), BF), V((512, MINE), BF), V((512, MINE), BF),
            V((512, MINE), BF), V((512, MINE), BF), V((2, 256, 256), F32),
            V((2, 16, 256), F32), V((C, MINE), F32), V((MINE, C), F32), V((2, 2, XC, 72) + tile, BF),
            V((3, 256, 512), BF), V((3, 256, 512), BF),
            V((3, 256, 512), BF), V((256, C), BF),
            V(field, F32), V(field, BF), V(field, BF),
            V((4, 10, 16, C), F32), V((4, 10, 16, C), F32), V((3,) + field, F32),
            V((3, XC, 36) + tile, BF), V((XC - 1, 2, 2, 36) + tile, BF),
            V((XC, 36) + tile, BF), V((2, 2, 36) + tile, BF),
            V((XC - 1, 36) + tile, BF), V((3, 36) + tile, BF),
            V((72,) + tile, BF), V((ZC - 1, 9) + tile, BF),
            V((2, 2, XC, 72) + tile, BF),
            V((8,) + some, F32), V((8,) + some, F32), V((8,) + some, F32), V((2, 8) + some, F32),
            V((3, 4) + some, F32), V((3, 4) + some, F32), V((3, 4) + some, F32), V((3, 4) + some, F32),
            V((ZC - 1,) + some, F32),
            DMA((copies,)), DMA((copies,)), DMA((2,)),
        ],
        compiler_params=pltpu.CompilerParams(
            collective_id=0, has_side_effects=True, vmem_limit_bytes=60 << 20
        ),
        name="whole_block",
    )(shift, scales, tokens, cot, wq, wp, weight, gain)


def per_device(tokens, cotangent, w_qkv, w_proj, conv_weight, norm_gain, head_scale, shift_offsets):
    slab = tokens[0]
    cot = cotangent[0].reshape(256, C)
    gain = norm_gain.reshape(1, C)
    scales = head_scale.reshape(2, 2, 6).transpose(1, 0, 2).reshape(2, 12)
    output, grad_tokens, grad_qkv, grad_proj, conv, gain_sum, scale = whole_block(
        shift_offsets, scales, slab, cot, w_qkv, w_proj.reshape(2, 192, C), conv_weight, gain
    )
    factor = 1.0 / math.sqrt(lax.axis_size("rep") * lax.axis_size("dp") * SEQ * 256)
    scale = scale[:, 0].reshape(2, 16)[:, :12].reshape(2, 2, 6).transpose(1, 0, 2).reshape(24)
    return (
        output[None],
        grad_tokens[None],
        grad_qkv * factor,
        grad_proj * factor,
        conv * factor,
        gain_sum.reshape(C) * factor,
        scale * factor,
    )


def solution(mesh):
    in_specs = (
        P(("rep", "dp"), "seq", None, None, None),
        P(("rep", "dp"), "seq", None, None, None),
        P("dp", None),
        P("dp", None),
        P(),
        P(),
        P(),
        P(),
    )
    out_specs = (
        P(("rep", "dp"), "seq", None, None, None),
        P(("rep", "dp"), "seq", None, None, None),
        P("dp", None),
        P("dp", None),
        P(),
        P(),
        P(),
    )
    return jax.shard_map(
        per_device, mesh=mesh, in_specs=in_specs, out_specs=out_specs, check_vma=False
    )
```

```python
import functools
import math

import jax
import jax.numpy as jnp
from jax import lax
from jax.experimental import pallas as pl
from jax.experimental.pallas import tpu as pltpu
from jax.sharding import PartitionSpec as P

MESH = pl.DeviceIdType.MESH
BF = jnp.bfloat16
F32 = jnp.float32
XC = 4
ZC = 8
SEQ = 64
C = 768
MINE = 384
TILES = (0, 36, 18)
VMEM = pl.BlockSpec(memory_space=pltpu.VMEM)
SMEM = pl.BlockSpec(memory_space=pltpu.SMEM)
DMA = pltpu.SemaphoreType.DMA


def nn(a, b):
    return lax.dot_general(a, b, (((1,), (0,)), ((), ())), preferred_element_type=F32)


def nt(a, b):
    return lax.dot_general(a, b, (((1,), (1,)), ((), ())), preferred_element_type=F32)


def tn(a, b):
    return lax.dot_general(a, b, (((0,), (0,)), ((), ())), preferred_element_type=F32)


def iota(shape, dim):
    return lax.broadcasted_iota(jnp.int32, shape, dim)


def place():
    rep, dp, seq = lax.axis_index("rep"), lax.axis_index("dp"), lax.axis_index("seq")
    return (rep, dp, seq, lax.rem(seq, 2))


def send(src, dst, s, r, to):
    c = pltpu.make_async_remote_copy(
        src_ref=src, dst_ref=dst, send_sem=s, recv_sem=r, device_id=to, device_id_type=MESH
    )
    c.start()
    return c


def greet(peers):
    barrier = pltpu.get_barrier_semaphore()
    for peer in peers:
        pl.semaphore_signal(barrier, inc=1, device_id=peer, device_id_type=MESH)
    pl.semaphore_wait(barrier, len(peers))


def fill_padded(xf, before, own, after):
    rows = jnp.zeros((4, 1, 16, C), F32)
    xf[:, 0:1] = rows
    xf[:, 9:10] = rows
    xf[0, 1:9] = before
    xf[1:3, 1:9] = own
    xf[3, 1:9] = after


def taps(xf, weight, d, lanes, flipped):
    sums = [jnp.zeros((8, 16, 128), F32) for _ in range(3)]
    for a in range(3):
        for b in range(3):
            rows = xf[d + a, b : b + 8, :, lanes]
            for e in range(3):
                t = 9 * a + 3 * b + e
                t = 26 - t if flipped else t
                sums[e] = sums[e] + weight[t : t + 1, lanes][None] * rows
    w = iota((8, 16, 128), 1)
    left = jnp.where(w == 0, 0.0, pltpu.roll(sums[0], 1, 1))
    right = jnp.where(w == 15, 0.0, pltpu.roll(sums[2], 15, 1))
    return sums[1] + left + right


def chunk(j):
    return pl.ds(pl.multiple_of(j * 128, 128), 128)


def normalise(rows):
    centred = rows - jnp.mean(rows, axis=-1, keepdims=True)
    inverse = lax.rsqrt(jnp.mean(centred * centred, axis=-1, keepdims=True) + 1e-05)
    return (centred * inverse, inverse)


def arrange(w, into, dp):
    lane, other = iota((128, 128), 0), iota((128, 128), 1)
    moves = {}
    for had in range(2):
        for gets in range(2):
            hit = (lane - 64 * had == other - 64 * gets) & (other // 64 == gets)
            moves[had, gets] = jnp.where(hit, 1.0, 0.0).astype(BF)
    for c in range(2):
        for k in range(9):
            part, group = k // 3, k % 3
            pieces = []
            for gets in range(2):
                block = 2 * group + gets
                old = part * 12 + block // 3 * 6 + c * 3 + block % 3
                start = old // 2 * 128
                pieces.append(nn(w[:, start : start + 128], moves[old % 2, gets]))
            start = group * MINE + part * 128
            into[c, dp, :, start : start + 128] = (pieces[0] + pieces[1]).astype(BF)


def source_of(n, r):
    b, d, h, j = n >> 8, (n >> 6) & 3, (n >> 3) & 7, n & 7
    return d * 128 + h * 16 + ((8 * b + j + r) & 15)


def head_sums(x, ones):
    high = x.astype(BF)
    low = (x - high.astype(F32)).astype(BF)
    return nn(high, ones) + nn(low, ones)


def attention(shift, scales, core, g, b, qkv_s, ba_s, att_s, bqkv_s, allow_s, scale_s):
    ones = jnp.where(iota((128, 128), 0) // 32 == iota((128, 128), 1) // 32, 1.0, 0.0).astype(BF)
    lane_head = iota((256, 128), 1) // 32
    rows = pl.ds(pl.multiple_of(b * 256, 256), 256)
    query = qkv_s[rows, 0:128].astype(F32)
    key = qkv_s[rows, 128:256].astype(F32)
    value = qkv_s[rows, 256:384]
    ba = ba_s[rows, g * 128 : g * 128 + 128]
    inv_q = lax.rsqrt(head_sums(query * query, ones) + 1.0)
    inv_k = lax.rsqrt(head_sums(key * key, ones) + 1.0)
    uq = (query * inv_q).astype(BF)
    uk = (key * inv_k).astype(BF)
    att = jnp.zeros((256, 128), F32)
    back_v = jnp.zeros((256, 128), F32)
    back_uq = jnp.zeros((256, 128), F32)
    back_uk = jnp.zeros((256, 128), F32)
    zero = jnp.zeros((256, 128), BF)
    for h in range(4):
        here = lane_head == h
        scale = scales[(g * 4 + h) // 6 * 12 + core * 6 + (g * 4 + h) % 6]
        uq_h = jnp.where(here, uq, zero)
        uk_h = jnp.where(here, uk, zero)
        v_h = jnp.where(here, value, zero)
        ba_h = jnp.where(here, ba, zero)
        cosine = nt(uk_h, uq)
        expo = jnp.exp(scale * cosine) * allow_s[b]
        prob = expo * (1.0 / jnp.sum(expo, axis=0, keepdims=True))
        weights = prob.astype(BF)
        att = att + tn(weights, v_h)
        back_v = back_v + nn(weights, ba_h)
        back_prob = nt(v_h, ba)
        mean = jnp.sum(prob * back_prob, axis=0, keepdims=True)
        back_score = prob * (back_prob - mean)
        scale_s[b, g * 4 + h : g * 4 + h + 1] = jnp.sum(back_score * cosine, axis=0, keepdims=True)
        scaled = (back_score * scale).astype(BF)
        back_uq = back_uq + tn(scaled, uk_h)
        back_uk = back_uk + nn(scaled, uq_h)
    att_s[rows, g * 128 : g * 128 + 128] = att.astype(BF)
    inner_q = head_sums(query * back_uq, ones)
    inner_k = head_sums(key * back_uk, ones)
    back_q = back_uq * inv_q - query * inner_q * (inv_q * inv_q * inv_q)
    back_k = back_uk * inv_k - key * inner_k * (inv_k * inv_k * inv_k)
    bqkv_s[rows, 0:128] = back_q.astype(BF)
    bqkv_s[rows, 128:256] = back_k.astype(BF)
    bqkv_s[rows, 256:384] = back_v.astype(BF)


def block_kernel(shift, scales, tokens, cot, wq_in, wp_in, weight, gain,
                 out, grad, full, small_out,
                 halo, nwin, cwin, wq, wp, mixed, sel, res, x_s, xt_s, ct_s, qkv_s, ba_s, att_s, bqkv_s, allow_s,
                 scale_s, gq_s, gp_s, g, own, given,
                 recv, bn_s, bm, bmh, ph, xf, tf, sh, ra0, ra1, sa0, sa1, rb0, rb1, sb, rc,
                 sm, s2, s3, sz, qy1, qx1, qx2, qy2, qz, s_sem, r_sem, l_sem):
    rep, dp, seq, core = place()
    z = lax.rem(seq // 2, ZC)
    x = seq // (2 * ZC)
    y = rep * 2 + dp

    def at_y(step):
        there = lax.rem(y + step, 4)
        return (there // 2, lax.rem(there, 2), seq)

    def at_x(step):
        there = lax.rem(x + step, XC)
        return (rep, dp, (there * ZC + z) * 2 + core)

    def at_z(step):
        there = lax.rem(z + step, ZC)
        return (rep, dp, (x * ZC + there) * 2 + core)

    up = (rep, dp, lax.rem(seq + 1, SEQ))
    down = (rep, dp, lax.rem(seq + SEQ - 1, SEQ))
    partner = (rep, dp, lax.rem(seq + SEQ - 1 + 2 * core, SEQ))
    other_core = (rep, dp, seq + 1 - 2 * core)
    other_rep = (1 - rep, dp, seq)
    peers = [at_y(k) for k in range(1, 4)] + [at_x(k) for k in range(1, XC)]
    peers += [at_z(k) for k in range(1, ZC)] + [up, down]
    greet(peers)
    used = [0]

    def go(src, dst, to):
        n = used[0]
        used[0] += 1
        return send(src, dst, s_sem.at[n], r_sem.at[n], to)

    def finish(copies):
        for c in copies:
            c.wait()

    low, high = pl.ds(0, 36), pl.ds(36, 36)
    first = jnp.where(seq == 0, 0.0, 1.0).astype(F32)
    last = jnp.where(seq == SEQ - 1, 0.0, 1.0).astype(F32)
    half = 1 - core
    halos = [go(tokens.at[0], halo.at[1], down), go(tokens.at[1], halo.at[0], up)]
    local = [
        pltpu.make_async_copy(cot, cwin.at[half], l_sem.at[0]),
        pltpu.make_async_copy(wp_in.at[pl.ds(0, 192)], wp.at[0, dp], l_sem.at[1]),
        pltpu.make_async_copy(wp_in.at[pl.ds(192, 192)], wp.at[1, dp], l_sem.at[2]),
    ]
    for c in local:
        c.start()
    y_to = lax.rem(y + 3 + 2 * core, 4)
    y_peer = (y_to // 2, lax.rem(y_to, 2), seq)
    wp_came = go(wp_in.at[pl.ds(pl.multiple_of(core * 192, 64), 192)], wp.at[core, dp], y_peer)
    cots = go(cot, cwin.at[half], partner)
    arrange(wq_in, wq, dp)
    wq_came = []
    for k in range(3):
        piece = wq.at[core, dp, :, k * MINE : k * MINE + MINE]
        wq_came.append(go(piece, piece, y_peer))
    finish(halos)
    fill_padded(tf, halo[0].astype(F32) * first, tokens[...].astype(F32), halo[1].astype(F32) * last)

    def mix_step(i, carry):
        d, j = i // 6, lax.rem(i, 6)
        lanes = chunk(j)
        mixed[d, :, :, lanes] = tf[d + 1, 1:9, :, lanes] + taps(tf, weight, d, lanes, False)
        return carry

    lax.fori_loop(0, 12, mix_step, 0)

    def unit_step(i, carry):
        d, h = i // 2, lax.rem(i, 2) * 4
        unit, _ = normalise(mixed[d, pl.ds(h, 4)].reshape(64, C))
        nwin[half, pl.ds(pl.multiple_of(i * 64, 64), 64)] = (unit * gain[...].reshape(1, C)).astype(BF)
        return carry

    lax.fori_loop(0, 4, unit_step, 0)
    norms = go(nwin.at[half], nwin.at[half], partner)

    s, r = shift[0], shift[1]
    sel[...] = jnp.where(iota((512, 512), 1) == source_of(iota((512, 512), 0), r), 1.0, 0.0).astype(BF)
    for k in range(2):
        target = source_of(iota((256, 512), 1), r)
        res[k] = jnp.where(iota((256, 512), 0) + 256 * k == target, 1.0, 0.0).astype(BF)

    def code(n, b):
        h, j = (n >> 3) & 7, n & 7
        return jnp.where(h < s, 2, 0) + jnp.where(8 * b + j + r >= 16, 1, 0)

    for b in range(2):
        same = code(iota((256, 256), 0), b) == code(iota((256, 256), 1), b)
        allow_s[b] = jnp.where(same, 1.0, 0.0).astype(F32)
    scale_s[...] = jnp.zeros((2, 16, 256), F32)
    for c in local:
        c.wait()
    cots.wait()
    ct_s[...] = nn(sel[...], cwin[...].reshape(512, C)).astype(BF)
    wp_came.wait()
    ba_s[...] = nt(ct_s[...], wp[core].reshape(MINE, C)).astype(BF)
    norms.wait()
    ordered = nn(sel[...], nwin[...].reshape(512, C))
    x_s[...] = ordered.astype(BF)
    xt_s[...] = ordered.T.astype(BF)

    exchanges, stage, swaps = [], [], []
    for k in range(3):
        wq_came[k].wait()
        if k == 2:
            piece = wq.at[core, 1 - dp]
            swaps.append(go(piece, piece, other_core))
            piece = wp.at[core, 1 - dp]
            swaps.append(go(piece, piece, other_core))
        columns = wq[core, :, :, k * MINE : k * MINE + MINE].reshape(C, MINE)
        qkv_s[...] = nn(x_s[...], columns).astype(BF)

        def window(b, carry):
            attention(shift, scales, core, k, b, qkv_s, ba_s, att_s, bqkv_s, allow_s, scale_s)
            return carry

        lax.fori_loop(0, 2, window, 0)
        lanes = slice(k * 128, k * 128 + 128)
        given[k, :, 0:128] = nn(res[core], att_s[:, lanes]).astype(BF)
        given[k, :, 128:] = nn(res[core], bqkv_s[...]).astype(BF)
        exchanges.append(go(given.at[k], recv.at[k], partner))
        gq_s[...] = nn(xt_s[...], bqkv_s[...])

        def store(i, carry):
            d, p, to = i // 8, lax.rem(i // 4, 2), lax.rem(i, 4)
            for c in range(3):
                block = gq_s[pl.ds(pl.multiple_of(i * 48, 48), 48), c * 128 : (c + 1) * 128]
                start = TILES[k] + c * 6
                g[d, p, to, start : start + 6] = block.reshape(6, 8, 128).astype(BF)
            return carry

        lax.fori_loop(0, 16, store, 0)
        tiles = pl.ds(TILES[k], 18)
        away = pl.ds(TILES[k] % 36, 18)
        for step in range(1, 4):
            if k == 1:
                stage.append(go(g.at[:, :, lax.rem(x + step, XC), tiles], ra1.at[step - 1, :, :, away], at_x(step)))
            else:
                to = at_y(step)
                stage.append(go(g.at[to[1], to[0], :, tiles], ra0.at[step - 1, :, away], to))
        own[k, :, 0:128] = nn(res[half], att_s[:, lanes]).astype(BF)
        own[k, :, 128:] = nn(res[half], bqkv_s[...]).astype(BF)
    gp_s[...] = tn(att_s[...], ct_s[...])

    def store_proj(i, carry):
        d, p, to = i // 8, lax.rem(i // 4, 2), lax.rem(i, 4)
        for c in range(6):
            block = gp_s[pl.ds(pl.multiple_of(i * 24, 24), 24), c * 128 : (c + 1) * 128]
            g[d, p, to, 54 + c * 3 : 57 + c * 3] = block.reshape(3, 8, 128).astype(BF)
        return carry

    lax.fori_loop(0, 16, store_proj, 0)
    tiles, away = pl.ds(54, 18), pl.ds(18, 18)
    for step in range(1, 4):
        stage.append(go(g.at[:, :, lax.rem(x + step, XC), tiles], ra1.at[step - 1, :, :, away], at_x(step)))

    def wq_of(c, k):
        return wq[c, :, :, k * MINE : k * MINE + MINE].reshape(C, MINE)

    finish(swaps)
    back = nt(own[0, :, 128:], wq_of(core, 0))
    for k in range(1, 3):
        back = back + nt(own[k, :, 128:], wq_of(core, k))
    for k in range(3):
        exchanges[k].wait()
        back = back + nt(recv[k, :, 128:], wq_of(1 - core, k))
    bn_s[...] = back.astype(BF)
    def norm_step(i, total):
        d, h = i // 2, lax.rem(i, 2) * 4
        rows = pl.ds(pl.multiple_of(i * 64, 64), 64)
        unit, inverse = normalise(mixed[d, pl.ds(h, 4)].reshape(64, C))
        back_float = bn_s[rows].astype(F32)
        total = total + jnp.sum((back_float * unit).reshape(8, 8, C), axis=0)
        grad_unit = back_float * gain[...].reshape(1, C)
        mean = jnp.mean(grad_unit, axis=-1, keepdims=True)
        slope = jnp.mean(grad_unit * unit, axis=-1, keepdims=True)
        result = cot[rows].astype(F32) + inverse * (grad_unit - mean - unit * slope)
        bm[d, pl.ds(h, 4)] = result.reshape(4, 16, C)
        bmh[d, pl.ds(h, 4)] = result.astype(BF).reshape(4, 16, C)
        return total

    gain_part = jnp.sum(lax.fori_loop(0, 4, norm_step, jnp.zeros((8, C), F32)), axis=0, keepdims=True)
    planes = [go(bmh.at[0], ph.at[1], down), go(bmh.at[1], ph.at[0], up)]
    finish(stage)

    def add_a(i, carry):
        total = g[dp, rep, i, low].astype(F32)
        for k in range(3):
            total = total + ra0[k, i].astype(F32)
        sa0[i] = total.astype(BF)
        d, r = lax.rem(i, 2), i // 2
        total = g[d, r, x, high].astype(F32)
        for k in range(XC - 1):
            total = total + ra1[k, d, r].astype(F32)
        sa1[d, r] = total.astype(BF)
        return carry

    lax.fori_loop(0, 4, add_a, 0)
    stage = []
    for k in range(1, XC):
        stage.append(go(sa0.at[lax.rem(x + k, XC)], rb0.at[k - 1], at_x(k)))
    for k in range(1, 4):
        to = at_y(k)
        stage.append(go(sa1.at[to[1], to[0]], rb1.at[k - 1], to))

    wp_mine, wp_other = wp[core].reshape(MINE, C), wp[1 - core].reshape(MINE, C)
    proj = jnp.zeros((256, C), F32)
    for k in range(3):
        rows = slice(k * 128, k * 128 + 128)
        proj = proj + nn(own[k, :, 0:128], wp_mine[rows]) + nn(recv[k, :, 0:128], wp_other[rows])
    out[...] = (mixed[...].reshape(256, C) + proj).astype(BF).reshape(2, 8, 16, C)

    finish(planes)
    fill_padded(xf, ph[0].astype(F32) * first, bm[...], ph[1].astype(F32) * last)

    def filter_step(i, carry):
        d, j = i // 6, lax.rem(i, 6)
        lanes = chunk(j)
        here = xf[d + 1, 1:9, :, lanes]
        grad[d, :, :, lanes] = (here + taps(xf, weight, d, lanes, True)).astype(BF)
        w = iota((8, 16, 128), 1)
        sh[0, d, :, :, lanes] = jnp.where(w == 15, 0.0, pltpu.roll(here, 15, 1))
        sh[1, d, :, :, lanes] = here
        sh[2, d, :, :, lanes] = jnp.where(w == 0, 0.0, pltpu.roll(here, 1, 1))
        return carry

    lax.fori_loop(0, 12, filter_step, 0)

    finish(stage)
    total = sa0[x].astype(F32)
    for k in range(XC - 1):
        total = total + rb0[k].astype(F32)
    sb[low] = total.astype(BF)
    total = sa1[dp, rep].astype(F32)
    for k in range(3):
        total = total + rb1[k].astype(F32)
    sb[high] = total.astype(BF)
    stage = []
    for k in range(1, ZC):
        stage.append(go(sb.at[pl.ds(lax.rem(z + k, ZC) * 9, 9)], rc.at[k - 1], at_z(k)))

    sm[...] = jnp.zeros((8, 32, 128), F32)

    def conv_step(j, carry):
        lanes = chunk(j)
        for a in range(3):
            for b in range(3):
                rows = tf[a : a + 2, b : b + 8, :, lanes]
                for e in range(3):
                    total = jnp.sum((sh[e, :, :, :, lanes] * rows).reshape(16, 16, 128), axis=0)
                    t = 9 * a + 3 * b + e
                    sm[j, t : t + 1] = jnp.sum(total, axis=0, keepdims=True)
        return carry

    lax.fori_loop(0, 6, conv_step, 0)
    for j in range(6):
        sm[j, 27:28] = gain_part[:, j * 128 : j * 128 + 128]
    scale = jnp.sum(scale_s[0] + scale_s[1], axis=-1, keepdims=True)
    sm[6, pl.ds(pl.multiple_of(core * 16, 16), 16)] = jnp.broadcast_to(scale, (16, 128))
    few, rest = pl.ds(0, 4), pl.ds(4, 4)
    little = []
    for k in range(1, 4):
        little.append(go(sm.at[few], qy1.at[k - 1], at_y(k)))
        little.append(go(sm.at[rest], qx1.at[k - 1], at_x(k)))

    finish(stage)
    mine = pl.ds(z * 9, 9)
    total = sb[mine].astype(F32)
    for k in range(ZC - 1):
        total = total + rc[k].astype(F32)
    full[core, rep, x, mine] = total.astype(BF)
    stage = []
    piece = full.at[core, rep, x, mine]
    for k in range(1, ZC):
        stage.append(go(piece, piece, at_z(k)))

    finish(little)
    s2[few] = sm[few] + qy1[0] + qy1[1] + qy1[2]
    s2[rest] = sm[rest] + qx1[0] + qx1[1] + qx1[2]
    little = []
    for k in range(1, 4):
        little.append(go(s2.at[few], qx2.at[k - 1], at_x(k)))
        little.append(go(s2.at[rest], qy2.at[k - 1], at_y(k)))

    finish(stage)
    piece = full.at[core, rep, x, low]
    stage = [go(piece, piece, other_rep)]
    piece = full.at[core, rep, x, high]
    stage += [go(piece, piece, at_x(k)) for k in range(1, XC)]
    piece = full.at[core, rep, x]
    handed = [go(piece, piece, other_core)]

    finish(little)
    s3[few] = s2[few] + qx2[0] + qx2[1] + qx2[2]
    s3[rest] = s2[rest] + qy2[0] + qy2[1] + qy2[2]
    little = [go(s3.at[lax.rem(z + k, ZC)], qz.at[k - 1], at_z(k)) for k in range(1, ZC)]

    finish(stage)
    piece = full.at[core, :, x, low]
    along = [go(piece, piece, at_x(k)) for k in range(1, XC)]
    piece = full.at[core, rep, :, high]
    across = go(piece, piece, other_rep)
    piece = full.at[core, 1 - rep, x, low]
    handed.append(go(piece, piece, other_core))
    for k in range(1, XC):
        piece = full.at[core, rep, lax.rem(x + k, XC), high]
        handed.append(go(piece, piece, other_core))

    finish(little)
    total = s3[z]
    for k in range(ZC - 1):
        total = total + qz[k]
    sz[core, z] = total
    little = [go(sz.at[core, z], sz.at[core, z], at_z(k)) for k in range(1, ZC)]

    for k in range(1, XC):
        along[k - 1].wait()
        piece = full.at[core, :, lax.rem(x + XC - k, XC), low]
        handed.append(go(piece, piece, other_core))
    across.wait()
    piece = full.at[core, 1 - rep, :, high]
    handed.append(go(piece, piece, other_core))
    finish(little)
    little = go(sz.at[core], sz.at[core], other_core)
    finish(handed)

    little.wait()
    small_out[...] = sz[0] + sz[1]


def assemble_kernel(factor, full, small, out_in, grad_in, gq_out, gp_out, conv_out, gain_out, scale_out, out, grad):
    out[...] = out_in[...]
    grad[...] = grad_in[...]
    lane = iota((48, 128), 1)
    for part in range(3):
        for m in range(6):
            halves = []
            for gets in range(2):
                block = 2 * m + gets
                c = block % 6 // 3
                old = block // 6 * 3 + block % 3
                start = TILES[old // 2] + part * 6
                tile = full[c, 0, 0, start : start + 6].astype(F32).reshape(48, 128)
                halves.append(tile if old % 2 == gets else pltpu.roll(tile, 64, 1))
            start = part * C + m * 128
            gq_out[:, start : start + 128] = jnp.where(lane < 64, halves[0], halves[1]) * factor
    for c in range(2):
        for m in range(6):
            tile = full[c, 0, 0, 54 + m * 3 : 57 + m * 3].astype(F32).reshape(24, 128)
            gp_out[c, :, m * 128 : m * 128 + 128] = tile * factor

    @pl.when(pl.program_id(0) == 0)
    def _():
        for j in range(6):
            conv_out[:, j * 128 : j * 128 + 128] = small[j, 0:27] * factor
            gain_out[:, j * 128 : j * 128 + 128] = small[j, 27:28] * factor
        head, row = iota((32, 128), 1), iota((32, 128), 0)
        mine = row == head % 12 // 6 * 16 + head // 12 * 6 + head % 6
        scale_out[...] = jnp.sum(jnp.where(mine, small[6], 0.0), axis=0, keepdims=True) * factor


def assemble(factor, full, small, out, grad):
    shape = jax.ShapeDtypeStruct
    return pl.pallas_call(
        functools.partial(assemble_kernel, factor),
        grid=(8,),
        out_shape=(
            shape((MINE, 3 * C), F32), shape((2, 192, C), F32),
            shape((27, C), F32), shape((1, C), F32), shape((1, 128), F32),
            shape(out.shape, BF), shape(out.shape, BF),
        ),
        in_specs=[
            pl.BlockSpec((2, 1, 1, 72, 8, 128), lambda i: (0, i // 4, i % 4, 0, 0, 0)),
            pl.BlockSpec((8, 32, 128), lambda i: (0, 0, 0)),
            pl.BlockSpec((1, 2, 16, C), lambda i: (i // 4, i % 4, 0, 0)),
            pl.BlockSpec((1, 2, 16, C), lambda i: (i // 4, i % 4, 0, 0)),
        ],
        out_specs=(
            pl.BlockSpec((48, 3 * C), lambda i: (i, 0)), pl.BlockSpec((2, 24, C), lambda i: (0, i, 0)),
            pl.BlockSpec((27, C), lambda i: (0, 0)), pl.BlockSpec((1, C), lambda i: (0, 0)),
            pl.BlockSpec((1, 128), lambda i: (0, 0)),
            pl.BlockSpec((1, 2, 16, C), lambda i: (i // 4, i % 4, 0, 0)),
            pl.BlockSpec((1, 2, 16, C), lambda i: (i // 4, i % 4, 0, 0)),
        ),
        compiler_params=pltpu.CompilerParams(vmem_limit_bytes=60 << 20),
        name="assemble",
    )(full, small, out, grad)


def whole_block(shift, scales, tokens, cot, wq, wp, weight, gain):
    shape = jax.ShapeDtypeStruct
    field = (2, 8, 16, C)
    tile = (8, 128)
    some = (32, 128)
    V = pltpu.VMEM
    copies = 96
    return pl.pallas_call(
        block_kernel,
        out_shape=(
            shape(field, BF), shape(field, BF), shape((2, 2, XC, 72) + tile, BF), shape((8,) + some, F32),
        ),
        in_specs=[SMEM, SMEM] + [VMEM] * 6,
        out_specs=(VMEM,) * 4,
        scratch_shapes=[
            V(field, BF), V((2, 256, C), BF), V((2, 256, C), BF),
            V((2, 2, MINE, 3 * MINE), BF), V((2, 2, MINE // 2, C), BF), V(field, F32),
            V((512, 512), BF), V((2, 256, 512), BF),
            V((512, C), BF), V((C, 512), BF), V((512, C), BF), V((512, MINE), BF), V((512, MINE), BF),
            V((512, MINE), BF), V((512, MINE), BF), V((2, 256, 256), F32),
            V((2, 16, 256), F32), V((C, MINE), F32), V((MINE, C), F32), V((2, 2, XC, 72) + tile, BF),
            V((3, 256, 512), BF), V((3, 256, 512), BF),
            V((3, 256, 512), BF), V((256, C), BF),
            V(field, F32), V(field, BF), V(field, BF),
            V((4, 10, 16, C), F32), V((4, 10, 16, C), F32), V((3,) + field, F32),
            V((3, XC, 36) + tile, BF), V((XC - 1, 2, 2, 36) + tile, BF),
            V((XC, 36) + tile, BF), V((2, 2, 36) + tile, BF),
            V((XC - 1, 36) + tile, BF), V((3, 36) + tile, BF),
            V((72,) + tile, BF), V((ZC - 1, 9) + tile, BF),
            V((8,) + some, F32), V((8,) + some, F32), V((8,) + some, F32), V((2, 8) + some, F32),
            V((3, 4) + some, F32), V((3, 4) + some, F32), V((3, 4) + some, F32), V((3, 4) + some, F32),
            V((ZC - 1,) + some, F32),
            DMA((copies,)), DMA((copies,)), DMA((3,)),
        ],
        compiler_params=pltpu.CompilerParams(
            collective_id=0, has_side_effects=True, vmem_limit_bytes=60 << 20
        ),
        name="whole_block",
    )(shift, scales, tokens, cot, wq, wp, weight, gain)


def per_device(tokens, cotangent, w_qkv, w_proj, conv_weight, norm_gain, head_scale, shift_offsets):
    output, grad_tokens, full, small = whole_block(
        shift_offsets, head_scale, tokens[0], cotangent[0].reshape(256, C), w_qkv, w_proj, conv_weight, norm_gain
    )
    factor = 1.0 / math.sqrt(lax.axis_size("rep") * lax.axis_size("dp") * SEQ * 256)
    grad_qkv, grad_proj, grad_conv, grad_gain, grad_scale, output, grad_tokens = assemble(
        factor, full, small, output, grad_tokens
    )
    return (
        output[None],
        grad_tokens[None],
        grad_qkv,
        grad_proj.reshape(MINE, C),
        grad_conv,
        grad_gain.reshape(C),
        grad_scale[0, :24],
    )


def solution(mesh):
    in_specs = (
        P(("rep", "dp"), "seq", None, None, None),
        P(("rep", "dp"), "seq", None, None, None),
        P("dp", None),
        P("dp", None),
        P(),
        P(),
        P(),
        P(),
    )
    out_specs = (
        P(("rep", "dp"), "seq", None, None, None),
        P(("rep", "dp"), "seq", None, None, None),
        P("dp", None),
        P("dp", None),
        P(),
        P(),
        P(),
    )
    return jax.shard_map(
        per_device, mesh=mesh, in_specs=in_specs, out_specs=out_specs, check_vma=False
    )
```

```python
import functools
import math

import jax
import jax.numpy as jnp
from jax import lax
from jax.experimental import pallas as pl
from jax.experimental.pallas import tpu as pltpu
from jax.sharding import PartitionSpec as P

MESH = pl.DeviceIdType.MESH
BF = jnp.bfloat16
F32 = jnp.float32
XC = 4
ZC = 8
SEQ = 64
C = 768
MINE = 384
TILES = (0, 36, 18)
VMEM = pl.BlockSpec(memory_space=pltpu.VMEM)
SMEM = pl.BlockSpec(memory_space=pltpu.SMEM)
DMA = pltpu.SemaphoreType.DMA


def nn(a, b):
    return lax.dot_general(a, b, (((1,), (0,)), ((), ())), preferred_element_type=F32)


def nt(a, b):
    return lax.dot_general(a, b, (((1,), (1,)), ((), ())), preferred_element_type=F32)


def tn(a, b):
    return lax.dot_general(a, b, (((0,), (0,)), ((), ())), preferred_element_type=F32)


def iota(shape, dim):
    return lax.broadcasted_iota(jnp.int32, shape, dim)


def place():
    rep, dp, seq = lax.axis_index("rep"), lax.axis_index("dp"), lax.axis_index("seq")
    return (rep, dp, seq, lax.rem(seq, 2))


def send(src, dst, s, r, to):
    c = pltpu.make_async_remote_copy(
        src_ref=src, dst_ref=dst, send_sem=s, recv_sem=r, device_id=to, device_id_type=MESH
    )
    c.start()
    return c


def greet(peers):
    barrier = pltpu.get_barrier_semaphore()
    for peer in peers:
        pl.semaphore_signal(barrier, inc=1, device_id=peer, device_id_type=MESH)
    pl.semaphore_wait(barrier, len(peers))


def fill_padded(xf, before, own, after):
    rows = jnp.zeros((4, 1, 16, C), F32)
    xf[:, 0:1] = rows
    xf[:, 9:10] = rows
    xf[0, 1:9] = before
    xf[1:3, 1:9] = own
    xf[3, 1:9] = after


def taps(xf, weight, d, lanes, flipped):
    sums = [jnp.zeros((8, 16, 128), F32) for _ in range(3)]
    for a in range(3):
        for b in range(3):
            rows = xf[d + a, b : b + 8, :, lanes]
            for e in range(3):
                t = 9 * a + 3 * b + e
                t = 26 - t if flipped else t
                sums[e] = sums[e] + weight[t : t + 1, lanes][None] * rows
    w = iota((8, 16, 128), 1)
    left = jnp.where(w == 0, 0.0, pltpu.roll(sums[0], 1, 1))
    right = jnp.where(w == 15, 0.0, pltpu.roll(sums[2], 15, 1))
    return sums[1] + left + right


def chunk(j):
    return pl.ds(pl.multiple_of(j * 128, 128), 128)


def normalise(rows):
    centred = rows - jnp.mean(rows, axis=-1, keepdims=True)
    inverse = lax.rsqrt(jnp.mean(centred * centred, axis=-1, keepdims=True) + 1e-05)
    return (centred * inverse, inverse)


def arrange(w, into, dp):
    lane, other = iota((128, 128), 0), iota((128, 128), 1)
    moves = {}
    for had in range(2):
        for gets in range(2):
            hit = (lane - 64 * had == other - 64 * gets) & (other // 64 == gets)
            moves[had, gets] = jnp.where(hit, 1.0, 0.0).astype(BF)
    for c in range(2):
        for k in range(9):
            part, group = k // 3, k % 3
            pieces = []
            for gets in range(2):
                block = 2 * group + gets
                old = part * 12 + block // 3 * 6 + c * 3 + block % 3
                start = old // 2 * 128
                pieces.append(nn(w[:, start : start + 128], moves[old % 2, gets]))
            start = group * MINE + part * 128
            into[c, dp, :, start : start + 128] = (pieces[0] + pieces[1]).astype(BF)


def source_of(n, r):
    b, d, h, j = n >> 8, (n >> 6) & 3, (n >> 3) & 7, n & 7
    return d * 128 + h * 16 + ((8 * b + j + r) & 15)


def head_sums(x, ones):
    high = x.astype(BF)
    low = (x - high.astype(F32)).astype(BF)
    return nn(high, ones) + nn(low, ones)


def attention(shift, scales, core, g, b, qkv_s, ba_s, att_s, bqkv_s, allow_s, scale_s):
    ones = jnp.where(iota((128, 128), 0) // 32 == iota((128, 128), 1) // 32, 1.0, 0.0).astype(BF)
    lane_head = iota((256, 128), 1) // 32
    rows = pl.ds(pl.multiple_of(b * 256, 256), 256)
    query = qkv_s[rows, 0:128].astype(F32)
    key = qkv_s[rows, 128:256].astype(F32)
    value = qkv_s[rows, 256:384]
    ba = ba_s[rows, g * 128 : g * 128 + 128]
    inv_q = lax.rsqrt(head_sums(query * query, ones) + 1.0)
    inv_k = lax.rsqrt(head_sums(key * key, ones) + 1.0)
    uq = (query * inv_q).astype(BF)
    uk = (key * inv_k).astype(BF)
    att = jnp.zeros((256, 128), F32)
    back_v = jnp.zeros((256, 128), F32)
    back_uq = jnp.zeros((256, 128), F32)
    back_uk = jnp.zeros((256, 128), F32)
    zero = jnp.zeros((256, 128), BF)
    for h in range(4):
        here = lane_head == h
        scale = scales[(g * 4 + h) // 6 * 12 + core * 6 + (g * 4 + h) % 6]
        uq_h = jnp.where(here, uq, zero)
        uk_h = jnp.where(here, uk, zero)
        v_h = jnp.where(here, value, zero)
        ba_h = jnp.where(here, ba, zero)
        cosine = nt(uk_h, uq)
        expo = jnp.exp(scale * cosine) * allow_s[b]
        prob = expo * (1.0 / jnp.sum(expo, axis=0, keepdims=True))
        weights = prob.astype(BF)
        att = att + tn(weights, v_h)
        back_v = back_v + nn(weights, ba_h)
        back_prob = nt(v_h, ba)
        mean = jnp.sum(prob * back_prob, axis=0, keepdims=True)
        back_score = prob * (back_prob - mean)
        scale_s[b, g * 4 + h : g * 4 + h + 1] = jnp.sum(back_score * cosine, axis=0, keepdims=True)
        scaled = (back_score * scale).astype(BF)
        back_uq = back_uq + tn(scaled, uk_h)
        back_uk = back_uk + nn(scaled, uq_h)
    att_s[rows, g * 128 : g * 128 + 128] = att.astype(BF)
    inner_q = head_sums(query * back_uq, ones)
    inner_k = head_sums(key * back_uk, ones)
    back_q = back_uq * inv_q - query * inner_q * (inv_q * inv_q * inv_q)
    back_k = back_uk * inv_k - key * inner_k * (inv_k * inv_k * inv_k)
    bqkv_s[rows, 0:128] = back_q.astype(BF)
    bqkv_s[rows, 128:256] = back_k.astype(BF)
    bqkv_s[rows, 256:384] = back_v.astype(BF)


def block_kernel(shift, scales, tokens_in, cot, wq_any, wp_in, weight, gain,
                 out, grad, full, small_out,
                 tokens, wq_in, halo, nwin, cwin, wq, wp, mixed, sel, res, x_s, xt_s, ct_s, qkv_s, ba_s, att_s, bqkv_s, allow_s,
                 scale_s, gq_s, gp_s, g, own, given,
                 recv, bn_s, bm, bmh, ph, xf, tf, sh, ra0, ra1, sa0, sa1, rb0, rb1, sb, rc,
                 sm, s2, s3, sz, qy1, qx1, qx2, qy2, qz, s_sem, r_sem, l_sem):
    rep, dp, seq, core = place()
    z = lax.rem(seq // 2, ZC)
    x = seq // (2 * ZC)
    y = rep * 2 + dp

    def at_y(step):
        there = lax.rem(y + step, 4)
        return (there // 2, lax.rem(there, 2), seq)

    def at_x(step):
        there = lax.rem(x + step, XC)
        return (rep, dp, (there * ZC + z) * 2 + core)

    def at_z(step):
        there = lax.rem(z + step, ZC)
        return (rep, dp, (x * ZC + there) * 2 + core)

    up = (rep, dp, lax.rem(seq + 1, SEQ))
    down = (rep, dp, lax.rem(seq + SEQ - 1, SEQ))
    partner = (rep, dp, lax.rem(seq + SEQ - 1 + 2 * core, SEQ))
    other_core = (rep, dp, seq + 1 - 2 * core)
    other_rep = (1 - rep, dp, seq)
    peers = [at_y(k) for k in range(1, 4)] + [at_x(k) for k in range(1, XC)]
    peers += [at_z(k) for k in range(1, ZC)] + [up, down]
    half = 1 - core
    local = [
        pltpu.make_async_copy(tokens_in, tokens, l_sem.at[0]),
        pltpu.make_async_copy(wq_any, wq_in, l_sem.at[1]),
        pltpu.make_async_copy(cot, cwin.at[half], l_sem.at[2]),
        pltpu.make_async_copy(wp_in.at[pl.ds(0, 192)], wp.at[0, dp], l_sem.at[3]),
        pltpu.make_async_copy(wp_in.at[pl.ds(192, 192)], wp.at[1, dp], l_sem.at[4]),
    ]
    for c in local:
        c.start()
    greet(peers)
    used = [0]

    def go(src, dst, to):
        n = used[0]
        used[0] += 1
        return send(src, dst, s_sem.at[n], r_sem.at[n], to)

    def finish(copies):
        for c in copies:
            c.wait()

    low, high = pl.ds(0, 36), pl.ds(36, 36)
    first = jnp.where(seq == 0, 0.0, 1.0).astype(F32)
    last = jnp.where(seq == SEQ - 1, 0.0, 1.0).astype(F32)
    halos = [go(tokens_in.at[0], halo.at[1], down), go(tokens_in.at[1], halo.at[0], up)]
    y_to = lax.rem(y + 3 + 2 * core, 4)
    y_peer = (y_to // 2, lax.rem(y_to, 2), seq)
    wp_came = go(wp_in.at[pl.ds(pl.multiple_of(core * 192, 64), 192)], wp.at[core, dp], y_peer)
    cots = go(cot, cwin.at[half], partner)
    local[1].wait()
    arrange(wq_in, wq, dp)
    wq_came = []
    for k in range(3):
        piece = wq.at[core, dp, :, k * MINE : k * MINE + MINE]
        wq_came.append(go(piece, piece, y_peer))
    local[0].wait()
    finish(halos)
    fill_padded(tf, halo[0].astype(F32) * first, tokens[...].astype(F32), halo[1].astype(F32) * last)

    norms = []
    for d in range(2):
        def mix_step(j, carry):
            lanes = chunk(j)
            mixed[d, :, :, lanes] = tf[d + 1, 1:9, :, lanes] + taps(tf, weight, d, lanes, False)
            return carry

        lax.fori_loop(0, 6, mix_step, 0)
        for h in range(0, 8, 4):
            unit, _ = normalise(mixed[d, h : h + 4].reshape(64, C))
            start = d * 128 + h * 16
            nwin[half, start : start + 64] = (unit * gain[...].reshape(1, C)).astype(BF)
        piece = nwin.at[half, pl.ds(d * 128, 128)]
        norms.append(go(piece, piece, partner))

    s, r = shift[0], shift[1]
    sel[...] = jnp.where(iota((512, 512), 1) == source_of(iota((512, 512), 0), r), 1.0, 0.0).astype(BF)
    for k in range(2):
        target = source_of(iota((256, 512), 1), r)
        res[k] = jnp.where(iota((256, 512), 0) + 256 * k == target, 1.0, 0.0).astype(BF)

    def code(n, b):
        h, j = (n >> 3) & 7, n & 7
        return jnp.where(h < s, 2, 0) + jnp.where(8 * b + j + r >= 16, 1, 0)

    for b in range(2):
        same = code(iota((256, 256), 0), b) == code(iota((256, 256), 1), b)
        allow_s[b] = jnp.where(same, 1.0, 0.0).astype(F32)
    scale_s[...] = jnp.zeros((2, 16, 256), F32)
    for c in local[2:]:
        c.wait()
    cots.wait()
    ct_s[...] = nn(sel[...], cwin[...].reshape(512, C)).astype(BF)
    wp_came.wait()
    ba_s[...] = nt(ct_s[...], wp[core].reshape(MINE, C)).astype(BF)
    finish(norms)
    ordered = nn(sel[...], nwin[...].reshape(512, C))
    x_s[...] = ordered.astype(BF)
    xt_s[...] = ordered.T.astype(BF)

    exchanges, stage, swaps = [], [], []
    for k in range(3):
        wq_came[k].wait()
        if k == 2:
            piece = wq.at[core, 1 - dp]
            swaps.append(go(piece, piece, other_core))
            piece = wp.at[core, 1 - dp]
            swaps.append(go(piece, piece, other_core))
        columns = wq[core, :, :, k * MINE : k * MINE + MINE].reshape(C, MINE)
        qkv_s[...] = nn(x_s[...], columns).astype(BF)

        def window(b, carry):
            attention(shift, scales, core, k, b, qkv_s, ba_s, att_s, bqkv_s, allow_s, scale_s)
            return carry

        lax.fori_loop(0, 2, window, 0)
        lanes = slice(k * 128, k * 128 + 128)
        given[k, :, 0:128] = nn(res[core], att_s[:, lanes]).astype(BF)
        given[k, :, 128:] = nn(res[core], bqkv_s[...]).astype(BF)
        exchanges.append(go(given.at[k], recv.at[k], partner))
        gq_s[...] = nn(xt_s[...], bqkv_s[...])

        def store(i, carry):
            d, p, to = i // 8, lax.rem(i // 4, 2), lax.rem(i, 4)
            for c in range(3):
                block = gq_s[pl.ds(pl.multiple_of(i * 48, 48), 48), c * 128 : (c + 1) * 128]
                start = TILES[k] + c * 6
                g[d, p, to, start : start + 6] = block.reshape(6, 8, 128).astype(BF)
            return carry

        lax.fori_loop(0, 16, store, 0)
        tiles = pl.ds(TILES[k], 18)
        away = pl.ds(TILES[k] % 36, 18)
        for step in range(1, 4):
            if k == 1:
                stage.append(go(g.at[:, :, lax.rem(x + step, XC), tiles], ra1.at[step - 1, :, :, away], at_x(step)))
            else:
                to = at_y(step)
                stage.append(go(g.at[to[1], to[0], :, tiles], ra0.at[step - 1, :, away], to))
        own[k, :, 0:128] = nn(res[half], att_s[:, lanes]).astype(BF)
        own[k, :, 128:] = nn(res[half], bqkv_s[...]).astype(BF)
    gp_s[...] = tn(att_s[...], ct_s[...])

    def store_proj(i, carry):
        d, p, to = i // 8, lax.rem(i // 4, 2), lax.rem(i, 4)
        for c in range(6):
            block = gp_s[pl.ds(pl.multiple_of(i * 24, 24), 24), c * 128 : (c + 1) * 128]
            g[d, p, to, 54 + c * 3 : 57 + c * 3] = block.reshape(3, 8, 128).astype(BF)
        return carry

    lax.fori_loop(0, 16, store_proj, 0)
    tiles, away = pl.ds(54, 18), pl.ds(18, 18)
    for step in range(1, 4):
        stage.append(go(g.at[:, :, lax.rem(x + step, XC), tiles], ra1.at[step - 1, :, :, away], at_x(step)))

    def wq_of(c, k):
        return wq[c, :, :, k * MINE : k * MINE + MINE].reshape(C, MINE)

    finish(swaps)
    back = nt(own[0, :, 128:], wq_of(core, 0))
    for k in range(1, 3):
        back = back + nt(own[k, :, 128:], wq_of(core, k))
    for k in range(3):
        exchanges[k].wait()
        back = back + nt(recv[k, :, 128:], wq_of(1 - core, k))
    bn_s[...] = back.astype(BF)
    def norm_step(i, total):
        d, h = i // 2, lax.rem(i, 2) * 4
        rows = pl.ds(pl.multiple_of(i * 64, 64), 64)
        unit, inverse = normalise(mixed[d, pl.ds(h, 4)].reshape(64, C))
        back_float = bn_s[rows].astype(F32)
        total = total + jnp.sum((back_float * unit).reshape(8, 8, C), axis=0)
        grad_unit = back_float * gain[...].reshape(1, C)
        mean = jnp.mean(grad_unit, axis=-1, keepdims=True)
        slope = jnp.mean(grad_unit * unit, axis=-1, keepdims=True)
        result = cwin[half, rows].astype(F32) + inverse * (grad_unit - mean - unit * slope)
        bm[d, pl.ds(h, 4)] = result.reshape(4, 16, C)
        bmh[d, pl.ds(h, 4)] = result.astype(BF).reshape(4, 16, C)
        return total

    gain_part = jnp.sum(lax.fori_loop(0, 4, norm_step, jnp.zeros((8, C), F32)), axis=0, keepdims=True)
    planes = [go(bmh.at[0], ph.at[1], down), go(bmh.at[1], ph.at[0], up)]
    finish(stage)

    def add_a(i, carry):
        total = g[dp, rep, i, low].astype(F32)
        for k in range(3):
            total = total + ra0[k, i].astype(F32)
        sa0[i] = total.astype(BF)
        d, r = lax.rem(i, 2), i // 2
        total = g[d, r, x, high].astype(F32)
        for k in range(XC - 1):
            total = total + ra1[k, d, r].astype(F32)
        sa1[d, r] = total.astype(BF)
        return carry

    lax.fori_loop(0, 4, add_a, 0)
    stage = []
    for k in range(1, XC):
        stage.append(go(sa0.at[lax.rem(x + k, XC)], rb0.at[k - 1], at_x(k)))
    for k in range(1, 4):
        to = at_y(k)
        stage.append(go(sa1.at[to[1], to[0]], rb1.at[k - 1], to))

    wp_mine, wp_other = wp[core].reshape(MINE, C), wp[1 - core].reshape(MINE, C)
    proj = jnp.zeros((256, C), F32)
    for k in range(3):
        rows = slice(k * 128, k * 128 + 128)
        proj = proj + nn(own[k, :, 0:128], wp_mine[rows]) + nn(recv[k, :, 0:128], wp_other[rows])
    out[...] = (mixed[...].reshape(256, C) + proj).astype(BF).reshape(2, 8, 16, C)

    finish(planes)
    fill_padded(xf, ph[0].astype(F32) * first, bm[...], ph[1].astype(F32) * last)

    def filter_step(i, carry):
        d, j = i // 6, lax.rem(i, 6)
        lanes = chunk(j)
        here = xf[d + 1, 1:9, :, lanes]
        grad[d, :, :, lanes] = (here + taps(xf, weight, d, lanes, True)).astype(BF)
        w = iota((8, 16, 128), 1)
        sh[0, d, :, :, lanes] = jnp.where(w == 15, 0.0, pltpu.roll(here, 15, 1))
        sh[1, d, :, :, lanes] = here
        sh[2, d, :, :, lanes] = jnp.where(w == 0, 0.0, pltpu.roll(here, 1, 1))
        return carry

    lax.fori_loop(0, 12, filter_step, 0)

    finish(stage)
    total = sa0[x].astype(F32)
    for k in range(XC - 1):
        total = total + rb0[k].astype(F32)
    sb[low] = total.astype(BF)
    total = sa1[dp, rep].astype(F32)
    for k in range(3):
        total = total + rb1[k].astype(F32)
    sb[high] = total.astype(BF)
    stage = []
    for k in range(1, ZC):
        stage.append(go(sb.at[pl.ds(lax.rem(z + k, ZC) * 9, 9)], rc.at[k - 1], at_z(k)))

    sm[...] = jnp.zeros((8, 32, 128), F32)

    def conv_step(j, carry):
        lanes = chunk(j)
        for a in range(3):
            for b in range(3):
                rows = tf[a : a + 2, b : b + 8, :, lanes]
                for e in range(3):
                    total = jnp.sum((sh[e, :, :, :, lanes] * rows).reshape(16, 16, 128), axis=0)
                    t = 9 * a + 3 * b + e
                    sm[j, t : t + 1] = jnp.sum(total, axis=0, keepdims=True)
        return carry

    lax.fori_loop(0, 6, conv_step, 0)
    for j in range(6):
        sm[j, 27:28] = gain_part[:, j * 128 : j * 128 + 128]
    scale = jnp.sum(scale_s[0] + scale_s[1], axis=-1, keepdims=True)
    sm[6, pl.ds(pl.multiple_of(core * 16, 16), 16)] = jnp.broadcast_to(scale, (16, 128))
    few, rest = pl.ds(0, 4), pl.ds(4, 4)
    little = []
    for k in range(1, 4):
        little.append(go(sm.at[few], qy1.at[k - 1], at_y(k)))
        little.append(go(sm.at[rest], qx1.at[k - 1], at_x(k)))

    finish(stage)
    mine = pl.ds(z * 9, 9)
    total = sb[mine].astype(F32)
    for k in range(ZC - 1):
        total = total + rc[k].astype(F32)
    full[core, rep, x, mine] = total.astype(BF)
    stage = []
    piece = full.at[core, rep, x, mine]
    for k in range(1, ZC):
        stage.append(go(piece, piece, at_z(k)))

    finish(little)
    s2[few] = sm[few] + qy1[0] + qy1[1] + qy1[2]
    s2[rest] = sm[rest] + qx1[0] + qx1[1] + qx1[2]
    little = []
    for k in range(1, 4):
        little.append(go(s2.at[few], qx2.at[k - 1], at_x(k)))
        little.append(go(s2.at[rest], qy2.at[k - 1], at_y(k)))

    finish(stage)
    piece = full.at[core, rep, x, low]
    stage = [go(piece, piece, other_rep)]
    piece = full.at[core, rep, x, high]
    stage += [go(piece, piece, at_x(k)) for k in range(1, XC)]
    piece = full.at[core, rep, x]
    handed = [go(piece, piece, other_core)]

    finish(little)
    s3[few] = s2[few] + qx2[0] + qx2[1] + qx2[2]
    s3[rest] = s2[rest] + qy2[0] + qy2[1] + qy2[2]
    little = [go(s3.at[lax.rem(z + k, ZC)], qz.at[k - 1], at_z(k)) for k in range(1, ZC)]

    finish(stage)
    piece = full.at[core, :, x, low]
    along = [go(piece, piece, at_x(k)) for k in range(1, XC)]
    piece = full.at[core, rep, :, high]
    across = go(piece, piece, other_rep)
    piece = full.at[core, 1 - rep, x, low]
    handed.append(go(piece, piece, other_core))
    for k in range(1, XC):
        piece = full.at[core, rep, lax.rem(x + k, XC), high]
        handed.append(go(piece, piece, other_core))

    finish(little)
    total = s3[z]
    for k in range(ZC - 1):
        total = total + qz[k]
    sz[core, z] = total
    little = [go(sz.at[core, z], sz.at[core, z], at_z(k)) for k in range(1, ZC)]

    for k in range(1, XC):
        along[k - 1].wait()
        piece = full.at[core, :, lax.rem(x + XC - k, XC), low]
        handed.append(go(piece, piece, other_core))
    across.wait()
    piece = full.at[core, 1 - rep, :, high]
    handed.append(go(piece, piece, other_core))
    finish(little)
    little = go(sz.at[core], sz.at[core], other_core)
    finish(handed)

    little.wait()
    small_out[...] = sz[0] + sz[1]


def assemble_kernel(factor, full, small, out_in, grad_in, gq_out, gp_out, conv_out, gain_out, scale_out, out, grad):
    out[...] = out_in[...]
    grad[...] = grad_in[...]
    lane = iota((48, 128), 1)
    for part in range(3):
        for m in range(6):
            halves = []
            for gets in range(2):
                block = 2 * m + gets
                c = block % 6 // 3
                old = block // 6 * 3 + block % 3
                start = TILES[old // 2] + part * 6
                tile = full[c, 0, 0, start : start + 6].astype(F32).reshape(48, 128)
                halves.append(tile if old % 2 == gets else pltpu.roll(tile, 64, 1))
            start = part * C + m * 128
            gq_out[:, start : start + 128] = jnp.where(lane < 64, halves[0], halves[1]) * factor
    for c in range(2):
        for m in range(6):
            tile = full[c, 0, 0, 54 + m * 3 : 57 + m * 3].astype(F32).reshape(24, 128)
            gp_out[c, :, m * 128 : m * 128 + 128] = tile * factor

    @pl.when(pl.program_id(0) == 0)
    def _():
        for j in range(6):
            conv_out[:, j * 128 : j * 128 + 128] = small[j, 0:27] * factor
            gain_out[j * 128 : j * 128 + 128] = small[j, 27] * factor
        head, row = iota((32, 128), 1), iota((32, 128), 0)
        mine = row == head % 12 // 6 * 16 + head // 12 * 6 + head % 6
        scale_out[...] = jnp.sum(jnp.where(mine, small[6], 0.0), axis=0) * factor


def assemble(factor, full, small, out, grad):
    shape = jax.ShapeDtypeStruct
    return pl.pallas_call(
        functools.partial(assemble_kernel, factor),
        grid=(8,),
        out_shape=(
            shape((MINE, 3 * C), F32), shape((2, 192, C), F32),
            shape((27, C), F32), shape((C,), F32), shape((128,), F32),
            shape(out.shape, BF), shape(out.shape, BF),
        ),
        in_specs=[
            pl.BlockSpec((2, 1, 1, 72, 8, 128), lambda i: (0, i // 4, i % 4, 0, 0, 0)),
            pl.BlockSpec((8, 32, 128), lambda i: (0, 0, 0)),
            pl.BlockSpec((1, 2, 16, C), lambda i: (i // 4, i % 4, 0, 0)),
            pl.BlockSpec((1, 2, 16, C), lambda i: (i // 4, i % 4, 0, 0)),
        ],
        out_specs=(
            pl.BlockSpec((48, 3 * C), lambda i: (i, 0)), pl.BlockSpec((2, 24, C), lambda i: (0, i, 0)),
            pl.BlockSpec((27, C), lambda i: (0, 0)), pl.BlockSpec((C,), lambda i: (0,)),
            pl.BlockSpec((128,), lambda i: (0,)),
            pl.BlockSpec((1, 2, 16, C), lambda i: (i // 4, i % 4, 0, 0)),
            pl.BlockSpec((1, 2, 16, C), lambda i: (i // 4, i % 4, 0, 0)),
        ),
        compiler_params=pltpu.CompilerParams(vmem_limit_bytes=60 << 20),
        name="assemble",
    )(full, small, out, grad)


def whole_block(shift, scales, tokens, cot, wq, wp, weight, gain):
    shape = jax.ShapeDtypeStruct
    field = (2, 8, 16, C)
    tile = (8, 128)
    some = (32, 128)
    V = pltpu.VMEM
    copies = 96
    return pl.pallas_call(
        block_kernel,
        out_shape=(
            shape(field, BF), shape(field, BF), shape((2, 2, XC, 72) + tile, BF), shape((8,) + some, F32),
        ),
        in_specs=[SMEM, SMEM] + [pl.BlockSpec(memory_space=pl.ANY)] * 4 + [VMEM] * 2,
        out_specs=(VMEM,) * 4,
        scratch_shapes=[
            V(field, BF), V((MINE, 3 * C), BF), V(field, BF), V((2, 256, C), BF), V((2, 256, C), BF),
            V((2, 2, MINE, 3 * MINE), BF), V((2, 2, MINE // 2, C), BF), V(field, F32),
            V((512, 512), BF), V((2, 256, 512), BF),
            V((512, C), BF), V((C, 512), BF), V((512, C), BF), V((512, MINE), BF), V((512, MINE), BF),
            V((512, MINE), BF), V((512, MINE), BF), V((2, 256, 256), F32),
            V((2, 16, 256), F32), V((C, MINE), F32), V((MINE, C), F32), V((2, 2, XC, 72) + tile, BF),
            V((3, 256, 512), BF), V((3, 256, 512), BF),
            V((3, 256, 512), BF), V((256, C), BF),
            V(field, F32), V(field, BF), V(field, BF),
            V((4, 10, 16, C), F32), V((4, 10, 16, C), F32), V((3,) + field, F32),
            V((3, XC, 36) + tile, BF), V((XC - 1, 2, 2, 36) + tile, BF),
            V((XC, 36) + tile, BF), V((2, 2, 36) + tile, BF),
            V((XC - 1, 36) + tile, BF), V((3, 36) + tile, BF),
            V((72,) + tile, BF), V((ZC - 1, 9) + tile, BF),
            V((8,) + some, F32), V((8,) + some, F32), V((8,) + some, F32), V((2, 8) + some, F32),
            V((3, 4) + some, F32), V((3, 4) + some, F32), V((3, 4) + some, F32), V((3, 4) + some, F32),
            V((ZC - 1,) + some, F32),
            DMA((copies,)), DMA((copies,)), DMA((5,)),
        ],
        compiler_params=pltpu.CompilerParams(
            collective_id=0, has_side_effects=True, vmem_limit_bytes=60 << 20
        ),
        name="whole_block",
    )(shift, scales, tokens, cot, wq, wp, weight, gain)


def per_device(tokens, cotangent, w_qkv, w_proj, conv_weight, norm_gain, head_scale, shift_offsets):
    output, grad_tokens, full, small = whole_block(
        shift_offsets, head_scale, tokens[0], cotangent[0].reshape(256, C), w_qkv, w_proj, conv_weight, norm_gain
    )
    factor = 1.0 / math.sqrt(lax.axis_size("rep") * lax.axis_size("dp") * SEQ * 256)
    grad_qkv, grad_proj, grad_conv, grad_gain, grad_scale, output, grad_tokens = assemble(
        factor, full, small, output, grad_tokens
    )
    return (
        output[None],
        grad_tokens[None],
        grad_qkv,
        grad_proj.reshape(MINE, C),
        grad_conv,
        grad_gain,
        grad_scale[:24],
    )


def solution(mesh):
    in_specs = (
        P(("rep", "dp"), "seq", None, None, None),
        P(("rep", "dp"), "seq", None, None, None),
        P("dp", None),
        P("dp", None),
        P(),
        P(),
        P(),
        P(),
    )
    out_specs = (
        P(("rep", "dp"), "seq", None, None, None),
        P(("rep", "dp"), "seq", None, None, None),
        P("dp", None),
        P("dp", None),
        P(),
        P(),
        P(),
    )
    return jax.shard_map(
        per_device, mesh=mesh, in_specs=in_specs, out_specs=out_specs, check_vma=False
    )
```

```python
import functools
import math

import jax
import jax.numpy as jnp
from jax import lax
from jax.experimental import pallas as pl
from jax.experimental.pallas import tpu as pltpu
from jax.sharding import PartitionSpec as P

MESH = pl.DeviceIdType.MESH
BF = jnp.bfloat16
F32 = jnp.float32
XC = 4
ZC = 8
SEQ = 64
C = 768
MINE = 384
TILES = (0, 36, 18)
VMEM = pl.BlockSpec(memory_space=pltpu.VMEM)
SMEM = pl.BlockSpec(memory_space=pltpu.SMEM)
DMA = pltpu.SemaphoreType.DMA


def nn(a, b):
    return lax.dot_general(a, b, (((1,), (0,)), ((), ())), preferred_element_type=F32)


def nt(a, b):
    return lax.dot_general(a, b, (((1,), (1,)), ((), ())), preferred_element_type=F32)


def tn(a, b):
    return lax.dot_general(a, b, (((0,), (0,)), ((), ())), preferred_element_type=F32)


def iota(shape, dim):
    return lax.broadcasted_iota(jnp.int32, shape, dim)


def place():
    rep, dp, seq = lax.axis_index("rep"), lax.axis_index("dp"), lax.axis_index("seq")
    return (rep, dp, seq, lax.rem(seq, 2))


def send(src, dst, s, r, to):
    c = pltpu.make_async_remote_copy(
        src_ref=src, dst_ref=dst, send_sem=s, recv_sem=r, device_id=to, device_id_type=MESH
    )
    c.start()
    return c


def greet(peers):
    barrier = pltpu.get_barrier_semaphore()
    for peer in peers:
        pl.semaphore_signal(barrier, inc=1, device_id=peer, device_id_type=MESH)
    pl.semaphore_wait(barrier, len(peers))


def fill_padded(xf, before, own, after):
    rows = jnp.zeros((4, 1, 16, C), F32)
    xf[:, 0:1] = rows
    xf[:, 9:10] = rows
    xf[0, 1:9] = before
    xf[1:3, 1:9] = own
    xf[3, 1:9] = after


def taps(xf, weight, d, lanes, flipped):
    sums = [jnp.zeros((8, 16, 128), F32) for _ in range(3)]
    for a in range(3):
        for b in range(3):
            rows = xf[d + a, b : b + 8, :, lanes]
            for e in range(3):
                t = 9 * a + 3 * b + e
                t = 26 - t if flipped else t
                sums[e] = sums[e] + weight[t : t + 1, lanes][None] * rows
    w = iota((8, 16, 128), 1)
    left = jnp.where(w == 0, 0.0, pltpu.roll(sums[0], 1, 1))
    right = jnp.where(w == 15, 0.0, pltpu.roll(sums[2], 15, 1))
    return sums[1] + left + right


def chunk(j):
    return pl.ds(pl.multiple_of(j * 128, 128), 128)


def normalise(rows):
    centred = rows - jnp.mean(rows, axis=-1, keepdims=True)
    inverse = lax.rsqrt(jnp.mean(centred * centred, axis=-1, keepdims=True) + 1e-05)
    return (centred * inverse, inverse)


def arrange(w, into, dp):
    lane, other = iota((128, 128), 0), iota((128, 128), 1)
    moves = {}
    for had in range(2):
        for gets in range(2):
            hit = (lane - 64 * had == other - 64 * gets) & (other // 64 == gets)
            moves[had, gets] = jnp.where(hit, 1.0, 0.0).astype(BF)
    for c in range(2):
        for k in range(9):
            part, group = k // 3, k % 3
            pieces = []
            for gets in range(2):
                block = 2 * group + gets
                old = part * 12 + block // 3 * 6 + c * 3 + block % 3
                start = old // 2 * 128
                pieces.append(nn(w[:, start : start + 128], moves[old % 2, gets]))
            start = group * MINE + part * 128
            into[c, dp, :, start : start + 128] = (pieces[0] + pieces[1]).astype(BF)


def source_of(n, r):
    b, d, h, j = n >> 8, (n >> 6) & 3, (n >> 3) & 7, n & 7
    return d * 128 + h * 16 + ((8 * b + j + r) & 15)


def head_sums(x, ones):
    high = x.astype(BF)
    low = (x - high.astype(F32)).astype(BF)
    return nn(high, ones) + nn(low, ones)


def attention(shift, scales, core, g, b, qkv_s, ba_s, att_s, bqkv_s, allow_s, scale_s):
    ones = jnp.where(iota((128, 128), 0) // 32 == iota((128, 128), 1) // 32, 1.0, 0.0).astype(BF)
    lane_head = iota((256, 128), 1) // 32
    rows = pl.ds(pl.multiple_of(b * 256, 256), 256)
    query = qkv_s[rows, 0:128].astype(F32)
    key = qkv_s[rows, 128:256].astype(F32)
    value = qkv_s[rows, 256:384]
    ba = ba_s[rows, g * 128 : g * 128 + 128]
    inv_q = lax.rsqrt(head_sums(query * query, ones) + 1.0)
    inv_k = lax.rsqrt(head_sums(key * key, ones) + 1.0)
    uq = (query * inv_q).astype(BF)
    uk = (key * inv_k).astype(BF)
    att = jnp.zeros((256, 128), F32)
    back_v = jnp.zeros((256, 128), F32)
    back_uq = jnp.zeros((256, 128), F32)
    back_uk = jnp.zeros((256, 128), F32)
    zero = jnp.zeros((256, 128), BF)
    for h in range(4):
        here = lane_head == h
        scale = scales[(g * 4 + h) // 6 * 12 + core * 6 + (g * 4 + h) % 6]
        uq_h = jnp.where(here, uq, zero)
        uk_h = jnp.where(here, uk, zero)
        v_h = jnp.where(here, value, zero)
        ba_h = jnp.where(here, ba, zero)
        cosine = nt(uk_h, uq)
        expo = jnp.exp(scale * cosine) * allow_s[b]
        prob = expo * (1.0 / jnp.sum(expo, axis=0, keepdims=True))
        weights = prob.astype(BF)
        att = att + tn(weights, v_h)
        back_v = back_v + nn(weights, ba_h)
        back_prob = nt(v_h, ba)
        mean = jnp.sum(prob * back_prob, axis=0, keepdims=True)
        back_score = prob * (back_prob - mean)
        scale_s[b, g * 4 + h : g * 4 + h + 1] = jnp.sum(back_score * cosine, axis=0, keepdims=True)
        scaled = (back_score * scale).astype(BF)
        back_uq = back_uq + tn(scaled, uk_h)
        back_uk = back_uk + nn(scaled, uq_h)
    att_s[rows, g * 128 : g * 128 + 128] = att.astype(BF)
    inner_q = head_sums(query * back_uq, ones)
    inner_k = head_sums(key * back_uk, ones)
    back_q = back_uq * inv_q - query * inner_q * (inv_q * inv_q * inv_q)
    back_k = back_uk * inv_k - key * inner_k * (inv_k * inv_k * inv_k)
    bqkv_s[rows, 0:128] = back_q.astype(BF)
    bqkv_s[rows, 128:256] = back_k.astype(BF)
    bqkv_s[rows, 256:384] = back_v.astype(BF)


def block_kernel(shift, scales, tokens_in, cot, wq_any, wp_in, weight, gain,
                 out, grad, full, small_out,
                 tokens, wq_in, halo, nwin, cwin, wq, wp, mixed, sel, res, x_s, xt_s, ct_s, qkv_s, ba_s, att_s, bqkv_s, allow_s,
                 scale_s, gq_s, gp_s, g, own, given,
                 recv, bn_s, bm, bmh, ph, xf, tf, sh, ra0, ra1, sa0, sa1, rb0, rb1, sb, rc,
                 sm, s2, s3, sz, qy1, qx1, qx2, qy2, qz, s_sem, r_sem, l_sem):
    rep, dp, seq, core = place()
    z = lax.rem(seq // 2, ZC)
    x = seq // (2 * ZC)
    y = rep * 2 + dp

    def at_y(step):
        there = lax.rem(y + step, 4)
        return (there // 2, lax.rem(there, 2), seq)

    def at_x(step):
        there = lax.rem(x + step, XC)
        return (rep, dp, (there * ZC + z) * 2 + core)

    def at_z(step):
        there = lax.rem(z + step, ZC)
        return (rep, dp, (x * ZC + there) * 2 + core)

    up = (rep, dp, lax.rem(seq + 1, SEQ))
    down = (rep, dp, lax.rem(seq + SEQ - 1, SEQ))
    partner = (rep, dp, lax.rem(seq + SEQ - 1 + 2 * core, SEQ))
    other_core = (rep, dp, seq + 1 - 2 * core)
    other_rep = (1 - rep, dp, seq)
    peers = [at_y(k) for k in range(1, 4)] + [at_x(k) for k in range(1, XC)]
    peers += [at_z(k) for k in range(1, ZC)] + [up, down]
    half = 1 - core
    local = [
        pltpu.make_async_copy(tokens_in, tokens, l_sem.at[0]),
        pltpu.make_async_copy(wq_any, wq_in, l_sem.at[1]),
        pltpu.make_async_copy(cot, cwin.at[half], l_sem.at[2]),
        pltpu.make_async_copy(wp_in.at[pl.ds(0, 192)], wp.at[0, dp], l_sem.at[3]),
        pltpu.make_async_copy(wp_in.at[pl.ds(192, 192)], wp.at[1, dp], l_sem.at[4]),
    ]
    for c in local:
        c.start()
    greet(peers)
    used = [0]

    def go(src, dst, to):
        n = used[0]
        used[0] += 1
        return send(src, dst, s_sem.at[n], r_sem.at[n], to)

    def finish(copies):
        for c in copies:
            c.wait()

    low, high = pl.ds(0, 36), pl.ds(36, 36)
    first = jnp.where(seq == 0, 0.0, 1.0).astype(F32)
    last = jnp.where(seq == SEQ - 1, 0.0, 1.0).astype(F32)
    halos = [go(tokens_in.at[0], halo.at[1], down), go(tokens_in.at[1], halo.at[0], up)]
    y_to = lax.rem(y + 3 + 2 * core, 4)
    y_peer = (y_to // 2, lax.rem(y_to, 2), seq)
    wp_came = go(wp_in.at[pl.ds(pl.multiple_of(core * 192, 64), 192)], wp.at[core, dp], y_peer)
    cots = go(cot, cwin.at[half], partner)
    local[1].wait()
    arrange(wq_in, wq, dp)
    wq_came = []
    for k in range(3):
        piece = wq.at[core, dp, :, k * MINE : k * MINE + MINE]
        wq_came.append(go(piece, piece, y_peer))
    local[0].wait()
    finish(halos)
    fill_padded(tf, halo[0].astype(F32) * first, tokens[...].astype(F32), halo[1].astype(F32) * last)

    norms = []
    for d in range(2):
        def mix_step(j, carry):
            lanes = chunk(j)
            mixed[d, :, :, lanes] = tf[d + 1, 1:9, :, lanes] + taps(tf, weight, d, lanes, False)
            return carry

        lax.fori_loop(0, 6, mix_step, 0)
        for h in range(0, 8, 4):
            unit, _ = normalise(mixed[d, h : h + 4].reshape(64, C))
            start = d * 128 + h * 16
            nwin[half, start : start + 64] = (unit * gain[...].reshape(1, C)).astype(BF)
        piece = nwin.at[half, pl.ds(d * 128, 128)]
        norms.append(go(piece, piece, partner))

    s, r = shift[0], shift[1]
    sel[...] = jnp.where(iota((512, 512), 1) == source_of(iota((512, 512), 0), r), 1.0, 0.0).astype(BF)
    for k in range(2):
        target = source_of(iota((256, 512), 1), r)
        res[k] = jnp.where(iota((256, 512), 0) + 256 * k == target, 1.0, 0.0).astype(BF)

    def code(n, b):
        h, j = (n >> 3) & 7, n & 7
        return jnp.where(h < s, 2, 0) + jnp.where(8 * b + j + r >= 16, 1, 0)

    for b in range(2):
        same = code(iota((256, 256), 0), b) == code(iota((256, 256), 1), b)
        allow_s[b] = jnp.where(same, 1.0, 0.0).astype(F32)
    scale_s[...] = jnp.zeros((2, 16, 256), F32)
    for c in local[2:]:
        c.wait()
    cots.wait()
    ct_s[...] = nn(sel[...], cwin[...].reshape(512, C)).astype(BF)
    wp_came.wait()
    ba_s[...] = nt(ct_s[...], wp[core].reshape(MINE, C)).astype(BF)
    finish(norms)
    ordered = nn(sel[...], nwin[...].reshape(512, C))
    x_s[...] = ordered.astype(BF)
    xt_s[...] = ordered.T.astype(BF)

    def keep_own(k):
        own[k, :, 0:128] = nn(res[half], att_s[:, k * 128 : k * 128 + 128]).astype(BF)
        own[k, :, 128:] = nn(res[half], bqkv_s[...]).astype(BF)

    exchanges, stage, swaps = [], [], []
    for k in range(3):
        wq_came[k].wait()
        if k == 2:
            piece = wq.at[core, 1 - dp]
            swaps.append(go(piece, piece, other_core))
            piece = wp.at[core, 1 - dp]
            swaps.append(go(piece, piece, other_core))
        columns = wq[core, :, :, k * MINE : k * MINE + MINE].reshape(C, MINE)
        qkv_s[...] = nn(x_s[...], columns).astype(BF)

        def window(b, carry):
            attention(shift, scales, core, k, b, qkv_s, ba_s, att_s, bqkv_s, allow_s, scale_s)
            return carry

        lax.fori_loop(0, 2, window, 0)
        lanes = slice(k * 128, k * 128 + 128)
        given[k, :, 0:128] = nn(res[core], att_s[:, lanes]).astype(BF)
        given[k, :, 128:] = nn(res[core], bqkv_s[...]).astype(BF)
        exchanges.append(go(given.at[k], recv.at[k], partner))
        gq_s[...] = nn(xt_s[...], bqkv_s[...])

        def store(i, carry):
            d, p, to = i // 8, lax.rem(i // 4, 2), lax.rem(i, 4)
            for c in range(3):
                block = gq_s[pl.ds(pl.multiple_of(i * 48, 48), 48), c * 128 : (c + 1) * 128]
                start = TILES[k] + c * 6
                g[d, p, to, start : start + 6] = block.reshape(6, 8, 128).astype(BF)
            return carry

        lax.fori_loop(0, 16, store, 0)
        tiles = pl.ds(TILES[k], 18)
        away = pl.ds(TILES[k] % 36, 18)
        for step in range(1, 4):
            if k == 1:
                stage.append(go(g.at[:, :, lax.rem(x + step, XC), tiles], ra1.at[step - 1, :, :, away], at_x(step)))
            else:
                to = at_y(step)
                stage.append(go(g.at[to[1], to[0], :, tiles], ra0.at[step - 1, :, away], to))
        if k < 2:
            keep_own(k)
    gp_s[...] = tn(att_s[...], ct_s[...])

    def store_proj(i, carry):
        d, p, to = i // 8, lax.rem(i // 4, 2), lax.rem(i, 4)
        for c in range(6):
            block = gp_s[pl.ds(pl.multiple_of(i * 24, 24), 24), c * 128 : (c + 1) * 128]
            g[d, p, to, 54 + c * 3 : 57 + c * 3] = block.reshape(3, 8, 128).astype(BF)
        return carry

    lax.fori_loop(0, 16, store_proj, 0)
    tiles, away = pl.ds(54, 18), pl.ds(18, 18)
    for step in range(1, 4):
        stage.append(go(g.at[:, :, lax.rem(x + step, XC), tiles], ra1.at[step - 1, :, :, away], at_x(step)))

    keep_own(2)

    def wq_of(c, k):
        return wq[c, :, :, k * MINE : k * MINE + MINE].reshape(C, MINE)

    finish(swaps)
    back = nt(own[0, :, 128:], wq_of(core, 0))
    for k in range(1, 3):
        back = back + nt(own[k, :, 128:], wq_of(core, k))
    for k in range(3):
        exchanges[k].wait()
        back = back + nt(recv[k, :, 128:], wq_of(1 - core, k))
    bn_s[...] = back.astype(BF)
    def norm_step(i, total):
        d, h = i // 2, lax.rem(i, 2) * 4
        rows = pl.ds(pl.multiple_of(i * 64, 64), 64)
        unit, inverse = normalise(mixed[d, pl.ds(h, 4)].reshape(64, C))
        back_float = bn_s[rows].astype(F32)
        total = total + jnp.sum((back_float * unit).reshape(8, 8, C), axis=0)
        grad_unit = back_float * gain[...].reshape(1, C)
        mean = jnp.mean(grad_unit, axis=-1, keepdims=True)
        slope = jnp.mean(grad_unit * unit, axis=-1, keepdims=True)
        result = cwin[half, rows].astype(F32) + inverse * (grad_unit - mean - unit * slope)
        bm[d, pl.ds(h, 4)] = result.reshape(4, 16, C)
        bmh[d, pl.ds(h, 4)] = result.astype(BF).reshape(4, 16, C)
        return total

    gain_part = jnp.sum(lax.fori_loop(0, 4, norm_step, jnp.zeros((8, C), F32)), axis=0, keepdims=True)
    planes = [go(bmh.at[0], ph.at[1], down), go(bmh.at[1], ph.at[0], up)]
    finish(stage)

    def add_a(i, carry):
        total = g[dp, rep, i, low].astype(F32)
        for k in range(3):
            total = total + ra0[k, i].astype(F32)
        sa0[i] = total.astype(BF)
        d, r = lax.rem(i, 2), i // 2
        total = g[d, r, x, high].astype(F32)
        for k in range(XC - 1):
            total = total + ra1[k, d, r].astype(F32)
        sa1[d, r] = total.astype(BF)
        return carry

    lax.fori_loop(0, 4, add_a, 0)
    stage = []
    for k in range(1, XC):
        stage.append(go(sa0.at[lax.rem(x + k, XC)], rb0.at[k - 1], at_x(k)))
    for k in range(1, 4):
        to = at_y(k)
        stage.append(go(sa1.at[to[1], to[0]], rb1.at[k - 1], to))

    wp_mine, wp_other = wp[core].reshape(MINE, C), wp[1 - core].reshape(MINE, C)
    proj = jnp.zeros((256, C), F32)
    for k in range(3):
        rows = slice(k * 128, k * 128 + 128)
        proj = proj + nn(own[k, :, 0:128], wp_mine[rows]) + nn(recv[k, :, 0:128], wp_other[rows])
    out[...] = (mixed[...].reshape(256, C) + proj).astype(BF).reshape(2, 8, 16, C)

    finish(planes)
    fill_padded(xf, ph[0].astype(F32) * first, bm[...], ph[1].astype(F32) * last)

    def filter_step(i, carry):
        d, j = i // 6, lax.rem(i, 6)
        lanes = chunk(j)
        here = xf[d + 1, 1:9, :, lanes]
        grad[d, :, :, lanes] = (here + taps(xf, weight, d, lanes, True)).astype(BF)
        w = iota((8, 16, 128), 1)
        sh[0, d, :, :, lanes] = jnp.where(w == 15, 0.0, pltpu.roll(here, 15, 1))
        sh[1, d, :, :, lanes] = here
        sh[2, d, :, :, lanes] = jnp.where(w == 0, 0.0, pltpu.roll(here, 1, 1))
        return carry

    lax.fori_loop(0, 12, filter_step, 0)

    finish(stage)
    total = sa0[x].astype(F32)
    for k in range(XC - 1):
        total = total + rb0[k].astype(F32)
    sb[low] = total.astype(BF)
    total = sa1[dp, rep].astype(F32)
    for k in range(3):
        total = total + rb1[k].astype(F32)
    sb[high] = total.astype(BF)
    stage = []
    for k in range(1, ZC):
        stage.append(go(sb.at[pl.ds(lax.rem(z + k, ZC) * 9, 9)], rc.at[k - 1], at_z(k)))

    sm[...] = jnp.zeros((8, 32, 128), F32)

    def conv_step(j, carry):
        lanes = chunk(j)
        for a in range(3):
            for b in range(3):
                rows = tf[a : a + 2, b : b + 8, :, lanes]
                for e in range(3):
                    total = jnp.sum((sh[e, :, :, :, lanes] * rows).reshape(16, 16, 128), axis=0)
                    t = 9 * a + 3 * b + e
                    sm[j, t : t + 1] = jnp.sum(total, axis=0, keepdims=True)
        return carry

    lax.fori_loop(0, 6, conv_step, 0)
    for j in range(6):
        sm[j, 27:28] = gain_part[:, j * 128 : j * 128 + 128]
    scale = jnp.sum(scale_s[0] + scale_s[1], axis=-1, keepdims=True)
    sm[6, pl.ds(pl.multiple_of(core * 16, 16), 16)] = jnp.broadcast_to(scale, (16, 128))
    few, rest = pl.ds(0, 4), pl.ds(4, 4)
    little = []
    for k in range(1, 4):
        little.append(go(sm.at[few], qy1.at[k - 1], at_y(k)))
        little.append(go(sm.at[rest], qx1.at[k - 1], at_x(k)))

    finish(stage)
    mine = pl.ds(z * 9, 9)
    total = sb[mine].astype(F32)
    for k in range(ZC - 1):
        total = total + rc[k].astype(F32)
    full[core, rep, x, mine] = total.astype(BF)
    stage = []
    piece = full.at[core, rep, x, mine]
    for k in range(1, ZC):
        stage.append(go(piece, piece, at_z(k)))

    finish(little)
    s2[few] = sm[few] + qy1[0] + qy1[1] + qy1[2]
    s2[rest] = sm[rest] + qx1[0] + qx1[1] + qx1[2]
    little = []
    for k in range(1, 4):
        little.append(go(s2.at[few], qx2.at[k - 1], at_x(k)))
        little.append(go(s2.at[rest], qy2.at[k - 1], at_y(k)))

    finish(stage)
    piece = full.at[core, rep, x, low]
    stage = [go(piece, piece, other_rep)]
    piece = full.at[core, rep, x, high]
    stage += [go(piece, piece, at_x(k)) for k in range(1, XC)]
    piece = full.at[core, rep, x]
    handed = [go(piece, piece, other_core)]

    finish(little)
    s3[few] = s2[few] + qx2[0] + qx2[1] + qx2[2]
    s3[rest] = s2[rest] + qy2[0] + qy2[1] + qy2[2]
    little = [go(s3.at[lax.rem(z + k, ZC)], qz.at[k - 1], at_z(k)) for k in range(1, ZC)]

    finish(stage)
    piece = full.at[core, :, x, low]
    along = [go(piece, piece, at_x(k)) for k in range(1, XC)]
    piece = full.at[core, rep, :, high]
    across = go(piece, piece, other_rep)
    piece = full.at[core, 1 - rep, x, low]
    handed.append(go(piece, piece, other_core))
    for k in range(1, XC):
        piece = full.at[core, rep, lax.rem(x + k, XC), high]
        handed.append(go(piece, piece, other_core))

    finish(little)
    total = s3[z]
    for k in range(ZC - 1):
        total = total + qz[k]
    sz[core, z] = total
    little = [go(sz.at[core, z], sz.at[core, z], at_z(k)) for k in range(1, ZC)]

    for k in range(1, XC):
        along[k - 1].wait()
        piece = full.at[core, :, lax.rem(x + XC - k, XC), low]
        handed.append(go(piece, piece, other_core))
    across.wait()
    piece = full.at[core, 1 - rep, :, high]
    handed.append(go(piece, piece, other_core))
    finish(little)
    little = go(sz.at[core], sz.at[core], other_core)
    finish(handed)

    little.wait()
    small_out[...] = sz[0] + sz[1]


def assemble_kernel(factor, full, small, out_in, grad_in, gq_out, gp_out, conv_out, gain_out, scale_out, out, grad):
    out[...] = out_in[...]
    grad[...] = grad_in[...]
    lane = iota((48, 128), 1)
    for k in range(2):
        for part in range(3):
            for m in range(6):
                halves = []
                for gets in range(2):
                    block = 2 * m + gets
                    c = block % 6 // 3
                    old = block // 6 * 3 + block % 3
                    start = TILES[old // 2] + part * 6
                    tile = full[c, 0, k, start : start + 6].astype(F32).reshape(48, 128)
                    halves.append(tile if old % 2 == gets else pltpu.roll(tile, 64, 1))
                start = part * C + m * 128
                rows = slice(k * 48, k * 48 + 48)
                gq_out[rows, start : start + 128] = jnp.where(lane < 64, halves[0], halves[1]) * factor
        for c in range(2):
            for m in range(6):
                tile = full[c, 0, k, 54 + m * 3 : 57 + m * 3].astype(F32).reshape(24, 128)
                gp_out[c, k * 24 : k * 24 + 24, m * 128 : m * 128 + 128] = tile * factor

    @pl.when(pl.program_id(0) == 0)
    def _():
        for j in range(6):
            conv_out[:, j * 128 : j * 128 + 128] = small[j, 0:27] * factor
            gain_out[j * 128 : j * 128 + 128] = small[j, 27] * factor
        head, row = iota((32, 128), 1), iota((32, 128), 0)
        mine = row == head % 12 // 6 * 16 + head // 12 * 6 + head % 6
        scale_out[...] = jnp.sum(jnp.where(mine, small[6], 0.0), axis=0) * factor


def assemble(factor, full, small, out, grad):
    shape = jax.ShapeDtypeStruct
    return pl.pallas_call(
        functools.partial(assemble_kernel, factor),
        grid=(4,),
        out_shape=(
            shape((MINE, 3 * C), F32), shape((2, 192, C), F32),
            shape((27, C), F32), shape((C,), F32), shape((128,), F32),
            shape(out.shape, BF), shape(out.shape, BF),
        ),
        in_specs=[
            pl.BlockSpec((2, 1, 2, 72, 8, 128), lambda i: (0, i // 2, i % 2, 0, 0, 0)),
            pl.BlockSpec((8, 32, 128), lambda i: (0, 0, 0)),
            pl.BlockSpec((1, 4, 16, C), lambda i: (i // 2, i % 2, 0, 0)),
            pl.BlockSpec((1, 4, 16, C), lambda i: (i // 2, i % 2, 0, 0)),
        ],
        out_specs=(
            pl.BlockSpec((96, 3 * C), lambda i: (i, 0)), pl.BlockSpec((2, 48, C), lambda i: (0, i, 0)),
            pl.BlockSpec((27, C), lambda i: (0, 0)), pl.BlockSpec((C,), lambda i: (0,)),
            pl.BlockSpec((128,), lambda i: (0,)),
            pl.BlockSpec((1, 4, 16, C), lambda i: (i // 2, i % 2, 0, 0)),
            pl.BlockSpec((1, 4, 16, C), lambda i: (i // 2, i % 2, 0, 0)),
        ),
        compiler_params=pltpu.CompilerParams(vmem_limit_bytes=60 << 20),
        name="assemble",
    )(full, small, out, grad)


def whole_block(shift, scales, tokens, cot, wq, wp, weight, gain):
    shape = jax.ShapeDtypeStruct
    field = (2, 8, 16, C)
    tile = (8, 128)
    some = (32, 128)
    V = pltpu.VMEM
    copies = 96
    return pl.pallas_call(
        block_kernel,
        out_shape=(
            shape(field, BF), shape(field, BF), shape((2, 2, XC, 72) + tile, BF), shape((8,) + some, F32),
        ),
        in_specs=[SMEM, SMEM] + [pl.BlockSpec(memory_space=pl.ANY)] * 4 + [VMEM] * 2,
        out_specs=(VMEM,) * 4,
        scratch_shapes=[
            V(field, BF), V((MINE, 3 * C), BF), V(field, BF), V((2, 256, C), BF), V((2, 256, C), BF),
            V((2, 2, MINE, 3 * MINE), BF), V((2, 2, MINE // 2, C), BF), V(field, F32),
            V((512, 512), BF), V((2, 256, 512), BF),
            V((512, C), BF), V((C, 512), BF), V((512, C), BF), V((512, MINE), BF), V((512, MINE), BF),
            V((512, MINE), BF), V((512, MINE), BF), V((2, 256, 256), F32),
            V((2, 16, 256), F32), V((C, MINE), F32), V((MINE, C), F32), V((2, 2, XC, 72) + tile, BF),
            V((3, 256, 512), BF), V((3, 256, 512), BF),
            V((3, 256, 512), BF), V((256, C), BF),
            V(field, F32), V(field, BF), V(field, BF),
            V((4, 10, 16, C), F32), V((4, 10, 16, C), F32), V((3,) + field, F32),
            V((3, XC, 36) + tile, BF), V((XC - 1, 2, 2, 36) + tile, BF),
            V((XC, 36) + tile, BF), V((2, 2, 36) + tile, BF),
            V((XC - 1, 36) + tile, BF), V((3, 36) + tile, BF),
            V((72,) + tile, BF), V((ZC - 1, 9) + tile, BF),
            V((8,) + some, F32), V((8,) + some, F32), V((8,) + some, F32), V((2, 8) + some, F32),
            V((3, 4) + some, F32), V((3, 4) + some, F32), V((3, 4) + some, F32), V((3, 4) + some, F32),
            V((ZC - 1,) + some, F32),
            DMA((copies,)), DMA((copies,)), DMA((5,)),
        ],
        compiler_params=pltpu.CompilerParams(
            collective_id=0, has_side_effects=True, vmem_limit_bytes=60 << 20
        ),
        name="whole_block",
    )(shift, scales, tokens, cot, wq, wp, weight, gain)


def per_device(tokens, cotangent, w_qkv, w_proj, conv_weight, norm_gain, head_scale, shift_offsets):
    output, grad_tokens, full, small = whole_block(
        shift_offsets, head_scale, tokens[0], cotangent[0].reshape(256, C), w_qkv, w_proj, conv_weight, norm_gain
    )
    factor = 1.0 / math.sqrt(lax.axis_size("rep") * lax.axis_size("dp") * SEQ * 256)
    grad_qkv, grad_proj, grad_conv, grad_gain, grad_scale, output, grad_tokens = assemble(
        factor, full, small, output, grad_tokens
    )
    return (
        output[None],
        grad_tokens[None],
        grad_qkv,
        grad_proj.reshape(MINE, C),
        grad_conv,
        grad_gain,
        grad_scale[:24],
    )


def solution(mesh):
    in_specs = (
        P(("rep", "dp"), "seq", None, None, None),
        P(("rep", "dp"), "seq", None, None, None),
        P("dp", None),
        P("dp", None),
        P(),
        P(),
        P(),
        P(),
    )
    out_specs = (
        P(("rep", "dp"), "seq", None, None, None),
        P(("rep", "dp"), "seq", None, None, None),
        P("dp", None),
        P("dp", None),
        P(),
        P(),
        P(),
    )
    return jax.shard_map(
        per_device, mesh=mesh, in_specs=in_specs, out_specs=out_specs, check_vma=False
    )
```
